256 devices in a mesh: dap: 128 (over x_lo, y, z, core), dp: 2 (over x_hi).
Axes of the slice: x: 4 (x_hi: 2, x_lo: 2; x = x_hi * 2 + x_lo), y: 4, z: 8, core: 2. Of those that a mesh axis runs over, the one named last changes fastest.
Arguments:
- alignment_embedding: bfloat16 [256, 128, 256], P('dp', 'dap'), parts along dimension 0, may hold values from -6 to 6
- alignment_existing_flags: int32 [256, 128], P('dp', 'dap'), parts along dimension 0, may hold values 0 or 1
- couple_embedding: bfloat16 [256, 128, 128], P(('dp', 'dap')), parts along dimension 0, may hold values from -6 to 6
- alignment_scaling_factor: float32 [256], replicated, may hold values from 0.1 to 1.9
- couple_scaling_factor: float32 [128], replicated, may hold values from 0.1 to 1.9
- request_matrix: bfloat16 [256, 256], replicated, may hold values from -0.375 to 0.375
- lookup_matrix: bfloat16 [256, 256], replicated, may hold values from -0.375 to 0.375
- content_matrix: bfloat16 [256, 256], replicated, may hold values from -0.375 to 0.375
- switch_matrix: bfloat16 [256, 256], replicated, may hold values from -0.375 to 0.375
- final_projection_matrix: bfloat16 [256, 256], replicated, may hold values from -0.375 to 0.375
- couple_to_headterm_matrix: bfloat16 [128, 8], replicated, may hold values from -30 to 30
- increment_adjoint: bfloat16 [256, 128, 256], P('dp', 'dap'), parts along dimension 0, may hold values from -48 to 48
Outputs:
- alignment_increment: bfloat16 [256, 128, 256], P('dp', 'dap'), parts along dimension 0
- alignment_adjoint: bfloat16 [256, 128, 256], P('dp', 'dap'), parts along dimension 0
- couple_adjoint: bfloat16 [256, 128, 128], P(('dp', 'dap')), parts along dimension 0
- d_w_query: float32 [512, 256], P('dp'), parts along dimension 0
- d_w_key: float32 [512, 256], P('dp'), parts along dimension 0
- d_w_value: float32 [512, 256], P('dp'), parts along dimension 0
- d_w_gate: float32 [512, 256], P('dp'), parts along dimension 0
- d_w_out: float32 [512, 256], P('dp'), parts along dimension 0
- couple_headterm_adjoint: float32 [256, 8], P('dp'), parts along dimension 0
- d_msa_gain: float32 [512], P('dp'), parts along dimension 0
- couple_scaling_adjoint: float32 [256], P('dp'), parts along dimension 0
The draws below stay inside these ranges and needn't reach their ends.
There are 2 independent parts, one for each index of `dp`. The reference program is written for one: setup_inputs(seed, part) draws one part's arguments, and reference() takes and returns one part's arrays. A program takes and returns all parts, laid end to end along the dimension named above; an argument that names none is the same for every part. Nothing has to cross between parts.
All inputs are finite; a program needn't handle non-finite values. No bound on the sum of `alignment_existing_flags` on one device may be relied on, other than what follows from the above.
Results may differ from the reference program's by a relative error of at most 0.012.
The reference program's roundings to bfloat16 on the way count: a program that leaves them out, or rounds other values in their place, can miss the bound.
Values may be sent and summed in bfloat16 or wider, within the bound.
No kernel may reach another device: no remote copies, remote signals or barrier semaphores. Data moves between devices by JAX's collectives and lax.ppermute only.
A program may use at most 64 MiB of HBM per device.

```python
import jax
import jax.numpy as jnp
from jax import lax

ALIGN_FEATURES = 256
CZ = 128
HEAD_NUMBER = 8
HEAD_DIMENSION = 32
WINDOW_AMINO = 128
ALIGN_DEPTH = 128


def draw_couple_to_headterm_matrix(key, part):
    leading_element, trailing_element = jax.random.split(jax.random.fold_in(key, 11))
    lower_bound_index = jax.random.normal(leading_element, (CZ, HEAD_NUMBER), jnp.float32) * CZ ** (-0.5)
    factors_list = jnp.exp(jax.random.uniform(trailing_element, (1, HEAD_NUMBER), jnp.float32, -0.3, 0.7))
    return jnp.clip(lower_bound_index * factors_list, -30.0, 30.0).astype(jnp.bfloat16)


def draw_increment_adjoint(key, part):
    leading_element = jax.random.fold_in(jax.random.fold_in(key, 23), 0)
    lower_bound_index = jax.random.normal(leading_element, (ALIGN_DEPTH, WINDOW_AMINO, ALIGN_FEATURES), jnp.float32)
    location_index = jnp.arange(ALIGN_DEPTH, dtype=jnp.float32) / max(ALIGN_DEPTH - 1, 1)
    factors_list = (3.0 ** location_index)[:, None, None] * jnp.ones((ALIGN_DEPTH, WINDOW_AMINO, 1), jnp.float32)
    return jnp.clip(lower_bound_index * factors_list, -48.0, 48.0).astype(jnp.bfloat16)


def place_ends(array, own_key, least, top_value):
    dims = array.shape
    spot = [jax.random.randint(jax.random.fold_in(own_key, axis), (), 0, dims[axis]) for axis in range(len(dims))]
    array = array.at[tuple(spot)].set(least)
    longest = dims.index(max(dims))
    spot[longest] = (spot[longest] + 1) % dims[longest]
    return array.at[tuple(spot)].set(top_value)


def levels(stream_key, dims, cuts, least, largest):
    def one(axis_at, parts):
        steps = jax.random.uniform(jax.random.fold_in(jax.random.fold_in(stream_key, 6), axis_at), (parts,), jnp.float32, least / len(cuts), largest / len(cuts))
        return jnp.repeat(jnp.exp(steps), dims[axis_at] // parts).reshape((-1,) + (1,) * (len(dims) - axis_at - 1))

    level = one(*cuts[0])
    for cut in cuts[1:]:
        level = level * one(*cut)
    return level


def normal_values(key, dims, width, most, cuts=(), held_as=jnp.bfloat16):
    array = width * jax.random.normal(key, dims, jnp.float32)
    if cuts:
        array = array * levels(key, dims, cuts, -0.22, 0.18)
    return jnp.clip(array, -most, most).astype(held_as)


def setup_inputs(seed: int = 0, part: int = 0) -> dict:
    seeds = jax.random.split(jax.random.key(seed), 13)
    part_keys = jax.random.split(jax.random.fold_in(seeds[12], part), 13)
    return {
        "alignment_embedding": normal_values(part_keys[0], (ALIGN_DEPTH, WINDOW_AMINO, ALIGN_FEATURES), 1.0, 6.0, ((1, 128),)),
        "alignment_existing_flags": place_ends((jax.random.randint(part_keys[1], (ALIGN_DEPTH, WINDOW_AMINO), 0, 4) < 3).astype(jnp.int32), jax.random.fold_in(part_keys[1], 1), 0, 1),
        "couple_embedding": normal_values(part_keys[2], (WINDOW_AMINO, WINDOW_AMINO, CZ), 1.0, 6.0, ((0, 128),)),
        "alignment_scaling_factor": jnp.clip(1.0 + 0.18 * jax.random.normal(seeds[3], (ALIGN_FEATURES,), jnp.float32), 0.1, 1.9),
        "couple_scaling_factor": jnp.clip(1.0 + 0.18 * jax.random.normal(seeds[4], (CZ,), jnp.float32), 0.1, 1.9),
        "request_matrix": normal_values(seeds[5], (ALIGN_FEATURES, HEAD_NUMBER * HEAD_DIMENSION), ALIGN_FEATURES ** -0.5, 0.375),
        "lookup_matrix": normal_values(seeds[6], (ALIGN_FEATURES, HEAD_NUMBER * HEAD_DIMENSION), ALIGN_FEATURES ** -0.5, 0.375),
        "content_matrix": normal_values(seeds[7], (ALIGN_FEATURES, HEAD_NUMBER * HEAD_DIMENSION), ALIGN_FEATURES ** -0.5, 0.375),
        "switch_matrix": normal_values(seeds[8], (ALIGN_FEATURES, HEAD_NUMBER * HEAD_DIMENSION), ALIGN_FEATURES ** -0.5, 0.375),
        "final_projection_matrix": normal_values(seeds[9], (HEAD_NUMBER * HEAD_DIMENSION, ALIGN_FEATURES), (HEAD_NUMBER * HEAD_DIMENSION) ** -0.5, 0.375),
        "couple_to_headterm_matrix": draw_couple_to_headterm_matrix(jax.random.fold_in(seeds[12], 71), part),
        "increment_adjoint": draw_increment_adjoint(jax.random.fold_in(jax.random.fold_in(seeds[12], part), 71), part),
    }


EPS = 1e-05

def standardise_features(value, gain):
    mean = lax.optimization_barrier(jnp.mean(value, axis=-1, keepdims=True))
    centered = value - mean
    variance = lax.optimization_barrier(jnp.mean(centered * centered, axis=-1, keepdims=True))
    reciprocal_spread = lax.rsqrt(variance + EPS)
    standardised_lines = centered * reciprocal_spread
    return (standardised_lines, reciprocal_spread, standardised_lines * gain)

def standardise_features_adjoint(upstream_gradient, standardised_lines, reciprocal_spread, gain):
    rescaled_request = upstream_gradient * gain
    return reciprocal_spread * (rescaled_request - lax.optimization_barrier(jnp.mean(rescaled_request, axis=-1, keepdims=True)) - standardised_lines * lax.optimization_barrier(jnp.mean(rescaled_request * standardised_lines, axis=-1, keepdims=True)))

def tensor_product(left, right):
    return jnp.dot(left.T, right, preferred_element_type=jnp.float32)

def onward_one_line(alignment_line_content, line_filter_flags, couple_headwise_terms, alignment_scaling_factor, request_matrix, lookup_matrix, content_matrix, switch_matrix, final_projection_matrix):
    element_number = alignment_line_content.shape[0]
    standardised_lines, reciprocal_spread, rescaled_request = standardise_features(alignment_line_content.astype(jnp.float32), alignment_scaling_factor)
    input_arrays = rescaled_request.astype(jnp.bfloat16)
    query = (jnp.dot(input_arrays, request_matrix, preferred_element_type=jnp.float32) * HEAD_DIMENSION ** (-0.5)).astype(jnp.bfloat16)
    keys = jnp.dot(input_arrays, lookup_matrix, preferred_element_type=jnp.float32).astype(jnp.bfloat16)
    values = jnp.dot(input_arrays, content_matrix, preferred_element_type=jnp.float32).astype(jnp.bfloat16)
    gate_sigmoid = jax.nn.sigmoid(jnp.dot(input_arrays, switch_matrix, preferred_element_type=jnp.float32))
    query = query.reshape(element_number, HEAD_NUMBER, HEAD_DIMENSION)
    keys = keys.reshape(element_number, HEAD_NUMBER, HEAD_DIMENSION)
    values = values.reshape(element_number, HEAD_NUMBER, HEAD_DIMENSION)
    scores = jnp.einsum('ihd,jhd->ihj', query.astype(jnp.float32), keys.astype(jnp.float32))
    scores = scores + couple_headwise_terms.astype(jnp.float32) + (1000000000.0 * (line_filter_flags.astype(jnp.float32) - 1.0))[None, None, :]
    probs = jax.nn.softmax(scores, axis=-1)
    probs_low = probs.astype(jnp.bfloat16)
    attention_probs = jnp.einsum('ihj,jhd->ihd', probs_low.astype(jnp.float32), values.astype(jnp.float32)).reshape(element_number, HEAD_NUMBER * HEAD_DIMENSION)
    weighted_values = (gate_sigmoid * attention_probs).astype(jnp.bfloat16)
    alignment_increment = jnp.dot(weighted_values, final_projection_matrix, preferred_element_type=jnp.float32).astype(jnp.bfloat16)
    kept_intermediates = (standardised_lines, reciprocal_spread, input_arrays, query, keys, values, gate_sigmoid, attention_probs, weighted_values, probs)
    return (alignment_increment, kept_intermediates)

def reverse_one_line(line_adjoint_routine, kept_intermediates, alignment_scaling_factor, request_matrix, lookup_matrix, content_matrix, switch_matrix, final_projection_matrix):
    standardised_lines, reciprocal_spread, input_arrays, query, keys, values, gate_sigmoid, attention_probs, weighted_values, probs = kept_intermediates
    element_number = line_adjoint_routine.shape[0]
    probs_low = probs.astype(jnp.bfloat16)
    upstream_gradient = jnp.dot(line_adjoint_routine, final_projection_matrix.T, preferred_element_type=jnp.float32)
    d_attn = (upstream_gradient * gate_sigmoid).astype(jnp.bfloat16)
    gate_logit_gradient = (upstream_gradient * attention_probs * gate_sigmoid * (1.0 - gate_sigmoid)).astype(jnp.bfloat16)
    d_attn_heads = d_attn.reshape(element_number, HEAD_NUMBER, HEAD_DIMENSION)
    d_probs = jnp.einsum('ihd,jhd->ihj', d_attn_heads.astype(jnp.float32), values.astype(jnp.float32))
    affinity_adjoint = probs * (d_probs - lax.optimization_barrier(jnp.sum(probs * d_probs, axis=-1, keepdims=True)))
    d_low = affinity_adjoint.astype(jnp.bfloat16).astype(jnp.float32)
    query_gradient = (jnp.einsum('ihj,jhd->ihd', d_low, keys.astype(jnp.float32)) * HEAD_DIMENSION ** (-0.5)).astype(jnp.bfloat16).reshape(element_number, HEAD_NUMBER * HEAD_DIMENSION)
    key_gradient = jnp.einsum('ihj,ihd->jhd', d_low, query.astype(jnp.float32)).astype(jnp.bfloat16).reshape(element_number, HEAD_NUMBER * HEAD_DIMENSION)
    value_gradient = jnp.einsum('ihj,ihd->jhd', probs_low.astype(jnp.float32), d_attn_heads.astype(jnp.float32)).astype(jnp.bfloat16).reshape(element_number, HEAD_NUMBER * HEAD_DIMENSION)
    argument_adjoints = jnp.dot(query_gradient, request_matrix.T, preferred_element_type=jnp.float32)
    argument_adjoints = argument_adjoints + jnp.dot(key_gradient, lookup_matrix.T, preferred_element_type=jnp.float32)
    argument_adjoints = argument_adjoints + jnp.dot(value_gradient, content_matrix.T, preferred_element_type=jnp.float32)
    argument_adjoints = argument_adjoints + jnp.dot(gate_logit_gradient, switch_matrix.T, preferred_element_type=jnp.float32)
    line_adjoint = standardise_features_adjoint(argument_adjoints, standardised_lines, reciprocal_spread, alignment_scaling_factor).astype(jnp.bfloat16)
    matrix_adjoints = (tensor_product(input_arrays, query_gradient), tensor_product(input_arrays, key_gradient), tensor_product(input_arrays, value_gradient), tensor_product(input_arrays, gate_logit_gradient), tensor_product(weighted_values, line_adjoint_routine), lax.optimization_barrier(jnp.sum(argument_adjoints * standardised_lines, axis=0)))
    return (line_adjoint, affinity_adjoint, matrix_adjoints)

def reference(alignment_embedding, alignment_existing_flags, couple_embedding, alignment_scaling_factor, couple_scaling_factor, request_matrix, lookup_matrix, content_matrix, switch_matrix, final_projection_matrix, couple_to_headterm_matrix, increment_adjoint):
    pair_hat, pair_inv, pair_scaled = standardise_features(couple_embedding.astype(jnp.float32), couple_scaling_factor)
    pair_ln = pair_scaled.astype(jnp.bfloat16)
    couple_headwise_terms = jnp.einsum('ijc,ch->ihj', pair_ln.astype(jnp.float32), couple_to_headterm_matrix.astype(jnp.float32), precision=lax.Precision.HIGHEST).astype(jnp.bfloat16)

    def loop_step(carry, loop_elements):
        bias_sum, subtotal_list = carry
        alignment_increment, kept_intermediates = onward_one_line(loop_elements[0], loop_elements[1], couple_headwise_terms, alignment_scaling_factor, request_matrix, lookup_matrix, content_matrix, switch_matrix, final_projection_matrix)
        line_adjoint, affinity_adjoint, matrix_adjoints = reverse_one_line(loop_elements[2], kept_intermediates, alignment_scaling_factor, request_matrix, lookup_matrix, content_matrix, switch_matrix, final_projection_matrix)
        subtotal_list = tuple((a + b for a, b in zip(subtotal_list, matrix_adjoints)))
        return ((bias_sum + affinity_adjoint, subtotal_list), (alignment_increment, line_adjoint))
    span_length = HEAD_NUMBER * HEAD_DIMENSION
    blank_matrix = (jnp.zeros((ALIGN_FEATURES, span_length), jnp.float32), jnp.zeros((ALIGN_FEATURES, span_length), jnp.float32), jnp.zeros((ALIGN_FEATURES, span_length), jnp.float32), jnp.zeros((ALIGN_FEATURES, span_length), jnp.float32), jnp.zeros((span_length, ALIGN_FEATURES), jnp.float32), jnp.zeros((ALIGN_FEATURES,), jnp.float32))
    beginning_shift = (jnp.zeros((WINDOW_AMINO, HEAD_NUMBER, WINDOW_AMINO), jnp.float32), blank_matrix)
    (additive_term_adjoint, subtotal_list), (alignment_increment, alignment_adjoint) = lax.scan(loop_step, beginning_shift, (alignment_embedding, alignment_existing_flags, increment_adjoint))
    d_pln = jnp.einsum('ihj,ch->ijc', additive_term_adjoint, couple_to_headterm_matrix.astype(jnp.float32), precision=lax.Precision.HIGHEST)
    couple_headterm_adjoint = jnp.einsum('ijc,ihj->ch', pair_ln.astype(jnp.float32), additive_term_adjoint, precision=lax.Precision.HIGHEST)
    couple_scaling_adjoint = lax.optimization_barrier(jnp.sum(d_pln * pair_hat, axis=(0, 1)))
    couple_adjoint = standardise_features_adjoint(d_pln, pair_hat, pair_inv, couple_scaling_factor).astype(jnp.bfloat16)
    return (alignment_increment, alignment_adjoint, couple_adjoint, subtotal_list[0], subtotal_list[1], subtotal_list[2], subtotal_list[3], subtotal_list[4], couple_headterm_adjoint, subtotal_list[5], couple_scaling_adjoint)
```

```python
import jax
import jax.numpy as jnp
from jax import lax
from jax.sharding import PartitionSpec as P

ALIGN_FEATURES = 256
CZ = 128
HEADS = 8
HEAD_DIM = 32
LANES = 128
EPS = 1e-05

F32 = jnp.float32
BF16 = jnp.bfloat16


def layer_norm(value, gain):
    mean = jnp.mean(value, axis=-1, keepdims=True)
    centered = value - mean
    variance = jnp.mean(centered * centered, axis=-1, keepdims=True)
    inv = lax.rsqrt(variance + EPS)
    hat = centered * inv
    return hat, inv, hat * gain


def layer_norm_adjoint(upstream, hat, inv, gain):
    ug = upstream * gain
    return inv * (
        ug
        - jnp.mean(ug, axis=-1, keepdims=True)
        - hat * jnp.mean(ug * hat, axis=-1, keepdims=True)
    )


def dot(a, b):
    return jnp.dot(a, b, preferred_element_type=F32)


def dot_nt(a, b):
    return lax.dot_general(a, b, (((1,), (1,)), ((), ())), preferred_element_type=F32)


def dot_tn(a, b):
    return lax.dot_general(a, b, (((0,), (0,)), ((), ())), preferred_element_type=F32)


def exchange(x):
    return lax.all_to_all(x, "dap", split_axis=0, concat_axis=0, tiled=True)


def one_sequence(msa, grad, mask, bias, gain, wq, wk, wv, wg, wo):
    n = msa.shape[0]
    hat, inv, scaled = layer_norm(msa.astype(F32), gain)
    x = scaled.astype(BF16)
    q = (dot(x, wq) * HEAD_DIM ** (-0.5)).astype(BF16).reshape(n, HEADS, HEAD_DIM)
    k = dot(x, wk).astype(BF16).reshape(n, HEADS, HEAD_DIM)
    v = dot(x, wv).astype(BF16).reshape(n, HEADS, HEAD_DIM)
    gate = jax.nn.sigmoid(dot(x, wg))
    scores = jnp.einsum("ihd,jhd->hij", q, k, preferred_element_type=F32)
    scores = scores + bias.astype(F32) + (1e9 * (mask.astype(F32) - 1.0))[None, None, :]
    p32 = jax.nn.softmax(scores, axis=-1)
    p = p32.astype(BF16)
    attn = jnp.einsum("hij,jhd->ihd", p, v, preferred_element_type=F32).reshape(n, -1)
    weighted = (gate * attn).astype(BF16)
    update = dot(weighted, wo).astype(BF16)
    dw = dot_nt(grad, wo)
    d_attn = (dw * gate).astype(BF16)
    d_glog = (dw * attn * gate * (1.0 - gate)).astype(BF16)
    d_attn_h = d_attn.reshape(n, HEADS, HEAD_DIM)
    d_p = jnp.einsum("ihd,jhd->hij", d_attn_h, v, preferred_element_type=F32)
    d_s = p32 * (d_p - jnp.sum(p32 * d_p, axis=-1, keepdims=True))
    d_sb = d_s.astype(BF16)
    d_q = (
        (jnp.einsum("hij,jhd->ihd", d_sb, k, preferred_element_type=F32) * HEAD_DIM ** (-0.5))
        .astype(BF16)
        .reshape(n, -1)
    )
    d_k = jnp.einsum("hij,ihd->jhd", d_sb, q, preferred_element_type=F32).astype(BF16).reshape(n, -1)
    d_v = jnp.einsum("hij,ihd->jhd", p, d_attn_h, preferred_element_type=F32).astype(BF16).reshape(n, -1)
    d_x = dot_nt(d_q, wq) + dot_nt(d_k, wk) + dot_nt(d_v, wv) + dot_nt(d_glog, wg)
    adjoint = layer_norm_adjoint(d_x, hat, inv, gain).astype(BF16)
    weights = (
        dot_tn(x, d_q),
        dot_tn(x, d_k),
        dot_tn(x, d_v),
        dot_tn(x, d_glog),
        dot_tn(weighted, grad),
    )
    d_gain = jnp.sum(d_x * hat, axis=0)
    return update, adjoint, d_s, weights, d_gain


def on_device(msa, flags, pair, gain, pair_gain, wq, wk, wv, wg, wo, w_bias, grad):
    n = msa.shape[0]
    pair_hat, pair_inv, pair_scaled = layer_norm(pair[0].astype(F32), pair_gain)
    pair_ln = pair_scaled.astype(BF16)
    bias_rows = lax.dot_general(
        w_bias, pair_ln, (((0,), (1,)), ((), ())), preferred_element_type=F32
    ).astype(BF16)
    send = jnp.concatenate(
        [
            msa.reshape(n, 2, LANES),
            grad.reshape(n, 2, LANES),
            jnp.broadcast_to(flags.astype(BF16)[:, :, None], (n, 4, LANES)),
            jnp.broadcast_to(bias_rows[None], (n, HEADS, LANES)),
        ],
        axis=1,
    )
    got = exchange(send)
    update, adjoint, d_s, weights, d_gain = one_sequence(
        got[:, 0:2].reshape(n, ALIGN_FEATURES),
        got[:, 2:4].reshape(n, ALIGN_FEATURES),
        got[:, 4, 0],
        got[:, 8:16].transpose(1, 0, 2),
        gain, wq, wk, wv, wg, wo,
    )
    w_rows = 5 * ALIGN_FEATURES * 2 // n
    send = jnp.concatenate(
        [
            update.reshape(n, 2, LANES),
            adjoint.reshape(n, 2, LANES),
            d_s.astype(F32).transpose(1, 0, 2).astype(BF16),
            jnp.stack(weights).astype(BF16).reshape(n, w_rows, LANES),
        ],
        axis=1,
    )
    got = exchange(send)
    update_out = got[:, 0:2].reshape(n, 1, ALIGN_FEATURES)
    adjoint_out = got[:, 2:4].reshape(n, 1, ALIGN_FEATURES)
    sums = jnp.sum(got[:, 4:].astype(F32), axis=0)
    d_bias = sums[:HEADS]
    d_pln = lax.dot_general(
        d_bias, w_bias.astype(F32), (((0,), (1,)), ((), ())), precision=lax.Precision.HIGHEST
    )
    w_bias_part = lax.dot_general(
        d_bias, pair_ln.astype(F32), (((1,), (0,)), ((), ())), precision=lax.Precision.HIGHEST
    )
    pair_gain_part = jnp.sum(d_pln * pair_hat, axis=0, keepdims=True)
    couple_adjoint = layer_norm_adjoint(d_pln, pair_hat, pair_inv, pair_gain).astype(BF16)[None]
    shard = jnp.concatenate(
        [
            sums[HEADS:],
            w_bias_part,
            pair_gain_part,
            d_gain.reshape(2, LANES),
            jnp.zeros((1, LANES), F32),
        ],
        axis=0,
    ).astype(BF16)
    got = exchange(jnp.broadcast_to(shard[None], (n,) + shard.shape))
    totals = got[:, :w_rows].astype(F32).reshape(5, ALIGN_FEATURES, ALIGN_FEATURES)
    small = jnp.sum(got[:, w_rows:].astype(F32), axis=0)
    return (
        update_out,
        adjoint_out,
        couple_adjoint,
        totals[0],
        totals[1],
        totals[2],
        totals[3],
        totals[4],
        small[:HEADS].T,
        small[HEADS + 1 : HEADS + 3].reshape(ALIGN_FEATURES),
        small[HEADS],
    )


def solution(mesh):
    rows = P("dp", "dap", None)
    pair = P(("dp", "dap"), None, None)
    in_specs = (rows, P("dp", "dap"), pair) + (P(),) * 8 + (rows,)
    out_specs = (rows, rows, pair) + (P("dp", None),) * 6 + (P("dp"), P("dp"))
    return jax.shard_map(
        on_device, mesh=mesh, in_specs=in_specs, out_specs=out_specs, check_vma=False
    )
```

```python
import jax
import jax.numpy as jnp
from jax import lax
from jax.experimental import pallas as pl
from jax.experimental.pallas import tpu as pltpu
from jax.sharding import PartitionSpec as P

FEATURES = 256
HEADS = 8
HEAD_DIM = 32
LANES = 128
CORES = 2
CHIPS = 64
N = CORES * CHIPS
SCALE = HEAD_DIM ** (-0.5)
EPS = 1e-05

F32 = jnp.float32
BF16 = jnp.bfloat16

IN_ROWS = 16
PART_ROWS = 40
SUM_ROWS = 32

VMEM = pl.BlockSpec(memory_space=pltpu.VMEM)
SMEM = pl.BlockSpec(memory_space=pltpu.SMEM)


def dot(a, b):
    return jnp.dot(a, b, preferred_element_type=F32)


def dot_nt(a, b):
    return lax.dot_general(a, b, (((1,), (1,)), ((), ())), preferred_element_type=F32)


def dot_tn(a, b):
    return lax.dot_general(a, b, (((0,), (0,)), ((), ())), preferred_element_type=F32)


def layer_norm(value, gain):
    mean = jnp.mean(value, axis=-1, keepdims=True)
    centered = value - mean
    variance = jnp.mean(centered * centered, axis=-1, keepdims=True)
    inv = lax.rsqrt(variance + EPS)
    hat = centered * inv
    return hat, inv, hat * gain


def layer_norm_adjoint(upstream, hat, inv, gain):
    ug = upstream * gain
    return inv * (
        ug
        - jnp.mean(ug, axis=-1, keepdims=True)
        - hat * jnp.mean(ug * hat, axis=-1, keepdims=True)
    )


def split(x):
    high = x.astype(BF16)
    rest = x - high.astype(F32)
    mid = rest.astype(BF16)
    return high, mid, (rest - mid.astype(F32)).astype(BF16)


def by_core(rows):
    return jnp.concatenate(
        [rows[pl.ds(c, CHIPS, stride=CORES), :] for c in range(CORES)], axis=0
    )


def call(kernel, out_shape, scratch, *operands):
    return pl.pallas_call(
        kernel,
        out_shape=out_shape,
        in_specs=[SMEM] + [VMEM] * (len(operands) - 1),
        out_specs=jax.tree.map(lambda _: VMEM, out_shape),
        scratch_shapes=scratch,
    )(*operands)


def entry_kernel(pos, msa, grad, flags, pair, gain, w_bias, out, stage, rows):
    for r, value in enumerate((msa, grad)):
        value = value[...].astype(F32)
        stage[pl.ds(2 * r, N, stride=8), :] = value[:, :LANES]
        stage[pl.ds(2 * r + 1, N, stride=8), :] = value[:, LANES:]
    stage[pl.ds(4, N, stride=8), :] = jnp.broadcast_to(flags[...].astype(F32), (N, LANES))
    for r in range(5, 8):
        stage[pl.ds(r, N, stride=8), :] = jnp.zeros((N, LANES), F32)
    out[:, 0:8, :] = stage[...].reshape(N, 8, LANES).astype(BF16)
    rows[...] = pair[0].astype(F32)
    _, _, scaled = layer_norm(by_core(rows), gain[...])
    bias = dot_nt(w_bias[...], scaled.astype(BF16)).astype(BF16)
    out[:, 8:16, :] = jnp.broadcast_to(bias[None], (N, HEADS, LANES))


def sequence_kernel(
    pos, got, gain_ref, wq_ref, wk_ref, wv_ref, wg_ref, wo_ref, own, other, rows, mine, theirs
):
    first = pos[0] == 0
    rows[...] = got[...].astype(F32).reshape(N * IN_ROWS, LANES)

    def row(r):
        return jnp.concatenate(
            [rows[pl.ds(c * IN_ROWS + r, CHIPS, stride=CORES * IN_ROWS), :] for c in range(CORES)],
            axis=0,
        )

    def halves(value):
        return (
            jnp.where(first, value[:CHIPS], value[CHIPS:]),
            jnp.where(first, value[CHIPS:], value[:CHIPS]),
        )

    gain = gain_ref[...]
    msa = jnp.concatenate([row(0), row(1)], axis=1)
    grad = jnp.concatenate([row(2), row(3)], axis=1).astype(BF16)
    lane = lax.broadcasted_iota(jnp.int32, (8, LANES), 1)
    pick = jnp.where(lane == pos[1], 1.0, 0.0).astype(BF16)
    flags = dot_nt(pick, row(4).astype(BF16))[:1]
    masking = 1e9 * (flags - 1.0)
    hat, inv, scaled = layer_norm(msa, gain)
    x = scaled.astype(BF16)
    wo = wo_ref[...]
    q = (dot(x, wq_ref[...]) * SCALE).astype(BF16)
    k = dot(x, wk_ref[...]).astype(BF16)
    v = dot(x, wv_ref[...]).astype(BF16)
    gate = jax.nn.sigmoid(dot(x, wg_ref[...]))
    dw = dot_nt(grad, wo)
    d_attn = (dw * gate).astype(BF16)
    lane = lax.broadcasted_iota(jnp.int32, (1, LANES), 1)
    q_t = q.T
    da_t = d_attn.T
    attn = []
    d_q = []
    dk_t = []
    dv_t = []
    for g in range(2):
        cols = slice(g * LANES, (g + 1) * LANES)
        qg, kg, vg, dg = q[:, cols], k[:, cols], v[:, cols], d_attn[:, cols]
        attn_g = jnp.zeros((N, LANES), F32)
        dq_g = jnp.zeros((N, LANES), F32)
        for s in range(4):
            h = 4 * g + s
            keep = jnp.where((lane >= s * HEAD_DIM) & (lane < (s + 1) * HEAD_DIM), 1.0, 0.0)
            keep = keep.astype(BF16)
            scores = dot_nt(qg * keep, kg) + row(8 + h) + masking
            e = jnp.exp(scores - jnp.max(scores, axis=-1, keepdims=True))
            p32 = e * (1.0 / jnp.sum(e, axis=-1, keepdims=True))
            p = p32.astype(BF16)
            attn_g += dot(p, vg * keep)
            d_p = dot_nt(dg * keep, vg)
            d_s = p32 * (d_p - jnp.sum(p32 * d_p, axis=-1, keepdims=True))
            a, b = halves(d_s)
            mine[pl.ds(h, CHIPS, stride=HEADS), :] = a
            theirs[pl.ds(h, CHIPS, stride=HEADS), :] = b
            d_sb = d_s.astype(BF16)
            dq_g += dot(d_sb, kg * keep)
            head = slice(h * HEAD_DIM, (h + 1) * HEAD_DIM)
            dk_t.append(dot(q_t[head], d_sb))
            dv_t.append(dot(da_t[head], p))
        attn.append(attn_g)
        d_q.append(dq_g)
    own[:, 8:16, :] = mine[...].reshape(CHIPS, HEADS, LANES)
    other[:, 8:16, :] = theirs[...].reshape(CHIPS, HEADS, LANES).astype(BF16)
    attn = jnp.concatenate(attn, axis=1)
    d_q = (jnp.concatenate(d_q, axis=1) * SCALE).astype(BF16)
    d_k = jnp.concatenate(dk_t, axis=0).astype(BF16).T
    d_v = jnp.concatenate(dv_t, axis=0).astype(BF16).T
    weighted = (gate * attn).astype(BF16)
    update = dot(weighted, wo)
    d_g = (dw * attn * gate * (1.0 - gate)).astype(BF16)
    d_x = (
        dot_nt(d_q, wq_ref[...])
        + dot_nt(d_k, wk_ref[...])
        + dot_nt(d_v, wv_ref[...])
        + dot_nt(d_g, wg_ref[...])
    )
    adjoint = layer_norm_adjoint(d_x, hat, inv, gain)
    zeros = jnp.zeros((CHIPS, LANES), F32)
    for r, value in enumerate(
        (update[:, :LANES], update[:, LANES:], adjoint[:, :LANES], adjoint[:, LANES:])
    ):
        a, b = halves(value)
        mine[pl.ds(r, CHIPS, stride=8), :] = a
        mine[pl.ds(4 + r, CHIPS, stride=8), :] = zeros
        theirs[pl.ds(r, CHIPS, stride=8), :] = zeros
        theirs[pl.ds(4 + r, CHIPS, stride=8), :] = b
    own[:, 0:8, :] = mine[...].reshape(CHIPS, 8, LANES)
    other[:, 0:8, :] = theirs[...].reshape(CHIPS, 8, LANES).astype(BF16)
    x_t = x.T
    w_t = weighted.T
    d_gain = jnp.broadcast_to(jnp.sum(d_x * hat, axis=0, keepdims=True), (LANES, FEATURES)).T
    low = lax.broadcasted_iota(jnp.int32, (1, 8, 1), 1) < 4
    pairs = ((x_t, d_q), (x_t, d_k), (x_t, d_v), (x_t, d_g), (w_t, grad))
    for ref, is_own in ((own, True), (other, False)):
        low_half = first == is_own
        mats = [dot(a, jnp.where(low_half, b[:, :LANES], b[:, LANES:])) for a, b in pairs]
        mats.append(d_gain)
        for t in range(3):
            a = mats[2 * t].reshape(CHIPS // 2, 8, LANES)
            b = mats[2 * t + 1].reshape(CHIPS // 2, 8, LANES)
            even = jnp.where(low, a, pltpu.roll(b, 4, 1)).astype(ref.dtype)
            odd = jnp.where(low, pltpu.roll(a, 4, 1), b).astype(ref.dtype)
            both = jnp.stack([even, odd], axis=1).reshape(CHIPS, 8, LANES)
            ref[:, 16 + 8 * t : 24 + 8 * t, :] = both


def owner_kernel(pos, got, pair, gain_ref, w_ref, couple, out, rows):
    total = jnp.sum(got[:, 8:, :].astype(F32), axis=0)
    d_bias = total[:HEADS]
    gain = gain_ref[...]
    rows[...] = pair[0].astype(F32)
    hat, inv, scaled = layer_norm(by_core(rows), gain)
    pair_ln = scaled.astype(BF16)
    w_bias = w_ref[...]
    d_pln = jnp.zeros((N, LANES), F32)
    head = jnp.zeros((HEADS, LANES), F32)
    for part in reversed(split(d_bias)):
        d_pln += dot_tn(part, w_bias)
        head += dot(part, pair_ln)
    adjoint = layer_norm_adjoint(d_pln, hat, inv, gain)
    for c in range(CORES):
        rows[pl.ds(c, CHIPS, stride=CORES), :] = adjoint[c * CHIPS : (c + 1) * CHIPS]
    couple[0] = rows[...].astype(BF16)
    pair_gain = jnp.sum(d_pln * hat, axis=0, keepdims=True)
    lane = lax.broadcasted_iota(jnp.int32, (4, LANES), 1)
    spot = lax.broadcasted_iota(jnp.int32, (4, LANES), 0) + 4 * pos[2] - LANES * pos[0]
    msa_gain = jnp.sum(jnp.where(lane == spot, total[28:32], 0.0), axis=0, keepdims=True)
    shard = jnp.concatenate(
        [total[8:28], pair_gain, msa_gain, jnp.zeros((2, LANES), F32), head], axis=0
    )
    out[...] = jnp.broadcast_to(shard.astype(BF16)[None], (CHIPS, SUM_ROWS, LANES))


def rows_kernel(pos, got, update, adjoint, stage, rows):
    stage[...] = got[:, 0:8, :].astype(F32).reshape(CHIPS * 8, LANES)
    first = pos[0] == 0
    for index, out in enumerate((update, adjoint)):
        for half in range(2):
            r = 2 * index + half
            same = stage[pl.ds(r, CHIPS, stride=8), :]
            cross = stage[pl.ds(4 + r, CHIPS, stride=8), :]
            rows[pl.ds(0, CHIPS, stride=CORES), :] = jnp.where(first, same, cross)
            rows[pl.ds(1, CHIPS, stride=CORES), :] = jnp.where(first, cross, same)
            out[:, half * LANES : (half + 1) * LANES] = rows[...].astype(BF16)


def final_kernel(pos, mine, theirs, *outs):
    first = pos[0] == 0
    low = lax.broadcasted_iota(jnp.int32, (1, 8, 1), 1) < 4
    weights, (head, msa_gain, pair_gain) = outs[:5], outs[5:]
    tail = [ref[:, 16:32, :].astype(F32) for ref in (mine, theirs)]
    sums = [jnp.sum(t[:, 4:], axis=0) for t in tail]
    head[...] = sums[0][4:12] + sums[1][4:12]
    pair_gain[...] = sums[0][0:1] + sums[1][0:1]
    msa_gain[:, :LANES] = jnp.where(first, sums[0][1:2], sums[1][1:2])
    msa_gain[:, LANES:] = jnp.where(first, sums[1][1:2], sums[0][1:2])
    for t in range(3):
        blocks = []
        for ref in (mine, theirs):
            tile = ref[:, 8 * t : 8 * t + 8, :].astype(F32).reshape(CHIPS // 2, 2, 8, LANES)
            even, odd = tile[:, 0], tile[:, 1]
            a = jnp.where(low, even, pltpu.roll(odd, 4, 1)).reshape(FEATURES, LANES)
            b = jnp.where(low, pltpu.roll(even, 4, 1), odd).reshape(FEATURES, LANES)
            blocks.append((a, b))
        for w in range(2):
            if 2 * t + w < 5:
                same, cross = blocks[0][w], blocks[1][w]
                weights[2 * t + w][:, :LANES] = jnp.where(first, same, cross)
                weights[2 * t + w][:, LANES:] = jnp.where(first, cross, same)


def on_device(msa, flags, pair, gain, pair_gain, wq, wk, wv, wg, wo, w_bias, grad):
    index = lax.axis_index("dap")
    pos = jnp.stack([index % CORES, index, index // CORES]).astype(jnp.int32)
    same_core = [[CORES * m + c for m in range(CHIPS)] for c in range(CORES)]
    partner = [(i, i ^ 1) for i in range(N)]

    def exchange(x, groups=None):
        return lax.all_to_all(
            x, "dap", split_axis=0, concat_axis=0, tiled=True, axis_index_groups=groups
        )

    w_bias = w_bias.T
    gain = gain.reshape(1, FEATURES)
    pair_gain = pair_gain.reshape(1, LANES)
    sent = call(
        entry_kernel,
        jax.ShapeDtypeStruct((N, IN_ROWS, LANES), BF16),
        [pltpu.VMEM((N * 8, LANES), F32), pltpu.VMEM((N, LANES), F32)],
        pos, msa.reshape(N, FEATURES), grad.reshape(N, FEATURES), flags.reshape(1, N),
        pair, pair_gain, w_bias,
    )
    got = exchange(sent)
    part = (CHIPS, PART_ROWS, LANES)
    own, other = call(
        sequence_kernel,
        (jax.ShapeDtypeStruct(part, F32), jax.ShapeDtypeStruct(part, BF16)),
        [pltpu.VMEM((N * IN_ROWS, LANES), F32)] + [pltpu.VMEM((CHIPS * 8, LANES), F32)] * 2,
        pos, got, gain, wq, wk, wv, wg, wo,
    )
    paired = (own + lax.ppermute(other, "dap", partner).astype(F32)).astype(BF16)
    got = exchange(paired, same_core)
    couple, shard = call(
        owner_kernel,
        (
            jax.ShapeDtypeStruct((1, N, LANES), BF16),
            jax.ShapeDtypeStruct((CHIPS, SUM_ROWS, LANES), BF16),
        ),
        [pltpu.VMEM((N, LANES), F32)],
        pos, got, pair, pair_gain, w_bias,
    )
    mine = exchange(shard, same_core)
    row_shape = jax.ShapeDtypeStruct((N, FEATURES), BF16)
    update, adjoint = call(
        rows_kernel,
        (row_shape, row_shape),
        [pltpu.VMEM((CHIPS * 8, LANES), F32), pltpu.VMEM((N, LANES), F32)],
        pos, got,
    )
    theirs = lax.ppermute(mine, "dap", partner)
    square = jax.ShapeDtypeStruct((FEATURES, FEATURES), F32)
    *weights, head, msa_gain, pair_gain = call(
        final_kernel,
        (square,) * 5
        + (
            jax.ShapeDtypeStruct((HEADS, LANES), F32),
            jax.ShapeDtypeStruct((1, FEATURES), F32),
            jax.ShapeDtypeStruct((1, LANES), F32),
        ),
        [],
        pos, mine, theirs,
    )
    return (
        update.reshape(N, 1, FEATURES),
        adjoint.reshape(N, 1, FEATURES),
        couple,
        *weights,
        head.T,
        msa_gain.reshape(FEATURES),
        pair_gain.reshape(LANES),
    )


def solution(mesh):
    rows = P("dp", "dap", None)
    pair = P(("dp", "dap"), None, None)
    in_specs = (rows, P("dp", "dap"), pair) + (P(),) * 8 + (rows,)
    out_specs = (rows, rows, pair) + (P("dp", None),) * 6 + (P("dp"), P("dp"))
    return jax.shard_map(
        on_device, mesh=mesh, in_specs=in_specs, out_specs=out_specs, check_vma=False
    )
```

```python
import jax
import jax.numpy as jnp
from jax import lax
from jax.experimental import pallas as pl
from jax.experimental.pallas import tpu as pltpu
from jax.sharding import PartitionSpec as P

FEATURES = 256
HEADS = 8
HEAD_DIM = 32
LANES = 128
CORES = 2
CHIPS = 64
N = CORES * CHIPS
SCALE = HEAD_DIM ** (-0.5)
EPS = 1e-05

F32 = jnp.float32
BF16 = jnp.bfloat16

IN_ROWS = 24
PART_ROWS = 40
SUM_ROWS = 32

VMEM = pl.BlockSpec(memory_space=pltpu.VMEM)
SMEM = pl.BlockSpec(memory_space=pltpu.SMEM)
HBM = pl.BlockSpec(memory_space=pltpu.HBM)


def dot(a, b):
    return jnp.dot(a, b, preferred_element_type=F32)


def dot_nt(a, b):
    return lax.dot_general(a, b, (((1,), (1,)), ((), ())), preferred_element_type=F32)


def dot_tn(a, b):
    return lax.dot_general(a, b, (((0,), (0,)), ((), ())), preferred_element_type=F32)


def layer_norm(value, gain):
    mean = jnp.mean(value, axis=-1, keepdims=True)
    centered = value - mean
    variance = jnp.mean(centered * centered, axis=-1, keepdims=True)
    inv = lax.rsqrt(variance + EPS)
    hat = centered * inv
    return hat, inv, hat * gain


def layer_norm_adjoint(upstream, hat, inv, gain):
    ug = upstream * gain
    return inv * (
        ug
        - jnp.mean(ug, axis=-1, keepdims=True)
        - hat * jnp.mean(ug * hat, axis=-1, keepdims=True)
    )


def split(x):
    high = x.astype(BF16)
    rest = x - high.astype(F32)
    mid = rest.astype(BF16)
    return high, mid, (rest - mid.astype(F32)).astype(BF16)


def by_core(rows):
    return jnp.concatenate(
        [rows[pl.ds(c, CHIPS, stride=CORES), :] for c in range(CORES)], axis=0
    )


def call(kernel, out_shape, scratch, *operands, first=SMEM, rest=VMEM, mib=12):
    return pl.pallas_call(
        kernel,
        out_shape=out_shape,
        in_specs=[first] + [rest] * (len(operands) - 1),
        out_specs=jax.tree.map(lambda _: VMEM, out_shape),
        scratch_shapes=scratch,
        compiler_params=pltpu.CompilerParams(vmem_limit_bytes=mib * 1024 * 1024),
    )(*operands)


def entry_kernel(
    msa_hbm, grad_hbm, flags_hbm, pair_hbm, gain_hbm, w_hbm,
    out, msa, grad, flags, pair, gain, w_bias, stage, rows, sems
):
    refs = (
        (pair_hbm, pair), (gain_hbm, gain), (w_hbm, w_bias),
        (msa_hbm, msa), (grad_hbm, grad), (flags_hbm, flags),
    )
    copies = [pltpu.make_async_copy(a, b, sems.at[i]) for i, (a, b) in enumerate(refs)]
    for copy in copies:
        copy.start()
    for copy in copies[:3]:
        copy.wait()
    rows[...] = pair[0].astype(F32)
    _, _, scaled = layer_norm(by_core(rows), gain[...])
    bias = dot_nt(w_bias[...], scaled.astype(BF16)).astype(BF16)
    out[:, 8:16, :] = jnp.broadcast_to(bias[None], (CHIPS, HEADS, LANES))
    for copy in copies[3:]:
        copy.wait()
    for r, ref in enumerate((msa, grad)):
        value = ref[...].astype(F32)
        stage[pl.ds(2 * r, N, stride=4), :] = value[:, :LANES]
        stage[pl.ds(2 * r + 1, N, stride=4), :] = value[:, LANES:]
    out[:, 0:8, :] = stage[...].reshape(CHIPS, 8, LANES).astype(BF16)
    present = jnp.broadcast_to(flags[...].astype(F32), (8, LANES)).astype(BF16)
    out[:, 16:24, :] = jnp.broadcast_to(present[None], (CHIPS, 8, LANES))


def sequence_kernel(
    pos, near, far, gain_ref, wq_ref, wk_ref, wv_ref, wg_ref, wo_ref, own, other, rows, mine, theirs
):
    core = pos[0]
    first = core == 0
    rows[core] = near[...].astype(F32).reshape(CHIPS * IN_ROWS, LANES)
    rows[1 - core] = far[...].astype(F32).reshape(CHIPS * IN_ROWS, LANES)

    def row(r):
        return jnp.concatenate(
            [rows.at[c][pl.ds(r, CHIPS, stride=IN_ROWS), :] for c in range(CORES)], axis=0
        )

    def line(r):
        return jnp.where(first, row(r), row(4 + r))

    def halves(value):
        return (
            jnp.where(first, value[:CHIPS], value[CHIPS:]),
            jnp.where(first, value[CHIPS:], value[:CHIPS]),
        )

    gain = gain_ref[...]
    msa = jnp.concatenate([line(0), line(1)], axis=1)
    grad = jnp.concatenate([line(2), line(3)], axis=1).astype(BF16)
    lane = lax.broadcasted_iota(jnp.int32, (8, LANES), 1)
    pick = jnp.where(lane == pos[1], 1.0, 0.0).astype(BF16)
    flags = dot_nt(pick, row(16).astype(BF16))[:1]
    masking = 1e9 * (flags - 1.0)
    hat, inv, scaled = layer_norm(msa, gain)
    x = scaled.astype(BF16)
    wo = wo_ref[...]
    q = (dot(x, wq_ref[...]) * SCALE).astype(BF16)
    k = dot(x, wk_ref[...]).astype(BF16)
    v = dot(x, wv_ref[...]).astype(BF16)
    gate = jax.nn.sigmoid(dot(x, wg_ref[...]))
    dw = dot_nt(grad, wo)
    d_attn = (dw * gate).astype(BF16)
    lane = lax.broadcasted_iota(jnp.int32, (1, LANES), 1)
    q_t = q.T
    da_t = d_attn.T
    attn = []
    d_q = []
    dk_t = []
    dv_t = []
    for g in range(2):
        cols = slice(g * LANES, (g + 1) * LANES)
        qg, kg, vg, dg = q[:, cols], k[:, cols], v[:, cols], d_attn[:, cols]
        attn_g = jnp.zeros((N, LANES), F32)
        dq_g = jnp.zeros((N, LANES), F32)
        for s in range(4):
            h = 4 * g + s
            keep = jnp.where((lane >= s * HEAD_DIM) & (lane < (s + 1) * HEAD_DIM), 1.0, 0.0)
            keep = keep.astype(BF16)
            scores = dot_nt(qg * keep, kg) + row(8 + h) + masking
            e = jnp.exp(scores - jnp.max(scores, axis=-1, keepdims=True))
            p32 = e * (1.0 / jnp.sum(e, axis=-1, keepdims=True))
            p = p32.astype(BF16)
            attn_g += dot(p, vg * keep)
            d_p = dot_nt(dg * keep, vg)
            d_s = p32 * (d_p - jnp.sum(p32 * d_p, axis=-1, keepdims=True))
            a, b = halves(d_s)
            mine[pl.ds(h, CHIPS, stride=HEADS), :] = a
            theirs[pl.ds(h, CHIPS, stride=HEADS), :] = b
            d_sb = d_s.astype(BF16)
            dq_g += dot(d_sb, kg * keep)
            head = slice(h * HEAD_DIM, (h + 1) * HEAD_DIM)
            dk_t.append(dot(q_t[head], d_sb))
            dv_t.append(dot(da_t[head], p))
        attn.append(attn_g)
        d_q.append(dq_g)
    own[:, 8:16, :] = mine[...].reshape(CHIPS, HEADS, LANES)
    other[:, 8:16, :] = theirs[...].reshape(CHIPS, HEADS, LANES).astype(BF16)
    attn = jnp.concatenate(attn, axis=1)
    d_q = (jnp.concatenate(d_q, axis=1) * SCALE).astype(BF16)
    d_k = jnp.concatenate(dk_t, axis=0).astype(BF16).T
    d_v = jnp.concatenate(dv_t, axis=0).astype(BF16).T
    weighted = (gate * attn).astype(BF16)
    update = dot(weighted, wo)
    d_g = (dw * attn * gate * (1.0 - gate)).astype(BF16)
    d_x = (
        dot_nt(d_q, wq_ref[...])
        + dot_nt(d_k, wk_ref[...])
        + dot_nt(d_v, wv_ref[...])
        + dot_nt(d_g, wg_ref[...])
    )
    adjoint = layer_norm_adjoint(d_x, hat, inv, gain)
    zeros = jnp.zeros((CHIPS, LANES), F32)
    for r, value in enumerate(
        (update[:, :LANES], update[:, LANES:], adjoint[:, :LANES], adjoint[:, LANES:])
    ):
        a, b = halves(value)
        mine[pl.ds(r, CHIPS, stride=8), :] = a
        mine[pl.ds(4 + r, CHIPS, stride=8), :] = zeros
        theirs[pl.ds(r, CHIPS, stride=8), :] = zeros
        theirs[pl.ds(4 + r, CHIPS, stride=8), :] = b
    own[:, 0:8, :] = mine[...].reshape(CHIPS, 8, LANES)
    other[:, 0:8, :] = theirs[...].reshape(CHIPS, 8, LANES).astype(BF16)
    x_t = x.T
    w_t = weighted.T
    d_gain = jnp.broadcast_to(jnp.sum(d_x * hat, axis=0, keepdims=True), (LANES, FEATURES)).T
    low = lax.broadcasted_iota(jnp.int32, (1, 8, 1), 1) < 4
    pairs = ((x_t, d_q), (x_t, d_k), (x_t, d_v), (x_t, d_g), (w_t, grad))
    for ref, is_own in ((own, True), (other, False)):
        low_half = first == is_own
        mats = [dot(a, jnp.where(low_half, b[:, :LANES], b[:, LANES:])) for a, b in pairs]
        mats.append(d_gain)
        for t in range(3):
            a = mats[2 * t].reshape(CHIPS // 2, 8, LANES)
            b = mats[2 * t + 1].reshape(CHIPS // 2, 8, LANES)
            even = jnp.where(low, a, pltpu.roll(b, 4, 1)).astype(ref.dtype)
            odd = jnp.where(low, pltpu.roll(a, 4, 1), b).astype(ref.dtype)
            both = jnp.stack([even, odd], axis=1).reshape(CHIPS, 8, LANES)
            ref[:, 16 + 8 * t : 24 + 8 * t, :] = both


def owner_kernel(pos, got, pair, gain_ref, w_ref, couple, out, rows):
    total = jnp.sum(got[:, 8:, :].astype(F32), axis=0)
    d_bias = total[:HEADS]
    gain = gain_ref[...]
    rows[...] = pair[0].astype(F32)
    hat, inv, scaled = layer_norm(by_core(rows), gain)
    pair_ln = scaled.astype(BF16)
    w_bias = w_ref[...]
    d_pln = jnp.zeros((N, LANES), F32)
    head = jnp.zeros((HEADS, LANES), F32)
    for part in reversed(split(d_bias)):
        d_pln += dot_tn(part, w_bias)
        head += dot(part, pair_ln)
    adjoint = layer_norm_adjoint(d_pln, hat, inv, gain)
    for c in range(CORES):
        rows[pl.ds(c, CHIPS, stride=CORES), :] = adjoint[c * CHIPS : (c + 1) * CHIPS]
    couple[0] = rows[...].astype(BF16)
    pair_gain = jnp.sum(d_pln * hat, axis=0, keepdims=True)
    lane = lax.broadcasted_iota(jnp.int32, (4, LANES), 1)
    spot = lax.broadcasted_iota(jnp.int32, (4, LANES), 0) + 4 * pos[2] - LANES * pos[0]
    msa_gain = jnp.sum(jnp.where(lane == spot, total[28:32], 0.0), axis=0, keepdims=True)
    shard = jnp.concatenate(
        [total[8:28], pair_gain, msa_gain, jnp.zeros((2, LANES), F32), head], axis=0
    )
    out[...] = jnp.broadcast_to(shard.astype(BF16)[None], (CHIPS, SUM_ROWS, LANES))


def rows_kernel(pos, got, update, adjoint, stage, rows):
    stage[...] = got[:, 0:8, :].astype(F32).reshape(CHIPS * 8, LANES)
    first = pos[0] == 0
    for index, out in enumerate((update, adjoint)):
        for half in range(2):
            r = 2 * index + half
            same = stage[pl.ds(r, CHIPS, stride=8), :]
            cross = stage[pl.ds(4 + r, CHIPS, stride=8), :]
            rows[pl.ds(0, CHIPS, stride=CORES), :] = jnp.where(first, same, cross)
            rows[pl.ds(1, CHIPS, stride=CORES), :] = jnp.where(first, cross, same)
            out[:, half * LANES : (half + 1) * LANES] = rows[...].astype(BF16)


def final_kernel(pos, mine, theirs, *outs):
    first = pos[0] == 0
    low = lax.broadcasted_iota(jnp.int32, (1, 8, 1), 1) < 4
    weights, (head, msa_gain, pair_gain) = outs[:5], outs[5:]
    tail = [ref[:, 16:32, :].astype(F32) for ref in (mine, theirs)]
    sums = [jnp.sum(t[:, 4:], axis=0) for t in tail]
    head[...] = sums[0][4:12] + sums[1][4:12]
    pair_gain[...] = sums[0][0:1] + sums[1][0:1]
    msa_gain[:, :LANES] = jnp.where(first, sums[0][1:2], sums[1][1:2])
    msa_gain[:, LANES:] = jnp.where(first, sums[1][1:2], sums[0][1:2])
    for t in range(3):
        blocks = []
        for ref in (mine, theirs):
            tile = ref[:, 8 * t : 8 * t + 8, :].astype(F32).reshape(CHIPS // 2, 2, 8, LANES)
            even, odd = tile[:, 0], tile[:, 1]
            a = jnp.where(low, even, pltpu.roll(odd, 4, 1)).reshape(FEATURES, LANES)
            b = jnp.where(low, pltpu.roll(even, 4, 1), odd).reshape(FEATURES, LANES)
            blocks.append((a, b))
        for w in range(2):
            if 2 * t + w < 5:
                same, cross = blocks[0][w], blocks[1][w]
                weights[2 * t + w][:, :LANES] = jnp.where(first, same, cross)
                weights[2 * t + w][:, LANES:] = jnp.where(first, cross, same)


def on_device(msa, flags, pair, gain, pair_gain, wq, wk, wv, wg, wo, w_bias, grad):
    index = lax.axis_index("dap")
    pos = jnp.stack([index % CORES, index, index // CORES]).astype(jnp.int32)
    same_core = [[CORES * m + c for m in range(CHIPS)] for c in range(CORES)]
    partner = [(i, i ^ 1) for i in range(N)]

    def exchange(x, groups):
        return lax.all_to_all(
            x, "dap", split_axis=0, concat_axis=0, tiled=True, axis_index_groups=groups
        )

    w_bias = w_bias.T
    gain = gain.reshape(1, FEATURES)
    pair_gain = pair_gain.reshape(1, LANES)
    sent = call(
        entry_kernel,
        jax.ShapeDtypeStruct((CHIPS, IN_ROWS, LANES), BF16),
        [
            pltpu.VMEM((N, FEATURES), BF16),
            pltpu.VMEM((N, FEATURES), BF16),
            pltpu.VMEM((1, N), jnp.int32),
            pltpu.VMEM((1, N, LANES), BF16),
            pltpu.VMEM((1, LANES), F32),
            pltpu.VMEM((HEADS, LANES), BF16),
            pltpu.VMEM((N * 4, LANES), F32),
            pltpu.VMEM((N, LANES), F32),
            pltpu.SemaphoreType.DMA((6,)),
        ],
        msa.reshape(N, FEATURES), grad.reshape(N, FEATURES), flags.reshape(1, N),
        pair, pair_gain, w_bias,
        first=HBM, rest=HBM, mib=60,
    )
    near = exchange(sent, same_core)
    far = lax.ppermute(near, "dap", partner)
    part = (CHIPS, PART_ROWS, LANES)
    own, other = call(
        sequence_kernel,
        (jax.ShapeDtypeStruct(part, F32), jax.ShapeDtypeStruct(part, BF16)),
        [pltpu.VMEM((CORES, CHIPS * IN_ROWS, LANES), F32)] + [pltpu.VMEM((CHIPS * 8, LANES), F32)] * 2,
        pos, near, far, gain, wq, wk, wv, wg, wo,
    )
    paired = (own + lax.ppermute(other, "dap", partner).astype(F32)).astype(BF16)
    got = exchange(paired, same_core)
    couple, shard = call(
        owner_kernel,
        (
            jax.ShapeDtypeStruct((1, N, LANES), BF16),
            jax.ShapeDtypeStruct((CHIPS, SUM_ROWS, LANES), BF16),
        ),
        [pltpu.VMEM((N, LANES), F32)],
        pos, got, pair, pair_gain, w_bias,
    )
    mine = exchange(shard, same_core)
    row_shape = jax.ShapeDtypeStruct((N, FEATURES), BF16)
    update, adjoint = call(
        rows_kernel,
        (row_shape, row_shape),
        [pltpu.VMEM((CHIPS * 8, LANES), F32), pltpu.VMEM((N, LANES), F32)],
        pos, got,
    )
    theirs = lax.ppermute(mine, "dap", partner)
    square = jax.ShapeDtypeStruct((FEATURES, FEATURES), F32)
    *weights, head, msa_gain, pair_gain = call(
        final_kernel,
        (square,) * 5
        + (
            jax.ShapeDtypeStruct((HEADS, LANES), F32),
            jax.ShapeDtypeStruct((1, FEATURES), F32),
            jax.ShapeDtypeStruct((1, LANES), F32),
        ),
        [],
        pos, mine, theirs,
    )
    return (
        update.reshape(N, 1, FEATURES),
        adjoint.reshape(N, 1, FEATURES),
        couple,
        *weights,
        head.T,
        msa_gain.reshape(FEATURES),
        pair_gain.reshape(LANES),
    )


def solution(mesh):
    rows = P("dp", "dap", None)
    pair = P(("dp", "dap"), None, None)
    in_specs = (rows, P("dp", "dap"), pair) + (P(),) * 8 + (rows,)
    out_specs = (rows, rows, pair) + (P("dp", None),) * 6 + (P("dp"), P("dp"))
    return jax.shard_map(
        on_device, mesh=mesh, in_specs=in_specs, out_specs=out_specs, check_vma=False
    )
```

```python
import jax
import jax.numpy as jnp
from jax import lax
from jax.experimental import pallas as pl
from jax.experimental.pallas import tpu as pltpu
from jax.sharding import PartitionSpec as P


FEATURES = 256
HEADS = 8
HEAD_DIM = 32
LANES = 128
CORES = 2
CHIPS = 64
N = CORES * CHIPS
TILES = CHIPS // 2
SCALE = HEAD_DIM ** (-0.5)
EPS = 1e-05

F32 = jnp.float32
BF16 = jnp.bfloat16

IN_ROWS = 24
PART_ROWS = 40
SUM_ROWS = 32

VMEM = pl.BlockSpec(memory_space=pltpu.VMEM)
SMEM = pl.BlockSpec(memory_space=pltpu.SMEM)
HBM = pl.BlockSpec(memory_space=pltpu.HBM)


def dot(a, b):
    return jnp.dot(a, b, preferred_element_type=F32)


def dot_nt(a, b):
    return lax.dot_general(a, b, (((1,), (1,)), ((), ())), preferred_element_type=F32)


def dot_tn(a, b):
    return lax.dot_general(a, b, (((0,), (0,)), ((), ())), preferred_element_type=F32)


def layer_norm(value, gain):
    mean = jnp.mean(value, axis=-1, keepdims=True)
    centered = value - mean
    variance = jnp.mean(centered * centered, axis=-1, keepdims=True)
    inv = lax.rsqrt(variance + EPS)
    hat = centered * inv
    return hat, inv, hat * gain


def layer_norm_adjoint(upstream, hat, inv, gain):
    ug = upstream * gain
    return inv * (
        ug
        - jnp.mean(ug, axis=-1, keepdims=True)
        - hat * jnp.mean(ug * hat, axis=-1, keepdims=True)
    )


def split(x):
    high = x.astype(BF16)
    rest = x - high.astype(F32)
    mid = rest.astype(BF16)
    return high, mid, (rest - mid.astype(F32)).astype(BF16)


def by_core(rows):
    return jnp.concatenate(
        [rows[pl.ds(c, CHIPS, stride=CORES), :] for c in range(CORES)], axis=0
    )


def call(kernel, out_shape, scratch, *operands, first=SMEM, rest=VMEM, mib=12):
    return pl.pallas_call(
        kernel,
        out_shape=out_shape,
        in_specs=[first] + [rest] * (len(operands) - 1),
        out_specs=jax.tree.map(lambda _: VMEM, out_shape),
        scratch_shapes=scratch,
        compiler_params=pltpu.CompilerParams(vmem_limit_bytes=mib * 1024 * 1024),
    )(*operands)


def entry_kernel(
    msa_hbm, grad_hbm, flags_hbm, pair_hbm, gain_hbm, w_hbm,
    out, msa, grad, flags, pair, gain, w_bias, stage, rows, sems
):
    refs = (
        (pair_hbm, pair), (gain_hbm, gain), (w_hbm, w_bias),
        (msa_hbm, msa), (grad_hbm, grad), (flags_hbm, flags),
    )
    copies = [pltpu.make_async_copy(a, b, sems.at[i]) for i, (a, b) in enumerate(refs)]
    for copy in copies:
        copy.start()
    for copy in copies[:3]:
        copy.wait()
    rows[...] = pair[0].astype(F32)
    _, _, scaled = layer_norm(by_core(rows), gain[...])
    bias = dot_nt(w_bias[...], scaled.astype(BF16)).astype(BF16)
    out[:, 8:16, :] = jnp.broadcast_to(bias[None], (CHIPS, HEADS, LANES))
    for copy in copies[3:]:
        copy.wait()
    for r, ref in enumerate((msa, grad)):
        value = ref[...].astype(F32)
        stage[pl.ds(2 * r, N, stride=4), :] = value[:, :LANES]
        stage[pl.ds(2 * r + 1, N, stride=4), :] = value[:, LANES:]
    out[:, 0:8, :] = stage[...].reshape(CHIPS, 8, LANES).astype(BF16)
    present = jnp.broadcast_to(flags[...].astype(F32), (8, LANES)).astype(BF16)
    out[:, 16:24, :] = jnp.broadcast_to(present[None], (CHIPS, 8, LANES))


def sequence_kernel(
    pos, near, far, gain_ref, wq_ref, wk_ref, wv_ref, wg_ref, wo_ref,
    own, other, rows, mine, theirs, scores_ref, dp_ref, p_ref, ds_ref
):
    core = pos[0]
    first = core == 0
    rows[core] = near[...].astype(F32).reshape(CHIPS * IN_ROWS, LANES)
    rows[1 - core] = far[...].astype(F32).reshape(CHIPS * IN_ROWS, LANES)

    def row(r):
        return jnp.concatenate(
            [rows.at[c][pl.ds(r, CHIPS, stride=IN_ROWS), :] for c in range(CORES)], axis=0
        )

    def line(r):
        return jnp.where(first, row(r), row(4 + r))

    def halves(value):
        return (
            jnp.where(first, value[:CHIPS], value[CHIPS:]),
            jnp.where(first, value[CHIPS:], value[:CHIPS]),
        )

    gain = gain_ref[...]
    msa = jnp.concatenate([line(0), line(1)], axis=1)
    grad = jnp.concatenate([line(2), line(3)], axis=1).astype(BF16)
    lane = lax.broadcasted_iota(jnp.int32, (8, LANES), 1)
    pick = jnp.where(lane == pos[1], 1.0, 0.0).astype(BF16)
    flags = dot_nt(pick, row(16).astype(BF16))[:1]
    masking = 1e9 * (flags - 1.0)
    hat, inv, scaled = layer_norm(msa, gain)
    x = scaled.astype(BF16)
    wo = wo_ref[...]
    q = (dot(x, wq_ref[...]) * SCALE).astype(BF16)
    k = dot(x, wk_ref[...]).astype(BF16)
    v = dot(x, wv_ref[...]).astype(BF16)
    gate = jax.nn.sigmoid(dot(x, wg_ref[...]))
    dw = dot_nt(grad, wo)
    d_attn = (dw * gate).astype(BF16)

    lane = lax.broadcasted_iota(jnp.int32, (1, FEATURES), 1)
    slot = (lane % LANES) // HEAD_DIM
    in_slot = [jnp.where(slot == s, 1.0, 0.0).astype(BF16) for s in range(4)]
    in_half = [jnp.where(lane // LANES == g, 1.0, 0.0).astype(BF16) for g in range(2)]

    def by_half(value):
        return jnp.concatenate([value * keep for keep in in_half], axis=0)

    def by_slot(value):
        return jnp.concatenate([value * keep for keep in in_slot], axis=0)

    k_halves, v_halves = by_half(k), by_half(v)
    scores_ref[...] = dot_nt(by_slot(q), k_halves)
    dp_ref[...] = dot_nt(by_slot(d_attn), v_halves)
    for s in range(4):
        for g in range(2):
            h = 4 * g + s
            span = (slice(s * N, (s + 1) * N), slice(g * LANES, (g + 1) * LANES))
            flat = slice((2 * s + g) * LANES, (2 * s + g + 1) * LANES)
            scores = scores_ref[span] + row(8 + h) + masking
            e = jnp.exp(scores - jnp.max(scores, axis=-1, keepdims=True))
            p32 = e * (1.0 / jnp.sum(e, axis=-1, keepdims=True))
            p_ref[:, flat] = p32.astype(BF16)
            d_p = dp_ref[span]
            d_s = p32 * (d_p - jnp.sum(p32 * d_p, axis=-1, keepdims=True))
            a, b = halves(d_s)
            mine[pl.ds(h, CHIPS, stride=HEADS), :] = a
            theirs[pl.ds(h, CHIPS, stride=HEADS), :] = b
            ds_ref[:, flat] = d_s.astype(BF16)
    own[:, 8:16, :] = mine[...].reshape(CHIPS, HEADS, LANES)
    other[:, 8:16, :] = theirs[...].reshape(CHIPS, HEADS, LANES).astype(BF16)
    attn = dot(p_ref[...], by_slot(v_halves))
    d_q = (dot(ds_ref[...], by_slot(k_halves)) * SCALE).astype(BF16)
    q_t = q.T
    da_t = d_attn.T
    dk_t = []
    dv_t = []
    for h in range(HEADS):
        g, s = divmod(h, 4)
        flat = slice((2 * s + g) * LANES, (2 * s + g + 1) * LANES)
        head = slice(h * HEAD_DIM, (h + 1) * HEAD_DIM)
        dk_t.append(dot(q_t[head], ds_ref[:, flat]))
        dv_t.append(dot(da_t[head], p_ref[:, flat]))
    d_k = jnp.concatenate(dk_t, axis=0).astype(BF16).T
    d_v = jnp.concatenate(dv_t, axis=0).astype(BF16).T
    weighted = (gate * attn).astype(BF16)
    update = dot(weighted, wo)
    d_g = (dw * attn * gate * (1.0 - gate)).astype(BF16)
    d_x = (
        dot_nt(d_q, wq_ref[...])
        + dot_nt(d_k, wk_ref[...])
        + dot_nt(d_v, wv_ref[...])
        + dot_nt(d_g, wg_ref[...])
    )
    adjoint = layer_norm_adjoint(d_x, hat, inv, gain)
    zeros = jnp.zeros((CHIPS, LANES), F32)
    for r, value in enumerate(
        (update[:, :LANES], update[:, LANES:], adjoint[:, :LANES], adjoint[:, LANES:])
    ):
        a, b = halves(value)
        mine[pl.ds(r, CHIPS, stride=8), :] = a
        mine[pl.ds(4 + r, CHIPS, stride=8), :] = zeros
        theirs[pl.ds(r, CHIPS, stride=8), :] = zeros
        theirs[pl.ds(4 + r, CHIPS, stride=8), :] = b
    own[:, 0:8, :] = mine[...].reshape(CHIPS, 8, LANES)
    other[:, 0:8, :] = theirs[...].reshape(CHIPS, 8, LANES).astype(BF16)
    x_t = x.T
    w_t = weighted.T
    pairs = ((x_t, d_q), (x_t, d_k), (x_t, d_v), (x_t, d_g), (w_t, grad))
    mats = []
    for a, b in pairs:
        turned = jnp.concatenate([b[:, LANES:], b[:, :LANES]], axis=1)
        mats.append(dot(a, jnp.where(first, b, turned)))
    d_gain = jnp.broadcast_to(jnp.sum(d_x * hat, axis=0, keepdims=True), (LANES, FEATURES)).T
    d_gain = d_gain.reshape(TILES, 8, LANES)
    low = lax.broadcasted_iota(jnp.int32, (1, 8, 1), 1) < 4
    for ref, cols in ((own, slice(0, LANES)), (other, slice(LANES, FEATURES))):
        tiles = [m[:, cols].reshape(TILES, 8, LANES) for m in mats]
        last = (jnp.where(low, tiles[4], d_gain), jnp.where(low, d_gain, tiles[4]))
        for t, (even, odd) in enumerate(((tiles[0], tiles[2]), (tiles[1], tiles[3]), last)):
            both = jnp.stack([even, odd], axis=1).reshape(CHIPS, 8, LANES)
            ref[:, 16 + 8 * t : 24 + 8 * t, :] = both.astype(ref.dtype)


def owner_kernel(pos, got, pair, gain_ref, w_ref, couple, out, rows):
    total = jnp.sum(got[:, 8:, :].astype(F32), axis=0)
    d_bias = total[:HEADS]
    gain = gain_ref[...]
    rows[...] = pair[0].astype(F32)
    hat, inv, scaled = layer_norm(by_core(rows), gain)
    pair_ln = scaled.astype(BF16)
    w_bias = w_ref[...]
    d_pln = jnp.zeros((N, LANES), F32)
    head = jnp.zeros((HEADS, LANES), F32)
    for part in reversed(split(d_bias)):
        d_pln += dot_tn(part, w_bias)
        head += dot(part, pair_ln)
    adjoint = layer_norm_adjoint(d_pln, hat, inv, gain)
    for c in range(CORES):
        rows[pl.ds(c, CHIPS, stride=CORES), :] = adjoint[c * CHIPS : (c + 1) * CHIPS]
    couple[0] = rows[...].astype(BF16)
    pair_gain = jnp.sum(d_pln * hat, axis=0, keepdims=True)
    even = pos[2] % 2 == 0
    sub = lax.broadcasted_iota(jnp.int32, (8, LANES), 0)
    lane = lax.broadcasted_iota(jnp.int32, (8, LANES), 1)
    channel = sub + 8 * (pos[2] // 2)
    kept = (sub < 4) == even
    here = jnp.logical_not(kept) & (lane + LANES * pos[0] == channel)
    msa_gain = jnp.sum(jnp.where(here, total[24:32], 0.0), axis=0, keepdims=True)
    sums = jnp.where(sub % 4 == 0, pair_gain, jnp.where(sub % 4 == 1, msa_gain, 0.0))
    shard = jnp.concatenate([total[8:24], jnp.where(kept, total[24:32], sums), head], axis=0)
    out[...] = jnp.broadcast_to(shard.astype(BF16)[None], (CHIPS, SUM_ROWS, LANES))


def rows_kernel(pos, got, update, adjoint, stage, rows):
    stage[...] = got[:, 0:8, :].astype(F32).reshape(CHIPS * 8, LANES)
    first = pos[0] == 0
    for index, out in enumerate((update, adjoint)):
        for half in range(2):
            r = 2 * index + half
            same = stage[pl.ds(r, CHIPS, stride=8), :]
            cross = stage[pl.ds(4 + r, CHIPS, stride=8), :]
            rows[pl.ds(0, CHIPS, stride=CORES), :] = jnp.where(first, same, cross)
            rows[pl.ds(1, CHIPS, stride=CORES), :] = jnp.where(first, cross, same)
            out[:, half * LANES : (half + 1) * LANES] = rows[...].astype(BF16)


def final_kernel(pos, mine, theirs, *outs):
    first = pos[0] == 0
    low = lax.broadcasted_iota(jnp.int32, (1, 8, 1), 1) < 4
    weights, (head, msa_gain, pair_gain) = outs[:5], outs[5:]
    blocks, sums, heads = [], [], []
    for ref in (mine, theirs):
        tiles = [
            ref[:, 8 * t : 8 * t + 8, :].astype(F32).reshape(TILES, 2, 8, LANES) for t in range(3)
        ]
        even, odd = tiles[2][:, 0], tiles[2][:, 1]
        blocks.append(
            (tiles[0][:, 0], tiles[1][:, 0], tiles[0][:, 1], tiles[1][:, 1],
             jnp.where(low, even, odd))
        )
        sums.append(jnp.sum(even, axis=0)[4:8] + jnp.sum(odd, axis=0)[0:4])
        heads.append(jnp.sum(ref[:, 24:32, :].astype(F32), axis=0))
    head[...] = heads[0] + heads[1]
    pair_gain[...] = sums[0][0:1] + sums[1][0:1]
    msa_gain[:, :LANES] = jnp.where(first, sums[0][1:2], sums[1][1:2])
    msa_gain[:, LANES:] = jnp.where(first, sums[1][1:2], sums[0][1:2])
    for out, same, cross in zip(weights, *blocks):
        same = same.reshape(FEATURES, LANES)
        cross = cross.reshape(FEATURES, LANES)
        out[:, :LANES] = jnp.where(first, same, cross)
        out[:, LANES:] = jnp.where(first, cross, same)


def on_device(msa, flags, pair, gain, pair_gain, wq, wk, wv, wg, wo, w_bias, grad):
    index = lax.axis_index("dap")
    pos = jnp.stack([index % CORES, index, index // CORES]).astype(jnp.int32)
    same_core = [[CORES * m + c for m in range(CHIPS)] for c in range(CORES)]
    partner = [(i, i ^ 1) for i in range(N)]

    def exchange(x, groups):
        return lax.all_to_all(
            x, "dap", split_axis=0, concat_axis=0, tiled=True, axis_index_groups=groups
        )

    w_bias = w_bias.T
    gain = gain.reshape(1, FEATURES)
    pair_gain = pair_gain.reshape(1, LANES)
    sent = call(
        entry_kernel,
        jax.ShapeDtypeStruct((CHIPS, IN_ROWS, LANES), BF16),
        [
            pltpu.VMEM((N, FEATURES), BF16),
            pltpu.VMEM((N, FEATURES), BF16),
            pltpu.VMEM((1, N), jnp.int32),
            pltpu.VMEM((1, N, LANES), BF16),
            pltpu.VMEM((1, LANES), F32),
            pltpu.VMEM((HEADS, LANES), BF16),
            pltpu.VMEM((N * 4, LANES), F32),
            pltpu.VMEM((N, LANES), F32),
            pltpu.SemaphoreType.DMA((6,)),
        ],
        msa.reshape(N, FEATURES), grad.reshape(N, FEATURES), flags.reshape(1, N),
        pair, pair_gain, w_bias,
        first=HBM, rest=HBM, mib=60,
    )
    near = exchange(sent, same_core)
    far = lax.ppermute(near, "dap", partner)
    part = (CHIPS, PART_ROWS, LANES)
    own, other = call(
        sequence_kernel,
        (jax.ShapeDtypeStruct(part, F32), jax.ShapeDtypeStruct(part, BF16)),
        [
            pltpu.VMEM((CORES, CHIPS * IN_ROWS, LANES), F32),
            pltpu.VMEM((CHIPS * 8, LANES), F32),
            pltpu.VMEM((CHIPS * 8, LANES), F32),
            pltpu.VMEM((4 * N, FEATURES), F32),
            pltpu.VMEM((4 * N, FEATURES), F32),
            pltpu.VMEM((N, HEADS * LANES), BF16),
            pltpu.VMEM((N, HEADS * LANES), BF16),
        ],
        pos, near, far, gain, wq, wk, wv, wg, wo,
    )
    paired = (own + lax.ppermute(other, "dap", partner).astype(F32)).astype(BF16)
    got = exchange(paired, same_core)
    couple, shard = call(
        owner_kernel,
        (
            jax.ShapeDtypeStruct((1, N, LANES), BF16),
            jax.ShapeDtypeStruct((CHIPS, SUM_ROWS, LANES), BF16),
        ),
        [pltpu.VMEM((N, LANES), F32)],
        pos, got, pair, pair_gain, w_bias,
    )
    mine = exchange(shard, same_core)
    row_shape = jax.ShapeDtypeStruct((N, FEATURES), BF16)
    update, adjoint = call(
        rows_kernel,
        (row_shape, row_shape),
        [pltpu.VMEM((CHIPS * 8, LANES), F32), pltpu.VMEM((N, LANES), F32)],
        pos, got,
    )
    theirs = lax.ppermute(mine, "dap", partner)
    square = jax.ShapeDtypeStruct((FEATURES, FEATURES), F32)
    *weights, head, msa_gain, pair_gain = call(
        final_kernel,
        (square,) * 5
        + (
            jax.ShapeDtypeStruct((HEADS, LANES), F32),
            jax.ShapeDtypeStruct((1, FEATURES), F32),
            jax.ShapeDtypeStruct((1, LANES), F32),
        ),
        [],
        pos, mine, theirs,
    )
    return (
        update.reshape(N, 1, FEATURES),
        adjoint.reshape(N, 1, FEATURES),
        couple,
        *weights,
        head.T,
        msa_gain.reshape(FEATURES),
        pair_gain.reshape(LANES),
    )


def solution(mesh):
    rows = P("dp", "dap", None)
    pair = P(("dp", "dap"), None, None)
    in_specs = (rows, P("dp", "dap"), pair) + (P(),) * 8 + (rows,)
    out_specs = (rows, rows, pair) + (P("dp", None),) * 6 + (P("dp"), P("dp"))
    return jax.shard_map(
        on_device, mesh=mesh, in_specs=in_specs, out_specs=out_specs, check_vma=False
    )
```

```python
import jax
import jax.numpy as jnp
from jax import lax
from jax.experimental import pallas as pl
from jax.experimental.pallas import tpu as pltpu
from jax.sharding import PartitionSpec as P


FEATURES = 256
HEADS = 8
HEAD_DIM = 32
LANES = 128
CORES = 2
CHIPS = 64
N = CORES * CHIPS
TILES = CHIPS // 2
SCALE = HEAD_DIM ** (-0.5)
EPS = 1e-05

F32 = jnp.float32
BF16 = jnp.bfloat16

IN_ROWS = 18
PART_ROWS = 36
PART_TILES = 9
SUM_ROWS = 32

VMEM = pl.BlockSpec(memory_space=pltpu.VMEM)
SMEM = pl.BlockSpec(memory_space=pltpu.SMEM)
HBM = pl.BlockSpec(memory_space=pltpu.HBM)


def dot(a, b):
    return jnp.dot(a, b, preferred_element_type=F32)


def dot_nt(a, b):
    return lax.dot_general(a, b, (((1,), (1,)), ((), ())), preferred_element_type=F32)


def dot_tn(a, b):
    return lax.dot_general(a, b, (((0,), (0,)), ((), ())), preferred_element_type=F32)


def layer_norm(value, gain):
    mean = jnp.mean(value, axis=-1, keepdims=True)
    centered = value - mean
    variance = jnp.mean(centered * centered, axis=-1, keepdims=True)
    inv = lax.rsqrt(variance + EPS)
    hat = centered * inv
    return hat, inv, hat * gain


def layer_norm_adjoint(upstream, hat, inv, gain):
    ug = upstream * gain
    return inv * (
        ug
        - jnp.mean(ug, axis=-1, keepdims=True)
        - hat * jnp.mean(ug * hat, axis=-1, keepdims=True)
    )


def split(x):
    high = x.astype(BF16)
    rest = x - high.astype(F32)
    mid = rest.astype(BF16)
    return high, mid, (rest - mid.astype(F32)).astype(BF16)


ORDER = [(c, p) for c in range(CORES) for p in range(2)]


def reordered(rows):
    return jnp.concatenate(
        [rows[pl.ds(2 * p + c, TILES, stride=4), :] for c, p in ORDER], axis=0
    )


def restore(rows, value):
    for n, (c, p) in enumerate(ORDER):
        rows[pl.ds(2 * p + c, TILES, stride=4), :] = value[n * TILES : (n + 1) * TILES]


def bias_row(h):
    return 4 + h if h < 5 else 8 + h


def call(
    kernel, out_shape, scratch, *operands, first=SMEM, rest=VMEM, mib=12, far_in=0, far_out=0
):
    out_specs = jax.tree.map(lambda _: VMEM, out_shape)
    if far_out:
        out_specs = (HBM,) * far_out + out_specs[far_out:]
    count = len(operands)
    return pl.pallas_call(
        kernel,
        out_shape=out_shape,
        in_specs=[first] + [rest] * (count - 1 - far_in) + [HBM] * far_in,
        out_specs=out_specs,
        scratch_shapes=scratch,
        input_output_aliases={count - far_in + i: i for i in range(far_in)},
        compiler_params=pltpu.CompilerParams(vmem_limit_bytes=mib * 1024 * 1024),
    )(*operands)


def entry_kernel(
    msa_hbm, grad_hbm, flags_hbm, pair_hbm, gain_hbm, w_hbm,
    out, msa, grad, flags, pair, gain, w_bias, stage, rows, sems
):
    refs = (
        (pair_hbm, pair), (gain_hbm, gain), (w_hbm, w_bias),
        (msa_hbm, msa), (grad_hbm, grad), (flags_hbm, flags),
    )
    copies = [pltpu.make_async_copy(a, b, sems.at[i]) for i, (a, b) in enumerate(refs)]
    for copy in copies:
        copy.start()
    for copy in copies[:3]:
        copy.wait()
    rows[...] = pair[0].astype(F32)
    _, _, scaled = layer_norm(reordered(rows), gain[...])
    bias = dot_nt(w_bias[...], scaled.astype(BF16))
    for copy in copies[3:]:
        copy.wait()
    for r, ref in enumerate((msa, grad)):
        value = ref[...].astype(F32)
        stage[pl.ds(2 * r, N, stride=9), :] = value[:, :LANES]
        stage[pl.ds(2 * r + 1, N, stride=9), :] = value[:, LANES:]
    lines = [(bias_row(h), bias[h : h + 1]) for h in range(HEADS)]
    lines += [(16, flags[...].astype(F32)), (17, jnp.zeros((1, LANES), F32))]
    for r, value in lines:
        stage[pl.ds(r, CHIPS, stride=IN_ROWS), :] = jnp.broadcast_to(value, (CHIPS, LANES))
    out[...] = stage[...].astype(BF16)


def sequence_kernel(
    pos, near, far, gain_ref, wq_ref, wk_ref, wv_ref, wg_ref, wo_ref,
    own, other, gain_out, rows, mine, theirs, scores_ref, dp_ref, p_ref, ds_ref
):
    core = pos[0]
    first = core == 0
    rows[core] = near[...].astype(F32)
    rows[1 - core] = far[...].astype(F32)

    def row(r):
        return jnp.concatenate(
            [
                rows.at[c][pl.ds(r + p * IN_ROWS, TILES, stride=2 * IN_ROWS), :]
                for c, p in ORDER
            ],
            axis=0,
        )

    def line(r):
        return jnp.where(first, row(r), row(9 + r))

    def halves(value):
        return (
            jnp.where(first, value[:CHIPS], value[CHIPS:]),
            jnp.where(first, value[CHIPS:], value[:CHIPS]),
        )

    gain = gain_ref[...]
    msa = jnp.concatenate([line(0), line(1)], axis=1)
    grad = jnp.concatenate([line(2), line(3)], axis=1).astype(BF16)
    lane = lax.broadcasted_iota(jnp.int32, (8, LANES), 1)
    pick = jnp.where(lane == pos[1], 1.0, 0.0).astype(BF16)
    flags = dot_nt(pick, row(16).astype(BF16))[:1]
    masking = 1e9 * (flags - 1.0)
    hat, inv, scaled = layer_norm(msa, gain)
    x = scaled.astype(BF16)
    wo = wo_ref[...]
    q = (dot(x, wq_ref[...]) * SCALE).astype(BF16)
    k = dot(x, wk_ref[...]).astype(BF16)
    v = dot(x, wv_ref[...]).astype(BF16)
    gate = jax.nn.sigmoid(dot(x, wg_ref[...]))
    dw = dot_nt(grad, wo)
    d_attn = (dw * gate).astype(BF16)

    lane = lax.broadcasted_iota(jnp.int32, (1, FEATURES), 1)
    slot = (lane % LANES) // HEAD_DIM
    in_slot = [jnp.where(slot == s, 1.0, 0.0).astype(BF16) for s in range(4)]
    in_half = [jnp.where(lane // LANES == g, 1.0, 0.0).astype(BF16) for g in range(2)]

    def by_half(value):
        return jnp.concatenate([value * keep for keep in in_half], axis=0)

    def by_slot(value):
        return jnp.concatenate([value * keep for keep in in_slot], axis=0)

    def put(even, odd):
        for ref, rows8 in ((own, mine), (other, theirs)):
            value = rows8[...].astype(ref.dtype).reshape(2, TILES, 8, LANES)
            ref[:, even] = value[0]
            ref[:, odd] = value[1]

    k_halves, v_halves = by_half(k), by_half(v)
    scores_ref[...] = dot_nt(by_slot(q), k_halves)
    dp_ref[...] = dot_nt(by_slot(d_attn), v_halves)
    for s in range(4):
        for g in range(2):
            h = 4 * g + s
            span = (slice(s * N, (s + 1) * N), slice(g * LANES, (g + 1) * LANES))
            flat = slice((2 * s + g) * LANES, (2 * s + g + 1) * LANES)
            scores = scores_ref[span] + row(bias_row(h)) + masking
            e = jnp.exp(scores - jnp.max(scores, axis=-1, keepdims=True))
            p32 = e * (1.0 / jnp.sum(e, axis=-1, keepdims=True))
            p_ref[:, flat] = p32.astype(BF16)
            d_p = dp_ref[span]
            d_s = p32 * (d_p - jnp.sum(p32 * d_p, axis=-1, keepdims=True))
            a, b = halves(d_s)
            mine[pl.ds(h, CHIPS, stride=HEADS), :] = a
            theirs[pl.ds(h, CHIPS, stride=HEADS), :] = b
            ds_ref[:, flat] = d_s.astype(BF16)
    put(1, 6)
    attn = dot(p_ref[...], by_slot(v_halves))
    d_q = (dot(ds_ref[...], by_slot(k_halves)) * SCALE).astype(BF16)
    q_t = q.T
    da_t = d_attn.T
    dk_t = []
    dv_t = []
    for h in range(HEADS):
        g, s = divmod(h, 4)
        flat = slice((2 * s + g) * LANES, (2 * s + g + 1) * LANES)
        head = slice(h * HEAD_DIM, (h + 1) * HEAD_DIM)
        dk_t.append(dot(q_t[head], ds_ref[:, flat]))
        dv_t.append(dot(da_t[head], p_ref[:, flat]))
    d_k = jnp.concatenate(dk_t, axis=0).astype(BF16).T
    d_v = jnp.concatenate(dv_t, axis=0).astype(BF16).T
    weighted = (gate * attn).astype(BF16)
    update = dot(weighted, wo)
    d_g = (dw * attn * gate * (1.0 - gate)).astype(BF16)
    d_x = (
        dot_nt(d_q, wq_ref[...])
        + dot_nt(d_k, wk_ref[...])
        + dot_nt(d_v, wv_ref[...])
        + dot_nt(d_g, wg_ref[...])
    )
    adjoint = layer_norm_adjoint(d_x, hat, inv, gain)
    zeros = jnp.zeros((CHIPS, LANES), F32)
    for r, value in enumerate(
        (update[:, :LANES], update[:, LANES:], adjoint[:, :LANES], adjoint[:, LANES:])
    ):
        a, b = halves(value)
        mine[pl.ds(r, CHIPS, stride=8), :] = a
        mine[pl.ds(4 + r, CHIPS, stride=8), :] = zeros
        theirs[pl.ds(r, CHIPS, stride=8), :] = zeros
        theirs[pl.ds(4 + r, CHIPS, stride=8), :] = b
    put(0, 5)
    gain_out[...] = jnp.sum(d_x * hat, axis=0, keepdims=True)
    x_t = x.T
    w_t = weighted.T
    pairs = ((x_t, d_q), (x_t, d_k), (x_t, d_v), (x_t, d_g), (w_t, grad))
    mats = []
    for a, b in pairs:
        turned = jnp.concatenate([b[:, LANES:], b[:, :LANES]], axis=1)
        mats.append(dot(a, jnp.where(first, b, turned)))
    for ref, cols in ((own, slice(0, LANES)), (other, slice(LANES, FEATURES))):
        for tile, m in zip((2, 3, 7, 8, 4), mats):
            ref[:, tile] = m[:, cols].reshape(TILES, 8, LANES).astype(ref.dtype)


def pair_gradient(d_bias, pair, gain, w_bias, rows):
    rows[...] = pair[0].astype(F32)
    hat, inv, scaled = layer_norm(reordered(rows), gain)
    parts = split(d_bias)[::-1]
    d_pln = sum(dot_tn(part, w_bias) for part in parts)
    head = sum(dot(part, scaled.astype(BF16)) for part in parts)
    return hat, inv, d_pln, head


def owner_kernel(pos, got, pair, gain, w_bias, d_gain, out, d_bias_out, rows, sums):
    value = got[...].astype(F32).reshape(TILES, 2 * PART_ROWS, LANES)
    sums[...] = jnp.sum(value, axis=0)
    total = sums[0:PART_ROWS, :] + sums[PART_ROWS:, :]
    sums[0:PART_ROWS, :] = total
    even = pos[2] % 2 == 0
    d_bias = jnp.where(even, sums[8:16, :], sums[12:20, :])
    weights = jnp.where(even, sums[16:32, :], sums[20:36, :])
    fifth = jnp.where(even, sums[32:36, :], sums[0:4, :])
    d_bias_out[...] = d_bias
    hat, _, d_pln, head = pair_gradient(d_bias, pair, gain[...], w_bias[...], rows)
    shard = jnp.concatenate(
        [
            weights,
            fifth,
            jnp.sum(d_pln * hat, axis=0, keepdims=True),
            d_gain[:, :LANES],
            d_gain[:, LANES:],
            jnp.zeros((1, LANES), F32),
            head,
        ],
        axis=0,
    )
    out[...] = jnp.broadcast_to(shard.astype(BF16)[None], (CHIPS, SUM_ROWS, LANES))


def unpack_kernel(pos, got, d_bias, pair, gain_ref, w_bias, update, adjoint, couple, stage, rows):
    stage[...] = got[...].astype(F32)
    first = pos[0] == 0
    even = pos[2] % 2 == 0

    def line(r):
        a, b = (stage[pl.ds(k, CHIPS, stride=PART_ROWS), :] for k in (r, 4 + r))
        return jnp.where(even, a, b)

    for index, out in enumerate((update, adjoint)):
        for half in range(2):
            r = 2 * index + half
            same, cross = line(r), line(4 + r)
            rows[pl.ds(0, CHIPS, stride=CORES), :] = jnp.where(first, same, cross)
            rows[pl.ds(1, CHIPS, stride=CORES), :] = jnp.where(first, cross, same)
            out[:, half * LANES : (half + 1) * LANES] = rows[...].astype(BF16)
    gain = gain_ref[...]
    hat, inv, d_pln, _ = pair_gradient(d_bias[...], pair, gain, w_bias[...], rows)
    restore(rows, layer_norm_adjoint(d_pln, hat, inv, gain))
    couple[0] = rows[...].astype(BF16)


def half_kernel(side, pos, got, sums_ref, weights, stage, sems):
    column = pl.multiple_of(LANES * jnp.bitwise_xor(pos[0], side), LANES)
    low = lax.broadcasted_iota(jnp.int32, (1, 8, 1), 1) < 4

    def tile(t):
        return got[:, 8 * t : 8 * t + 8, :].astype(F32).reshape(TILES, 2, 8, LANES)

    copies = []

    def put(w, value):
        stage[w] = value.reshape(FEATURES, LANES)
        copy = pltpu.make_async_copy(
            stage.at[w], weights[w].at[:, pl.ds(column, LANES)], sems.at[w]
        )
        copy.start()
        copies.append(copy)

    for t in range(2):
        both = tile(t)
        put(t, both[:, 0])
        put(2 + t, both[:, 1])
    last = tile(2)
    put(4, jnp.where(low, last[:, 0], pltpu.roll(last[:, 1], 4, 1)))
    sums_ref[0] = jnp.sum(got[:, 24:32, :].astype(F32), axis=0)
    sums_ref[1] = jnp.sum(got[:, 16:24, :].astype(F32), axis=0)
    for copy in copies:
        copy.wait()


def near_kernel(pos, got, *refs):
    half_kernel(0, pos, got, refs[5], refs[:5], *refs[6:])


def far_kernel(pos, got, near_sums, *refs):
    weights, (head, msa_gain, pair_gain), (sums, stage, sems) = refs[5:10], refs[10:13], refs[13:]
    half_kernel(1, pos, got, sums, weights, stage, sems)
    head[...] = near_sums[0] + sums[0]
    gains = near_sums[1] + sums[1]
    pair_gain[...] = gains[4:5]
    msa_gain[:, :LANES] = gains[5:6]
    msa_gain[:, LANES:] = gains[6:7]


def on_device(msa, flags, pair, gain, pair_gain, wq, wk, wv, wg, wo, w_bias, grad):
    index = lax.axis_index("dap")
    pos = jnp.stack([index % CORES, index, index // CORES]).astype(jnp.int32)
    same_core = [[CORES * m + c for m in range(CHIPS)] for c in range(CORES)]
    partner = [(i, i ^ 1) for i in range(N)]

    def exchange(x, groups):
        return lax.all_to_all(
            x, "dap", split_axis=0, concat_axis=0, tiled=True, axis_index_groups=groups
        )

    w_bias = w_bias.T
    gain = gain.reshape(1, FEATURES)
    pair_gain = pair_gain.reshape(1, LANES)
    sent = call(
        entry_kernel,
        jax.ShapeDtypeStruct((CHIPS * IN_ROWS, LANES), BF16),
        [
            pltpu.VMEM((N, FEATURES), BF16),
            pltpu.VMEM((N, FEATURES), BF16),
            pltpu.VMEM((1, N), jnp.int32),
            pltpu.VMEM((1, N, LANES), BF16),
            pltpu.VMEM((1, LANES), F32),
            pltpu.VMEM((HEADS, LANES), BF16),
            pltpu.VMEM((CHIPS * IN_ROWS, LANES), F32),
            pltpu.VMEM((N, LANES), F32),
            pltpu.SemaphoreType.DMA((6,)),
        ],
        msa.reshape(N, FEATURES), grad.reshape(N, FEATURES), flags.reshape(1, N),
        pair, pair_gain, w_bias,
        first=HBM, rest=HBM, mib=60,
    )
    near = exchange(sent.reshape(CHIPS, IN_ROWS // 2, 2, LANES), same_core)
    near = near.reshape(CHIPS * IN_ROWS, LANES)
    far = lax.ppermute(near, "dap", partner)
    part = (TILES, PART_TILES, 8, LANES)
    own, other, d_gain = call(
        sequence_kernel,
        (
            jax.ShapeDtypeStruct(part, F32),
            jax.ShapeDtypeStruct(part, BF16),
            jax.ShapeDtypeStruct((1, FEATURES), F32),
        ),
        [
            pltpu.VMEM((CORES, CHIPS * IN_ROWS, LANES), F32),
            pltpu.VMEM((CHIPS * 8, LANES), F32),
            pltpu.VMEM((CHIPS * 8, LANES), F32),
            pltpu.VMEM((4 * N, FEATURES), F32),
            pltpu.VMEM((4 * N, FEATURES), F32),
            pltpu.VMEM((N, HEADS * LANES), BF16),
            pltpu.VMEM((N, HEADS * LANES), BF16),
        ],
        pos, near, far, gain, wq, wk, wv, wg, wo,
    )
    paired = (own + lax.ppermute(other, "dap", partner).astype(F32)).astype(BF16)
    got = exchange(paired.reshape(CHIPS, PART_TILES, 4, LANES), same_core)
    got = got.reshape(CHIPS * PART_ROWS, LANES)
    shard, d_bias = call(
        owner_kernel,
        (
            jax.ShapeDtypeStruct((CHIPS, SUM_ROWS, LANES), BF16),
            jax.ShapeDtypeStruct((HEADS, LANES), F32),
        ),
        [pltpu.VMEM((N, LANES), F32), pltpu.VMEM((2 * PART_ROWS, LANES), F32)],
        pos, got, pair, pair_gain, w_bias, d_gain,
    )
    mine = exchange(shard, same_core)
    row_shape = jax.ShapeDtypeStruct((N, FEATURES), BF16)
    update, adjoint, couple = call(
        unpack_kernel,
        (row_shape, row_shape, jax.ShapeDtypeStruct((1, N, LANES), BF16)),
        [pltpu.VMEM((CHIPS * PART_ROWS, LANES), F32), pltpu.VMEM((N, LANES), F32)],
        pos, got, d_bias, pair, pair_gain, w_bias,
    )
    theirs = lax.ppermute(mine, "dap", partner)
    squares = (jax.ShapeDtypeStruct((FEATURES, FEATURES), F32),) * 5
    sums_shape = (2, 8, LANES)
    scratch = [pltpu.VMEM((5, FEATURES, LANES), F32), pltpu.SemaphoreType.DMA((5,))]
    *weights, sums = call(
        near_kernel, squares + (jax.ShapeDtypeStruct(sums_shape, F32),), scratch, pos, mine, far_out=5
    )
    *weights, head, msa_gain, pair_gain = call(
        far_kernel,
        squares
        + (
            jax.ShapeDtypeStruct((HEADS, LANES), F32),
            jax.ShapeDtypeStruct((1, FEATURES), F32),
            jax.ShapeDtypeStruct((1, LANES), F32),
        ),
        [pltpu.VMEM(sums_shape, F32)] + scratch,
        pos, theirs, sums, *weights,
        far_in=5, far_out=5,
    )
    return (
        update.reshape(N, 1, FEATURES),
        adjoint.reshape(N, 1, FEATURES),
        couple,
        *weights,
        head.T,
        msa_gain.reshape(FEATURES),
        pair_gain.reshape(LANES),
    )


def solution(mesh):
    rows = P("dp", "dap", None)
    pair = P(("dp", "dap"), None, None)
    in_specs = (rows, P("dp", "dap"), pair) + (P(),) * 8 + (rows,)
    out_specs = (rows, rows, pair) + (P("dp", None),) * 6 + (P("dp"), P("dp"))
    return jax.shard_map(
        on_device, mesh=mesh, in_specs=in_specs, out_specs=out_specs, check_vma=False
    )
```

```python
import jax
import jax.numpy as jnp
from jax import lax
from jax.experimental import pallas as pl
from jax.experimental.pallas import tpu as pltpu
from jax.sharding import PartitionSpec as P


FEATURES = 256
HEADS = 8
HEAD_DIM = 32
LANES = 128
CORES = 2
CHIPS = 64
N = CORES * CHIPS
TILES = CHIPS // 2
SCALE = HEAD_DIM ** (-0.5)
EPS = 1e-05

F32 = jnp.float32
BF16 = jnp.bfloat16

IN_ROWS = 18
PART_ROWS = 36
PART_TILES = 9
SUM_ROWS = 32
LINE = 8
LINE_TILES = 22

VMEM = pl.BlockSpec(memory_space=pltpu.VMEM)
SMEM = pl.BlockSpec(memory_space=pltpu.SMEM)
HBM = pl.BlockSpec(memory_space=pltpu.HBM)


def dot(a, b):
    return jnp.dot(a, b, preferred_element_type=F32)


def dot_nt(a, b):
    return lax.dot_general(a, b, (((1,), (1,)), ((), ())), preferred_element_type=F32)


def dot_tn(a, b):
    return lax.dot_general(a, b, (((0,), (0,)), ((), ())), preferred_element_type=F32)


def layer_norm(value, gain):
    mean = jnp.mean(value, axis=-1, keepdims=True)
    centered = value - mean
    variance = jnp.mean(centered * centered, axis=-1, keepdims=True)
    inv = lax.rsqrt(variance + EPS)
    hat = centered * inv
    return hat, inv, hat * gain


def layer_norm_adjoint(upstream, hat, inv, gain):
    ug = upstream * gain
    return inv * (
        ug
        - jnp.mean(ug, axis=-1, keepdims=True)
        - hat * jnp.mean(ug * hat, axis=-1, keepdims=True)
    )


def split(x):
    high = x.astype(BF16)
    rest = x - high.astype(F32)
    mid = rest.astype(BF16)
    return high, mid, (rest - mid.astype(F32)).astype(BF16)


ORDER = [(c, p) for c in range(CORES) for p in range(2)]


def reordered(rows):
    return jnp.concatenate(
        [rows[pl.ds(2 * p + c, TILES, stride=4), :] for c, p in ORDER], axis=0
    )


def restore(rows, value):
    for n, (c, p) in enumerate(ORDER):
        rows[pl.ds(2 * p + c, TILES, stride=4), :] = value[n * TILES : (n + 1) * TILES]


def bias_row(h):
    return 4 + h if h < 5 else 8 + h


def call(kernel, out_shape, scratch, *operands, first=SMEM, rest=VMEM, mib=12, far_out=0):
    out_specs = jax.tree.map(lambda _: VMEM, out_shape)
    if far_out:
        out_specs = (HBM,) * far_out + out_specs[far_out:]
    return pl.pallas_call(
        kernel,
        out_shape=out_shape,
        in_specs=[first] + [rest] * (len(operands) - 1),
        out_specs=out_specs,
        scratch_shapes=scratch,
        compiler_params=pltpu.CompilerParams(vmem_limit_bytes=mib * 1024 * 1024),
    )(*operands)


def entry_kernel(
    msa_hbm, grad_hbm, flags_hbm, pair_hbm, gain_hbm, w_hbm,
    out, msa, grad, flags, pair, gain, w_bias, stage, rows, sems
):
    refs = (
        (pair_hbm, pair), (gain_hbm, gain), (w_hbm, w_bias),
        (msa_hbm, msa), (grad_hbm, grad), (flags_hbm, flags),
    )
    copies = [pltpu.make_async_copy(a, b, sems.at[i]) for i, (a, b) in enumerate(refs)]
    for copy in copies:
        copy.start()
    for copy in copies[:3]:
        copy.wait()
    rows[...] = pair[0].astype(F32)
    _, _, scaled = layer_norm(reordered(rows), gain[...])
    bias = dot_nt(w_bias[...], scaled.astype(BF16))
    for copy in copies[3:]:
        copy.wait()
    for r, ref in enumerate((msa, grad)):
        value = ref[...].astype(F32)
        stage[pl.ds(2 * r, N, stride=9), :] = value[:, :LANES]
        stage[pl.ds(2 * r + 1, N, stride=9), :] = value[:, LANES:]
    lines = [(bias_row(h), bias[h : h + 1]) for h in range(HEADS)]
    lines += [(16, flags[...].astype(F32)), (17, jnp.zeros((1, LANES), F32))]
    for r, value in lines:
        stage[pl.ds(r, CHIPS, stride=IN_ROWS), :] = jnp.broadcast_to(value, (CHIPS, LANES))
    out[...] = stage[...].astype(BF16)


def sequence_kernel(
    pos, near, far, gain_ref, wq_ref, wk_ref, wv_ref, wg_ref, wo_ref,
    own, other, gain_out, rows, mine, theirs, scores_ref, dp_ref, p_ref, ds_ref
):
    core = pos[0]
    first = core == 0
    rows[core] = near[...].astype(F32)
    rows[1 - core] = far[...].astype(F32)

    def row(r):
        return jnp.concatenate(
            [
                rows.at[c][pl.ds(r + p * IN_ROWS, TILES, stride=2 * IN_ROWS), :]
                for c, p in ORDER
            ],
            axis=0,
        )

    def line(r):
        return jnp.where(first, row(r), row(9 + r))

    def halves(value):
        return (
            jnp.where(first, value[:CHIPS], value[CHIPS:]),
            jnp.where(first, value[CHIPS:], value[:CHIPS]),
        )

    gain = gain_ref[0:1, :]
    msa = jnp.concatenate([line(0), line(1)], axis=1)
    grad = jnp.concatenate([line(2), line(3)], axis=1).astype(BF16)
    lane = lax.broadcasted_iota(jnp.int32, (8, LANES), 1)
    pick = jnp.where(lane == pos[1], 1.0, 0.0).astype(BF16)
    flags = dot_nt(pick, row(16).astype(BF16))[:1]
    masking = 1e9 * (flags - 1.0)
    hat, inv, scaled = layer_norm(msa, gain)
    x = scaled.astype(BF16)
    wo = wo_ref[...]
    q = (dot(x, wq_ref[...]) * SCALE).astype(BF16)
    k = dot(x, wk_ref[...]).astype(BF16)
    v = dot(x, wv_ref[...]).astype(BF16)
    gate = jax.nn.sigmoid(dot(x, wg_ref[...]))
    dw = dot_nt(grad, wo)
    d_attn = (dw * gate).astype(BF16)

    lane = lax.broadcasted_iota(jnp.int32, (1, FEATURES), 1)
    slot = (lane % LANES) // HEAD_DIM
    in_slot = [jnp.where(slot == s, 1.0, 0.0).astype(BF16) for s in range(4)]
    in_half = [jnp.where(lane // LANES == g, 1.0, 0.0).astype(BF16) for g in range(2)]

    def by_half(value):
        return jnp.concatenate([value * keep for keep in in_half], axis=0)

    def by_slot(value):
        return jnp.concatenate([value * keep for keep in in_slot], axis=0)

    def put(even, odd):
        for ref, rows8 in ((own, mine), (other, theirs)):
            value = rows8[...].astype(ref.dtype).reshape(2, TILES, 8, LANES)
            ref[:, even] = value[0]
            ref[:, odd] = value[1]

    k_halves, v_halves = by_half(k), by_half(v)
    scores_ref[...] = dot_nt(by_slot(q), k_halves)
    dp_ref[...] = dot_nt(by_slot(d_attn), v_halves)
    for s in range(4):
        for g in range(2):
            h = 4 * g + s
            span = (slice(s * N, (s + 1) * N), slice(g * LANES, (g + 1) * LANES))
            flat = slice((2 * s + g) * LANES, (2 * s + g + 1) * LANES)
            scores = scores_ref[span] + row(bias_row(h)) + masking
            e = jnp.exp(scores - jnp.max(scores, axis=-1, keepdims=True))
            p32 = e * (1.0 / jnp.sum(e, axis=-1, keepdims=True))
            p_ref[:, flat] = p32.astype(BF16)
            d_p = dp_ref[span]
            d_s = p32 * (d_p - jnp.sum(p32 * d_p, axis=-1, keepdims=True))
            a, b = halves(d_s)
            mine[pl.ds(h, CHIPS, stride=HEADS), :] = a
            theirs[pl.ds(h, CHIPS, stride=HEADS), :] = b
            ds_ref[:, flat] = d_s.astype(BF16)
    put(1, 6)
    attn = dot(p_ref[...], by_slot(v_halves))
    d_q = (dot(ds_ref[...], by_slot(k_halves)) * SCALE).astype(BF16)
    q_t = q.T
    da_t = d_attn.T
    dk_t = []
    dv_t = []
    for h in range(HEADS):
        g, s = divmod(h, 4)
        flat = slice((2 * s + g) * LANES, (2 * s + g + 1) * LANES)
        head = slice(h * HEAD_DIM, (h + 1) * HEAD_DIM)
        dk_t.append(dot(q_t[head], ds_ref[:, flat]))
        dv_t.append(dot(da_t[head], p_ref[:, flat]))
    d_k = jnp.concatenate(dk_t, axis=0).astype(BF16).T
    d_v = jnp.concatenate(dv_t, axis=0).astype(BF16).T
    weighted = (gate * attn).astype(BF16)
    update = dot(weighted, wo)
    d_g = (dw * attn * gate * (1.0 - gate)).astype(BF16)
    d_x = (
        dot_nt(d_q, wq_ref[...])
        + dot_nt(d_k, wk_ref[...])
        + dot_nt(d_v, wv_ref[...])
        + dot_nt(d_g, wg_ref[...])
    )
    adjoint = layer_norm_adjoint(d_x, hat, inv, gain)
    zeros = jnp.zeros((CHIPS, LANES), F32)
    for r, value in enumerate(
        (update[:, :LANES], update[:, LANES:], adjoint[:, :LANES], adjoint[:, LANES:])
    ):
        a, b = halves(value)
        mine[pl.ds(r, CHIPS, stride=8), :] = a
        mine[pl.ds(4 + r, CHIPS, stride=8), :] = zeros
        theirs[pl.ds(r, CHIPS, stride=8), :] = zeros
        theirs[pl.ds(4 + r, CHIPS, stride=8), :] = b
    put(0, 5)
    gain_out[...] = jnp.sum(d_x * hat, axis=0, keepdims=True)
    x_t = x.T
    w_t = weighted.T
    pairs = ((x_t, d_q), (x_t, d_k), (x_t, d_v), (x_t, d_g), (w_t, grad))
    mats = []
    for a, b in pairs:
        turned = jnp.concatenate([b[:, LANES:], b[:, :LANES]], axis=1)
        mats.append(dot(a, jnp.where(first, b, turned)))
    for ref, cols in ((own, slice(0, LANES)), (other, slice(LANES, FEATURES))):
        for tile, m in zip((2, 3, 7, 8, 4), mats):
            ref[:, tile] = m[:, cols].reshape(TILES, 8, LANES).astype(ref.dtype)


def pair_gradient(d_bias, pair, gain, w_bias, rows):
    rows[...] = pair[0].astype(F32)
    hat, inv, scaled = layer_norm(reordered(rows), gain)
    parts = split(d_bias)[::-1]
    d_pln = sum(dot_tn(part, w_bias) for part in parts)
    head = sum(dot(part, scaled.astype(BF16)) for part in parts)
    return hat, inv, d_pln, head


def owner_kernel(pos, got, pair, gain, w_bias, d_gain, out, d_bias_out, rows, sums):
    value = got[...].astype(F32).reshape(TILES, 2 * PART_ROWS, LANES)
    sums[...] = jnp.sum(value, axis=0)
    total = sums[0:PART_ROWS, :] + sums[PART_ROWS:, :]
    sums[0:PART_ROWS, :] = total
    even = pos[2] % 2 == 0
    d_bias = jnp.where(even, sums[8:16, :], sums[12:20, :])
    weights = jnp.where(even, sums[16:32, :], sums[20:36, :])
    fifth = jnp.where(even, sums[32:36, :], sums[0:4, :])
    d_bias_out[...] = d_bias
    hat, _, d_pln, head = pair_gradient(d_bias, pair, gain[...], w_bias[...], rows)
    shard = jnp.concatenate(
        [
            weights,
            fifth,
            jnp.sum(d_pln * hat, axis=0, keepdims=True),
            d_gain[:, :LANES],
            d_gain[:, LANES:],
            jnp.zeros((1, LANES), F32),
            head,
        ],
        axis=0,
    )
    out[...] = jnp.broadcast_to(shard.astype(BF16)[None], (LINE, SUM_ROWS, LANES))


def unpack_kernel(pos, got, d_bias, pair, gain_ref, w_bias, update, adjoint, couple, stage, rows):
    stage[...] = got[...].astype(F32)
    first = pos[0] == 0
    even = pos[2] % 2 == 0

    def line(r):
        a, b = (stage[pl.ds(k, CHIPS, stride=PART_ROWS), :] for k in (r, 4 + r))
        return jnp.where(even, a, b)

    for index, out in enumerate((update, adjoint)):
        for half in range(2):
            r = 2 * index + half
            same, cross = line(r), line(4 + r)
            rows[pl.ds(0, CHIPS, stride=CORES), :] = jnp.where(first, same, cross)
            rows[pl.ds(1, CHIPS, stride=CORES), :] = jnp.where(first, cross, same)
            out[:, half * LANES : (half + 1) * LANES] = rows[...].astype(BF16)
    gain = gain_ref[...]
    hat, inv, d_pln, _ = pair_gradient(d_bias[...], pair, gain, w_bias[...], rows)
    restore(rows, layer_norm_adjoint(d_pln, hat, inv, gain))
    couple[0] = rows[...].astype(BF16)


def line_kernel(pos, got, out):
    low = lax.broadcasted_iota(jnp.int32, (1, 8, 1), 1) < 4
    tiles = got[...].astype(F32).reshape(LINE // 2, 2, 4, 8, LANES)
    even, odd = tiles[:, 0], tiles[:, 1]
    fifth = jnp.where(low, even[:, 2], pltpu.roll(odd[:, 2], 4, 1))
    sums = jnp.sum(tiles[:, :, 2:], axis=(0, 1))
    weights = (even[:, 0], even[:, 1], fifth, odd[:, 0], odd[:, 1])
    for w, value in enumerate(weights):
        value = value.astype(BF16)
        for t in range(LINE // 2):
            out[:, 5 * t + w] = jnp.broadcast_to(value[t][None], (LINE, 8, LANES))
    for n in range(2):
        out[:, 20 + n] = jnp.broadcast_to(sums[n].astype(BF16)[None], (LINE, 8, LANES))


def final_kernel(pos, mine, theirs, *refs):
    weights, (head, msa_gain, pair_gain), (stage, sems) = refs[:5], refs[5:8], refs[8:]
    copies = []
    sums = jnp.zeros((2, 8, LANES), F32)
    for side, got in enumerate((mine, theirs)):
        column = pl.multiple_of(LANES * jnp.bitwise_xor(pos[0], side), LANES)
        for n, w in enumerate((0, 1, 4, 2, 3)):
            value = jnp.stack([got[:, 5 * t + n] for t in range(LINE // 2)], axis=1)
            stage[side, w] = value.astype(F32).reshape(FEATURES, LANES)
            copy = pltpu.make_async_copy(
                stage.at[side, w], weights[w].at[:, pl.ds(column, LANES)], sems.at[side, w]
            )
            copy.start()
            copies.append(copy)
        sums += jnp.sum(got[:, 20:].astype(F32), axis=0)
    head[...] = sums[1]
    pair_gain[...] = sums[0, 4:5]
    msa_gain[:, :LANES] = sums[0, 5:6]
    msa_gain[:, LANES:] = sums[0, 6:7]
    for copy in copies:
        copy.wait()


def on_device(msa, flags, pair, gain, pair_gain, wq, wk, wv, wg, wo, w_bias, grad):
    index = lax.axis_index("dap")
    pos = jnp.stack([index % CORES, index, index // CORES]).astype(jnp.int32)
    same_core = [[CORES * m + c for m in range(CHIPS)] for c in range(CORES)]
    along_z = [[g[LINE * q + z] for z in range(LINE)] for g in same_core for q in range(LINE)]
    across = [[g[LINE * q + z] for q in range(LINE)] for g in same_core for z in range(LINE)]
    partner = [(i, i ^ 1) for i in range(N)]

    def exchange(x, groups):
        return lax.all_to_all(
            x, "dap", split_axis=0, concat_axis=0, tiled=True, axis_index_groups=groups
        )

    w_bias = w_bias.T
    gain = jnp.broadcast_to(gain.reshape(1, FEATURES), (8, FEATURES))
    pair_gain = pair_gain.reshape(1, LANES)
    sent = call(
        entry_kernel,
        jax.ShapeDtypeStruct((CHIPS * IN_ROWS, LANES), BF16),
        [
            pltpu.VMEM((N, FEATURES), BF16),
            pltpu.VMEM((N, FEATURES), BF16),
            pltpu.VMEM((1, N), jnp.int32),
            pltpu.VMEM((1, N, LANES), BF16),
            pltpu.VMEM((1, LANES), F32),
            pltpu.VMEM((HEADS, LANES), BF16),
            pltpu.VMEM((CHIPS * IN_ROWS, LANES), F32),
            pltpu.VMEM((N, LANES), F32),
            pltpu.SemaphoreType.DMA((6,)),
        ],
        msa.reshape(N, FEATURES), grad.reshape(N, FEATURES), flags.reshape(1, N),
        pair, pair_gain, w_bias,
        first=HBM, rest=HBM, mib=60,
    )
    near = exchange(sent.reshape(CHIPS, IN_ROWS // 2, 2, LANES), same_core)
    near = near.reshape(CHIPS * IN_ROWS, LANES)
    far = lax.ppermute(near, "dap", partner)
    part = (TILES, PART_TILES, 8, LANES)
    own, other, d_gain = call(
        sequence_kernel,
        (
            jax.ShapeDtypeStruct(part, F32),
            jax.ShapeDtypeStruct(part, BF16),
            jax.ShapeDtypeStruct((1, FEATURES), F32),
        ),
        [
            pltpu.VMEM((CORES, CHIPS * IN_ROWS, LANES), F32),
            pltpu.VMEM((CHIPS * 8, LANES), F32),
            pltpu.VMEM((CHIPS * 8, LANES), F32),
            pltpu.VMEM((4 * N, FEATURES), F32),
            pltpu.VMEM((4 * N, FEATURES), F32),
            pltpu.VMEM((N, HEADS * LANES), BF16),
            pltpu.VMEM((N, HEADS * LANES), BF16),
        ],
        pos, near, far, gain, wq, wk, wv, wg, wo,
    )
    paired = (own + lax.ppermute(other, "dap", partner).astype(F32)).astype(BF16)
    got = exchange(paired.reshape(CHIPS, PART_TILES, 4, LANES), same_core)
    got = got.reshape(CHIPS * PART_ROWS, LANES)
    shard, d_bias = call(
        owner_kernel,
        (
            jax.ShapeDtypeStruct((LINE, SUM_ROWS, LANES), BF16),
            jax.ShapeDtypeStruct((HEADS, LANES), F32),
        ),
        [pltpu.VMEM((N, LANES), F32), pltpu.VMEM((2 * PART_ROWS, LANES), F32)],
        pos, got, pair, pair_gain, w_bias, d_gain,
    )
    line = call(
        line_kernel,
        jax.ShapeDtypeStruct((LINE, LINE_TILES, 8, LANES), BF16),
        [],
        pos, exchange(shard, along_z),
    )
    mine = exchange(line, across)
    row_shape = jax.ShapeDtypeStruct((N, FEATURES), BF16)
    update, adjoint, couple = call(
        unpack_kernel,
        (row_shape, row_shape, jax.ShapeDtypeStruct((1, N, LANES), BF16)),
        [pltpu.VMEM((CHIPS * PART_ROWS, LANES), F32), pltpu.VMEM((N, LANES), F32)],
        pos, got, d_bias, pair, pair_gain, w_bias,
    )
    theirs = lax.ppermute(mine, "dap", partner)
    *weights, head, msa_gain, pair_gain = call(
        final_kernel,
        (jax.ShapeDtypeStruct((FEATURES, FEATURES), F32),) * 5
        + (
            jax.ShapeDtypeStruct((HEADS, LANES), F32),
            jax.ShapeDtypeStruct((1, FEATURES), F32),
            jax.ShapeDtypeStruct((1, LANES), F32),
        ),
        [pltpu.VMEM((CORES, 5, FEATURES, LANES), F32), pltpu.SemaphoreType.DMA((CORES, 5))],
        pos, mine, theirs,
        far_out=5,
    )
    return (
        update.reshape(N, 1, FEATURES),
        adjoint.reshape(N, 1, FEATURES),
        couple,
        *weights,
        head.T,
        msa_gain.reshape(FEATURES),
        pair_gain.reshape(LANES),
    )


def solution(mesh):
    rows = P("dp", "dap", None)
    pair = P(("dp", "dap"), None, None)
    in_specs = (rows, P("dp", "dap"), pair) + (P(),) * 8 + (rows,)
    out_specs = (rows, rows, pair) + (P("dp", None),) * 6 + (P("dp"), P("dp"))
    return jax.shard_map(
        on_device, mesh=mesh, in_specs=in_specs, out_specs=out_specs, check_vma=False
    )
```

```python
import jax
import jax.numpy as jnp
from jax import lax
from jax.experimental import pallas as pl
from jax.experimental.pallas import tpu as pltpu
from jax.sharding import PartitionSpec as P

FEATURES = 256
HEADS = 8
HEAD_DIM = 32
LANES = 128
CORES = 2
CHIPS = 64
N = CORES * CHIPS
TILES = CHIPS // 2
SCALE = HEAD_DIM ** (-0.5)
EPS = 1e-05

F32 = jnp.float32
BF16 = jnp.bfloat16

IN_ROWS = 18
PART_ROWS = 36
PART_TILES = 9
SUM_ROWS = 32
LINE = 8
LINE_TILES = 22

VMEM = pl.BlockSpec(memory_space=pltpu.VMEM)
SMEM = pl.BlockSpec(memory_space=pltpu.SMEM)
HBM = pl.BlockSpec(memory_space=pltpu.HBM)


def dot(a, b):
    return jnp.dot(a, b, preferred_element_type=F32)


def dot_nt(a, b):
    return lax.dot_general(a, b, (((1,), (1,)), ((), ())), preferred_element_type=F32)


def dot_tn(a, b):
    return lax.dot_general(a, b, (((0,), (0,)), ((), ())), preferred_element_type=F32)


def layer_norm(value, gain):
    mean = jnp.mean(value, axis=-1, keepdims=True)
    centered = value - mean
    variance = jnp.mean(centered * centered, axis=-1, keepdims=True)
    inv = lax.rsqrt(variance + EPS)
    hat = centered * inv
    return hat, inv, hat * gain


def layer_norm_adjoint(upstream, hat, inv, gain):
    ug = upstream * gain
    return inv * (
        ug
        - jnp.mean(ug, axis=-1, keepdims=True)
        - hat * jnp.mean(ug * hat, axis=-1, keepdims=True)
    )


def split(x):
    high = x.astype(BF16)
    rest = x - high.astype(F32)
    mid = rest.astype(BF16)
    return high, mid, (rest - mid.astype(F32)).astype(BF16)


ORDER = [(c, p) for c in range(CORES) for p in range(2)]


def reordered(rows):
    return jnp.concatenate(
        [rows[pl.ds(2 * p + c, TILES, stride=4), :] for c, p in ORDER], axis=0
    )


def restore(rows, value):
    for n, (c, p) in enumerate(ORDER):
        rows[pl.ds(2 * p + c, TILES, stride=4), :] = value[n * TILES : (n + 1) * TILES]


def bias_row(h):
    return 4 + h if h < 5 else 8 + h


def call(kernel, out_shape, scratch, *operands, far_in=(), far_out=0):
    in_specs = [SMEM] + [VMEM] * (len(operands) - 1)
    operands = list(operands)
    for n in far_in:
        in_specs[n] = HBM
        operands[n] = pltpu.with_memory_space_constraint(operands[n], pltpu.HBM)
    out_specs = jax.tree.map(lambda _: VMEM, out_shape)
    if far_out:
        out_specs = (HBM,) * far_out + out_specs[far_out:]
    return pl.pallas_call(
        kernel,
        out_shape=out_shape,
        in_specs=in_specs,
        out_specs=out_specs,
        scratch_shapes=scratch,
        compiler_params=pltpu.CompilerParams(vmem_limit_bytes=12 * 1024 * 1024),
    )(*operands)


def entry_kernel(
    msa_hbm, grad_hbm, flags_hbm, pair_hbm, gain_hbm, w_hbm,
    out, msa, grad, flags, pair, gain, w_bias, stage, rows, sems
):
    refs = (
        (pair_hbm, pair), (gain_hbm, gain), (w_hbm, w_bias),
        (msa_hbm, msa), (grad_hbm, grad), (flags_hbm, flags),
    )
    copies = [pltpu.make_async_copy(a, b, sems.at[i]) for i, (a, b) in enumerate(refs)]
    for copy in copies:
        copy.start()
    for copy in copies[:3]:
        copy.wait()
    rows[...] = pair[0].astype(F32)
    _, _, scaled = layer_norm(reordered(rows), gain[...])
    bias = dot_nt(w_bias[...], scaled.astype(BF16))
    for copy in copies[3:]:
        copy.wait()
    for r, ref in enumerate((msa, grad)):
        value = ref[...].astype(F32)
        stage[pl.ds(2 * r, N, stride=9), :] = value[:, :LANES]
        stage[pl.ds(2 * r + 1, N, stride=9), :] = value[:, LANES:]
    lines = [(bias_row(h), bias[h : h + 1]) for h in range(HEADS)]
    lines += [(16, flags[...].astype(F32)), (17, jnp.zeros((1, LANES), F32))]
    for r, value in lines:
        stage[pl.ds(r, CHIPS, stride=IN_ROWS), :] = jnp.broadcast_to(value, (CHIPS, LANES))
    out[...] = stage[...].astype(BF16)


def sequence_kernel(
    pos, near, far, gain_hbm, wq_ref, wk_ref, wv_ref, wg_ref, wo_ref,
    own, other, gain_out, rows, mine, theirs, scores_ref, dp_ref, p_ref, ds_ref, gain_ref, sem
):
    gain_copy = pltpu.make_async_copy(gain_hbm, gain_ref, sem)
    gain_copy.start()
    core = pos[0]
    first = core == 0
    rows[core] = near[...].astype(F32)
    rows[1 - core] = far[...].astype(F32)

    def row(r):
        return jnp.concatenate(
            [
                rows.at[c][pl.ds(r + p * IN_ROWS, TILES, stride=2 * IN_ROWS), :]
                for c, p in ORDER
            ],
            axis=0,
        )

    def line(r):
        return jnp.where(first, row(r), row(9 + r))

    def halves(value):
        return (
            jnp.where(first, value[:CHIPS], value[CHIPS:]),
            jnp.where(first, value[CHIPS:], value[:CHIPS]),
        )

    gain_copy.wait()
    gain = gain_ref[...]
    msa = jnp.concatenate([line(0), line(1)], axis=1)
    grad = jnp.concatenate([line(2), line(3)], axis=1).astype(BF16)
    lane = lax.broadcasted_iota(jnp.int32, (8, LANES), 1)
    pick = jnp.where(lane == pos[1], 1.0, 0.0).astype(BF16)
    flags = dot_nt(pick, row(16).astype(BF16))[:1]
    masking = 1e9 * (flags - 1.0)
    hat, inv, scaled = layer_norm(msa, gain)
    x = scaled.astype(BF16)
    wo = wo_ref[...]
    q = (dot(x, wq_ref[...]) * SCALE).astype(BF16)
    k = dot(x, wk_ref[...]).astype(BF16)
    v = dot(x, wv_ref[...]).astype(BF16)
    gate = jax.nn.sigmoid(dot(x, wg_ref[...]))
    dw = dot_nt(grad, wo)
    d_attn = (dw * gate).astype(BF16)

    lane = lax.broadcasted_iota(jnp.int32, (1, FEATURES), 1)
    slot = (lane % LANES) // HEAD_DIM
    in_slot = [jnp.where(slot == s, 1.0, 0.0).astype(BF16) for s in range(4)]
    in_half = [jnp.where(lane // LANES == g, 1.0, 0.0).astype(BF16) for g in range(2)]

    def by_half(value):
        return jnp.concatenate([value * keep for keep in in_half], axis=0)

    def by_slot(value):
        return jnp.concatenate([value * keep for keep in in_slot], axis=0)

    def put(even, odd):
        for ref, rows8 in ((own, mine), (other, theirs)):
            value = rows8[...].astype(ref.dtype).reshape(2, TILES, 8, LANES)
            ref[:, even] = value[0]
            ref[:, odd] = value[1]

    k_halves, v_halves = by_half(k), by_half(v)
    scores_ref[...] = dot_nt(by_slot(q), k_halves)
    dp_ref[...] = dot_nt(by_slot(d_attn), v_halves)
    for s in range(4):
        for g in range(2):
            h = 4 * g + s
            span = (slice(s * N, (s + 1) * N), slice(g * LANES, (g + 1) * LANES))
            flat = slice((2 * s + g) * LANES, (2 * s + g + 1) * LANES)
            scores = scores_ref[span] + row(bias_row(h)) + masking
            e = jnp.exp(scores - jnp.max(scores, axis=-1, keepdims=True))
            p32 = e * (1.0 / jnp.sum(e, axis=-1, keepdims=True))
            p_ref[:, flat] = p32.astype(BF16)
            d_p = dp_ref[span]
            d_s = p32 * (d_p - jnp.sum(p32 * d_p, axis=-1, keepdims=True))
            a, b = halves(d_s)
            mine[pl.ds(h, CHIPS, stride=HEADS), :] = a
            theirs[pl.ds(h, CHIPS, stride=HEADS), :] = b
            ds_ref[:, flat] = d_s.astype(BF16)
    put(1, 6)
    attn = dot(p_ref[...], by_slot(v_halves))
    d_q = (dot(ds_ref[...], by_slot(k_halves)) * SCALE).astype(BF16)
    q_t = q.T
    da_t = d_attn.T
    dk_t = []
    dv_t = []
    for h in range(HEADS):
        g, s = divmod(h, 4)
        flat = slice((2 * s + g) * LANES, (2 * s + g + 1) * LANES)
        head = slice(h * HEAD_DIM, (h + 1) * HEAD_DIM)
        dk_t.append(dot(q_t[head], ds_ref[:, flat]))
        dv_t.append(dot(da_t[head], p_ref[:, flat]))
    d_k = jnp.concatenate(dk_t, axis=0).astype(BF16).T
    d_v = jnp.concatenate(dv_t, axis=0).astype(BF16).T
    weighted = (gate * attn).astype(BF16)
    update = dot(weighted, wo)
    d_g = (dw * attn * gate * (1.0 - gate)).astype(BF16)
    d_x = (
        dot_nt(d_q, wq_ref[...])
        + dot_nt(d_k, wk_ref[...])
        + dot_nt(d_v, wv_ref[...])
        + dot_nt(d_g, wg_ref[...])
    )
    adjoint = layer_norm_adjoint(d_x, hat, inv, gain)
    zeros = jnp.zeros((CHIPS, LANES), F32)
    for r, value in enumerate(
        (update[:, :LANES], update[:, LANES:], adjoint[:, :LANES], adjoint[:, LANES:])
    ):
        a, b = halves(value)
        mine[pl.ds(r, CHIPS, stride=8), :] = a
        mine[pl.ds(4 + r, CHIPS, stride=8), :] = zeros
        theirs[pl.ds(r, CHIPS, stride=8), :] = zeros
        theirs[pl.ds(4 + r, CHIPS, stride=8), :] = b
    put(0, 5)
    gain_out[...] = jnp.sum(d_x * hat, axis=0, keepdims=True)
    x_t = x.T
    w_t = weighted.T
    pairs = ((x_t, d_q), (x_t, d_k), (x_t, d_v), (x_t, d_g), (w_t, grad))
    mats = []
    for a, b in pairs:
        turned = jnp.concatenate([b[:, LANES:], b[:, :LANES]], axis=1)
        mats.append(dot(a, jnp.where(first, b, turned)))
    for ref, cols in ((own, slice(0, LANES)), (other, slice(LANES, FEATURES))):
        for tile, m in zip((2, 3, 7, 8, 4), mats):
            ref[:, tile] = m[:, cols].reshape(TILES, 8, LANES).astype(ref.dtype)


def pair_gradient(d_bias, pair, gain, w_bias, rows):
    rows[...] = pair[0].astype(F32)
    hat, inv, scaled = layer_norm(reordered(rows), gain)
    parts = split(d_bias)[::-1]
    d_pln = sum(dot_tn(part, w_bias) for part in parts)
    head = sum(dot(part, scaled.astype(BF16)) for part in parts)
    return hat, inv, d_pln, head


def owner_kernel(pos, got, pair, gain, w_bias, d_gain, out, d_bias_out, rows, sums):
    value = got[...].astype(F32).reshape(TILES, 2 * PART_ROWS, LANES)
    sums[...] = jnp.sum(value, axis=0)
    total = sums[0:PART_ROWS, :] + sums[PART_ROWS:, :]
    sums[0:PART_ROWS, :] = total
    even = pos[2] % 2 == 0
    d_bias = jnp.where(even, sums[8:16, :], sums[12:20, :])
    weights = jnp.where(even, sums[16:32, :], sums[20:36, :])
    fifth = jnp.where(even, sums[32:36, :], sums[0:4, :])
    d_bias_out[...] = d_bias
    hat, _, d_pln, head = pair_gradient(d_bias, pair, gain[...], w_bias[...], rows)
    shard = jnp.concatenate(
        [
            weights,
            fifth,
            jnp.sum(d_pln * hat, axis=0, keepdims=True),
            d_gain[:, :LANES],
            d_gain[:, LANES:],
            jnp.zeros((1, LANES), F32),
            head,
        ],
        axis=0,
    )
    out[...] = jnp.broadcast_to(shard.astype(BF16)[None], (LINE, SUM_ROWS, LANES))


def unpack_kernel(pos, got, d_bias, pair, gain_ref, w_bias, update, adjoint, couple, stage, rows):
    stage[...] = got[...].astype(F32)
    first = pos[0] == 0
    even = pos[2] % 2 == 0

    def line(r):
        a, b = (stage[pl.ds(k, CHIPS, stride=PART_ROWS), :] for k in (r, 4 + r))
        return jnp.where(even, a, b)

    for index, out in enumerate((update, adjoint)):
        for half in range(2):
            r = 2 * index + half
            same, cross = line(r), line(4 + r)
            rows[pl.ds(0, CHIPS, stride=CORES), :] = jnp.where(first, same, cross)
            rows[pl.ds(1, CHIPS, stride=CORES), :] = jnp.where(first, cross, same)
            out[:, half * LANES : (half + 1) * LANES] = rows[...].astype(BF16)
    gain = gain_ref[...]
    hat, inv, d_pln, _ = pair_gradient(d_bias[...], pair, gain, w_bias[...], rows)
    restore(rows, layer_norm_adjoint(d_pln, hat, inv, gain))
    couple[0] = rows[...].astype(BF16)


def line_kernel(pos, got, out):
    low = lax.broadcasted_iota(jnp.int32, (1, 8, 1), 1) < 4
    tiles = got[...].astype(F32).reshape(LINE // 2, 2, 4, 8, LANES)
    even, odd = tiles[:, 0], tiles[:, 1]
    fifth = jnp.where(low, even[:, 2], pltpu.roll(odd[:, 2], 4, 1))
    sums = jnp.sum(tiles[:, :, 2:], axis=(0, 1))
    weights = (even[:, 0], even[:, 1], fifth, odd[:, 0], odd[:, 1])
    for w, value in enumerate(weights):
        value = value.astype(BF16)
        for t in range(LINE // 2):
            out[:, 5 * t + w] = jnp.broadcast_to(value[t][None], (LINE, 8, LANES))
    for n in range(2):
        out[:, 20 + n] = jnp.broadcast_to(sums[n].astype(BF16)[None], (LINE, 8, LANES))


def final_kernel(pos, mine, theirs, *refs):
    weights, (head, msa_gain, pair_gain), (stage, sems) = refs[:5], refs[5:8], refs[8:]
    copies = []
    for n, w in enumerate((0, 1, 4, 2, 3)):
        for side, got in enumerate((mine, theirs)):
            column = pl.multiple_of(LANES * jnp.bitwise_xor(pos[0], side), LANES)
            value = jnp.stack([got[:, 5 * t + n] for t in range(LINE // 2)], axis=1)
            value = value.astype(F32).reshape(FEATURES, LANES)
            stage.at[w][:, pl.ds(column, LANES)] = value
        copy = pltpu.make_async_copy(stage.at[w], weights[w], sems.at[w])
        copy.start()
        copies.append(copy)
    sums = sum(jnp.sum(got[:, 20:].astype(F32), axis=0) for got in (mine, theirs))
    head[...] = sums[1]
    pair_gain[...] = sums[0, 4:5]
    msa_gain[:, :LANES] = sums[0, 5:6]
    msa_gain[:, LANES:] = sums[0, 6:7]
    for copy in copies:
        copy.wait()


def on_device(msa, flags, pair, gain, pair_gain, wq, wk, wv, wg, wo, w_bias, grad):
    index = lax.axis_index("dap")
    pos = jnp.stack([index % CORES, index, index // CORES]).astype(jnp.int32)
    same_core = [[CORES * m + c for m in range(CHIPS)] for c in range(CORES)]
    along_z = [[g[LINE * q + z] for z in range(LINE)] for g in same_core for q in range(LINE)]
    across = [[g[LINE * q + z] for q in range(LINE)] for g in same_core for z in range(LINE)]
    partner = [(i, i ^ 1) for i in range(N)]

    def exchange(x, groups):
        return lax.all_to_all(
            x, "dap", split_axis=0, concat_axis=0, tiled=True, axis_index_groups=groups
        )

    w_bias = w_bias.T
    gain = gain.reshape(1, FEATURES)
    pair_gain = pair_gain.reshape(1, LANES)
    sent = call(
        entry_kernel,
        jax.ShapeDtypeStruct((CHIPS * IN_ROWS, LANES), BF16),
        [
            pltpu.VMEM((N, FEATURES), BF16),
            pltpu.VMEM((N, FEATURES), BF16),
            pltpu.VMEM((1, N), jnp.int32),
            pltpu.VMEM((1, N, LANES), BF16),
            pltpu.VMEM((1, LANES), F32),
            pltpu.VMEM((HEADS, LANES), BF16),
            pltpu.VMEM((CHIPS * IN_ROWS, LANES), F32),
            pltpu.VMEM((N, LANES), F32),
            pltpu.SemaphoreType.DMA((6,)),
        ],
        msa.reshape(N, FEATURES), grad.reshape(N, FEATURES), flags.reshape(1, N),
        pair, pair_gain, w_bias,
        far_in=(0, 1, 2, 3, 4, 5),
    )
    near = exchange(sent.reshape(CHIPS, IN_ROWS // 2, 2, LANES), same_core)
    near = near.reshape(CHIPS * IN_ROWS, LANES)
    far = lax.ppermute(near, "dap", partner)
    part = (TILES, PART_TILES, 8, LANES)
    own, other, d_gain = call(
        sequence_kernel,
        (
            jax.ShapeDtypeStruct(part, F32),
            jax.ShapeDtypeStruct(part, BF16),
            jax.ShapeDtypeStruct((1, FEATURES), F32),
        ),
        [
            pltpu.VMEM((CORES, CHIPS * IN_ROWS, LANES), F32),
            pltpu.VMEM((CHIPS * 8, LANES), F32),
            pltpu.VMEM((CHIPS * 8, LANES), F32),
            pltpu.VMEM((4 * N, FEATURES), F32),
            pltpu.VMEM((4 * N, FEATURES), F32),
            pltpu.VMEM((N, HEADS * LANES), BF16),
            pltpu.VMEM((N, HEADS * LANES), BF16),
            pltpu.VMEM((1, FEATURES), F32),
            pltpu.SemaphoreType.DMA,
        ],
        pos, near, far, gain, wq, wk, wv, wg, wo,
        far_in=(3,),
    )
    paired = (own + lax.ppermute(other, "dap", partner).astype(F32)).astype(BF16)
    got = exchange(paired.reshape(CHIPS, PART_TILES, 4, LANES), same_core)
    got = got.reshape(CHIPS * PART_ROWS, LANES)
    shard, d_bias = call(
        owner_kernel,
        (
            jax.ShapeDtypeStruct((LINE, SUM_ROWS, LANES), BF16),
            jax.ShapeDtypeStruct((HEADS, LANES), F32),
        ),
        [pltpu.VMEM((N, LANES), F32), pltpu.VMEM((2 * PART_ROWS, LANES), F32)],
        pos, got, pair, pair_gain, w_bias, d_gain,
    )
    line = call(
        line_kernel,
        jax.ShapeDtypeStruct((LINE, LINE_TILES, 8, LANES), BF16),
        [],
        pos, exchange(shard, along_z),
    )
    mine = exchange(line, across)
    row_shape = jax.ShapeDtypeStruct((N, FEATURES), BF16)
    update, adjoint, couple = call(
        unpack_kernel,
        (row_shape, row_shape, jax.ShapeDtypeStruct((1, N, LANES), BF16)),
        [pltpu.VMEM((CHIPS * PART_ROWS, LANES), F32), pltpu.VMEM((N, LANES), F32)],
        pos, got, d_bias, pair, pair_gain, w_bias,
    )
    theirs = lax.ppermute(mine, "dap", partner)
    *weights, head, msa_gain, pair_gain = call(
        final_kernel,
        (jax.ShapeDtypeStruct((FEATURES, FEATURES), F32),) * 5
        + (
            jax.ShapeDtypeStruct((HEADS, LANES), F32),
            jax.ShapeDtypeStruct((1, FEATURES), F32),
            jax.ShapeDtypeStruct((1, LANES), F32),
        ),
        [pltpu.VMEM((5, FEATURES, FEATURES), F32), pltpu.SemaphoreType.DMA((5,))],
        pos, mine, theirs,
        far_out=5,
    )
    return (
        update.reshape(N, 1, FEATURES),
        adjoint.reshape(N, 1, FEATURES),
        couple,
        *weights,
        head.T,
        msa_gain.reshape(FEATURES),
        pair_gain.reshape(LANES),
    )


def solution(mesh):
    rows = P("dp", "dap", None)
    pair = P(("dp", "dap"), None, None)
    in_specs = (rows, P("dp", "dap"), pair) + (P(),) * 8 + (rows,)
    out_specs = (rows, rows, pair) + (P("dp", None),) * 6 + (P("dp"), P("dp"))
    return jax.shard_map(
        on_device, mesh=mesh, in_specs=in_specs, out_specs=out_specs, check_vma=False
    )
```

```python
import jax
import jax.numpy as jnp
from jax import lax
from jax.experimental import pallas as pl
from jax.experimental.pallas import tpu as pltpu
from jax.sharding import PartitionSpec as P

FEATURES = 256
HEADS = 8
HEAD_DIM = 32
LANES = 128
CORES = 2
CHIPS = 64
N = CORES * CHIPS
TILES = CHIPS // 2
SCALE = HEAD_DIM ** (-0.5)
EPS = 1e-05

F32 = jnp.float32
BF16 = jnp.bfloat16

IN_ROWS = 18
PART_ROWS = 36
PART_TILES = 9
SUM_ROWS = 32
LINE = 8
LINE_TILES = 22

VMEM = pl.BlockSpec(memory_space=pltpu.VMEM)
SMEM = pl.BlockSpec(memory_space=pltpu.SMEM)
HBM = pl.BlockSpec(memory_space=pltpu.HBM)


def dot(a, b):
    return jnp.dot(a, b, preferred_element_type=F32)


def dot_nt(a, b):
    return lax.dot_general(a, b, (((1,), (1,)), ((), ())), preferred_element_type=F32)


def dot_tn(a, b):
    return lax.dot_general(a, b, (((0,), (0,)), ((), ())), preferred_element_type=F32)


def layer_norm(value, gain):
    mean = jnp.mean(value, axis=-1, keepdims=True)
    centered = value - mean
    variance = jnp.mean(centered * centered, axis=-1, keepdims=True)
    inv = lax.rsqrt(variance + EPS)
    hat = centered * inv
    return hat, inv, hat * gain


def layer_norm_adjoint(upstream, hat, inv, gain):
    ug = upstream * gain
    return inv * (
        ug
        - jnp.mean(ug, axis=-1, keepdims=True)
        - hat * jnp.mean(ug * hat, axis=-1, keepdims=True)
    )


def split(x):
    high = x.astype(BF16)
    rest = x - high.astype(F32)
    mid = rest.astype(BF16)
    return high, mid, (rest - mid.astype(F32)).astype(BF16)


ORDER = [(c, p) for c in range(CORES) for p in range(2)]


def reordered(rows):
    return jnp.concatenate(
        [rows[pl.ds(2 * p + c, TILES, stride=4), :] for c, p in ORDER], axis=0
    )


def restore(rows, value):
    for n, (c, p) in enumerate(ORDER):
        rows[pl.ds(2 * p + c, TILES, stride=4), :] = value[n * TILES : (n + 1) * TILES]


def bias_row(h):
    return 4 + h if h < 5 else 8 + h


def call(kernel, out_shape, scratch, *operands, far_in=()):
    in_specs = [SMEM] + [VMEM] * (len(operands) - 1)
    operands = list(operands)
    for n in far_in:
        in_specs[n] = HBM
        operands[n] = pltpu.with_memory_space_constraint(operands[n], pltpu.HBM)
    return pl.pallas_call(
        kernel,
        out_shape=out_shape,
        in_specs=in_specs,
        out_specs=jax.tree.map(lambda _: VMEM, out_shape),
        scratch_shapes=scratch,
        compiler_params=pltpu.CompilerParams(vmem_limit_bytes=12 * 1024 * 1024),
    )(*operands)


def entry_kernel(*refs):
    sources, out, kept, (msa, grad, flags, stage, rows, sems) = (
        refs[:12], refs[12], refs[13:22], refs[22:]
    )
    targets = kept + (msa, grad, flags)
    copies = [
        pltpu.make_async_copy(a, b, sems.at[i]) for i, (a, b) in enumerate(zip(sources, targets))
    ]
    for n in (0, 1, 2, 9, 10, 11, 3, 4, 5, 6, 7, 8):
        copies[n].start()
    pair, gain, w_bias = kept[:3]
    for copy in copies[:3]:
        copy.wait()
    rows[...] = pair[0].astype(F32)
    _, _, scaled = layer_norm(reordered(rows), gain[...])
    bias = dot_nt(w_bias[...], scaled.astype(BF16))
    for copy in copies[9:]:
        copy.wait()
    for r, ref in enumerate((msa, grad)):
        value = ref[...].astype(F32)
        stage[pl.ds(2 * r, N, stride=9), :] = value[:, :LANES]
        stage[pl.ds(2 * r + 1, N, stride=9), :] = value[:, LANES:]
    lines = [(bias_row(h), bias[h : h + 1]) for h in range(HEADS)]
    lines += [(16, flags[...].astype(F32)), (17, jnp.zeros((1, LANES), F32))]
    for r, value in lines:
        stage[pl.ds(r, CHIPS, stride=IN_ROWS), :] = jnp.broadcast_to(value, (CHIPS, LANES))
    out[...] = stage[...].astype(BF16)
    for copy in copies[3:9]:
        copy.wait()


def sequence_kernel(
    pos, near, far, gain_ref, wq_ref, wk_ref, wv_ref, wg_ref, wo_ref,
    own, other, gain_out, rows, mine, theirs, scores_ref, dp_ref, p_ref, ds_ref
):
    core = pos[0]
    first = core == 0
    rows[core] = near[...].astype(F32)
    rows[1 - core] = far[...].astype(F32)

    def row(r):
        return jnp.concatenate(
            [
                rows.at[c][pl.ds(r + p * IN_ROWS, TILES, stride=2 * IN_ROWS), :]
                for c, p in ORDER
            ],
            axis=0,
        )

    def line(r):
        return jnp.where(first, row(r), row(9 + r))

    def halves(value):
        return (
            jnp.where(first, value[:CHIPS], value[CHIPS:]),
            jnp.where(first, value[CHIPS:], value[:CHIPS]),
        )

    gain = gain_ref[...]
    msa = jnp.concatenate([line(0), line(1)], axis=1)
    grad = jnp.concatenate([line(2), line(3)], axis=1).astype(BF16)
    lane = lax.broadcasted_iota(jnp.int32, (8, LANES), 1)
    pick = jnp.where(lane == pos[1], 1.0, 0.0).astype(BF16)
    flags = dot_nt(pick, row(16).astype(BF16))[:1]
    masking = 1e9 * (flags - 1.0)
    hat, inv, scaled = layer_norm(msa, gain)
    x = scaled.astype(BF16)
    wo = wo_ref[...]
    q = (dot(x, wq_ref[...]) * SCALE).astype(BF16)
    k = dot(x, wk_ref[...]).astype(BF16)
    v = dot(x, wv_ref[...]).astype(BF16)
    gate = jax.nn.sigmoid(dot(x, wg_ref[...]))
    dw = dot_nt(grad, wo)
    d_attn = (dw * gate).astype(BF16)

    lane = lax.broadcasted_iota(jnp.int32, (1, FEATURES), 1)
    slot = (lane % LANES) // HEAD_DIM
    in_slot = [jnp.where(slot == s, 1.0, 0.0).astype(BF16) for s in range(4)]
    in_half = [jnp.where(lane // LANES == g, 1.0, 0.0).astype(BF16) for g in range(2)]

    def by_half(value):
        return jnp.concatenate([value * keep for keep in in_half], axis=0)

    def by_slot(value):
        return jnp.concatenate([value * keep for keep in in_slot], axis=0)

    def put(even, odd):
        for ref, rows8 in ((own, mine), (other, theirs)):
            value = rows8[...].astype(ref.dtype).reshape(2, TILES, 8, LANES)
            ref[:, even] = value[0]
            ref[:, odd] = value[1]

    k_halves, v_halves = by_half(k), by_half(v)
    scores_ref[...] = dot_nt(by_slot(q), k_halves)
    dp_ref[...] = dot_nt(by_slot(d_attn), v_halves)
    for s in range(4):
        for g in range(2):
            h = 4 * g + s
            span = (slice(s * N, (s + 1) * N), slice(g * LANES, (g + 1) * LANES))
            flat = slice((2 * s + g) * LANES, (2 * s + g + 1) * LANES)
            scores = scores_ref[span] + row(bias_row(h)) + masking
            e = jnp.exp(scores - jnp.max(scores, axis=-1, keepdims=True))
            p32 = e * (1.0 / jnp.sum(e, axis=-1, keepdims=True))
            p_ref[:, flat] = p32.astype(BF16)
            d_p = dp_ref[span]
            d_s = p32 * (d_p - jnp.sum(p32 * d_p, axis=-1, keepdims=True))
            a, b = halves(d_s)
            mine[pl.ds(h, CHIPS, stride=HEADS), :] = a
            theirs[pl.ds(h, CHIPS, stride=HEADS), :] = b
            ds_ref[:, flat] = d_s.astype(BF16)
    put(1, 6)
    attn = dot(p_ref[...], by_slot(v_halves))
    d_q = (dot(ds_ref[...], by_slot(k_halves)) * SCALE).astype(BF16)
    q_t = q.T
    da_t = d_attn.T
    dk_t = []
    dv_t = []
    for h in range(HEADS):
        g, s = divmod(h, 4)
        flat = slice((2 * s + g) * LANES, (2 * s + g + 1) * LANES)
        head = slice(h * HEAD_DIM, (h + 1) * HEAD_DIM)
        dk_t.append(dot(q_t[head], ds_ref[:, flat]))
        dv_t.append(dot(da_t[head], p_ref[:, flat]))
    d_k = jnp.concatenate(dk_t, axis=0).astype(BF16).T
    d_v = jnp.concatenate(dv_t, axis=0).astype(BF16).T
    weighted = (gate * attn).astype(BF16)
    update = dot(weighted, wo)
    d_g = (dw * attn * gate * (1.0 - gate)).astype(BF16)
    d_x = (
        dot_nt(d_q, wq_ref[...])
        + dot_nt(d_k, wk_ref[...])
        + dot_nt(d_v, wv_ref[...])
        + dot_nt(d_g, wg_ref[...])
    )
    adjoint = layer_norm_adjoint(d_x, hat, inv, gain)
    zeros = jnp.zeros((CHIPS, LANES), F32)
    for r, value in enumerate(
        (update[:, :LANES], update[:, LANES:], adjoint[:, :LANES], adjoint[:, LANES:])
    ):
        a, b = halves(value)
        mine[pl.ds(r, CHIPS, stride=8), :] = a
        mine[pl.ds(4 + r, CHIPS, stride=8), :] = zeros
        theirs[pl.ds(r, CHIPS, stride=8), :] = zeros
        theirs[pl.ds(4 + r, CHIPS, stride=8), :] = b
    put(0, 5)
    gain_out[...] = jnp.sum(d_x * hat, axis=0, keepdims=True)
    x_t = x.T
    w_t = weighted.T
    pairs = ((x_t, d_q), (x_t, d_k), (x_t, d_v), (x_t, d_g), (w_t, grad))
    mats = []
    for a, b in pairs:
        turned = jnp.concatenate([b[:, LANES:], b[:, :LANES]], axis=1)
        mats.append(dot(a, jnp.where(first, b, turned)))
    for ref, cols in ((own, slice(0, LANES)), (other, slice(LANES, FEATURES))):
        for tile, m in zip((2, 3, 7, 8, 4), mats):
            ref[:, tile] = m[:, cols].reshape(TILES, 8, LANES).astype(ref.dtype)


def pair_gradient(d_bias, pair, gain, w_bias, rows):
    rows[...] = pair[0].astype(F32)
    hat, inv, scaled = layer_norm(reordered(rows), gain)
    parts = split(d_bias)[::-1]
    d_pln = sum(dot_tn(part, w_bias) for part in parts)
    head = sum(dot(part, scaled.astype(BF16)) for part in parts)
    return hat, inv, d_pln, head


def owner_kernel(pos, got, pair, gain, w_bias, d_gain, out, d_bias_out, rows, sums):
    value = got[...].astype(F32).reshape(TILES, 2 * PART_ROWS, LANES)
    sums[...] = jnp.sum(value, axis=0)
    total = sums[0:PART_ROWS, :] + sums[PART_ROWS:, :]
    sums[0:PART_ROWS, :] = total
    even = pos[2] % 2 == 0
    d_bias = jnp.where(even, sums[8:16, :], sums[12:20, :])
    weights = jnp.where(even, sums[16:32, :], sums[20:36, :])
    fifth = jnp.where(even, sums[32:36, :], sums[0:4, :])
    d_bias_out[...] = d_bias
    hat, _, d_pln, head = pair_gradient(d_bias, pair, gain[...], w_bias[...], rows)
    shard = jnp.concatenate(
        [
            weights,
            fifth,
            jnp.sum(d_pln * hat, axis=0, keepdims=True),
            d_gain[:, :LANES],
            d_gain[:, LANES:],
            jnp.zeros((1, LANES), F32),
            head,
        ],
        axis=0,
    )
    out[...] = jnp.broadcast_to(shard.astype(BF16)[None], (LINE, SUM_ROWS, LANES))


def unpack_kernel(pos, got, d_bias, pair, gain_ref, w_bias, update, adjoint, couple, stage, rows):
    stage[...] = got[...].astype(F32)
    first = pos[0] == 0
    even = pos[2] % 2 == 0

    def line(r):
        a, b = (stage[pl.ds(k, CHIPS, stride=PART_ROWS), :] for k in (r, 4 + r))
        return jnp.where(even, a, b)

    for index, out in enumerate((update, adjoint)):
        for half in range(2):
            r = 2 * index + half
            same, cross = line(r), line(4 + r)
            rows[pl.ds(0, CHIPS, stride=CORES), :] = jnp.where(first, same, cross)
            rows[pl.ds(1, CHIPS, stride=CORES), :] = jnp.where(first, cross, same)
            out[:, half * LANES : (half + 1) * LANES] = rows[...].astype(BF16)
    gain = gain_ref[...]
    hat, inv, d_pln, _ = pair_gradient(d_bias[...], pair, gain, w_bias[...], rows)
    restore(rows, layer_norm_adjoint(d_pln, hat, inv, gain))
    couple[0] = rows[...].astype(BF16)


def line_kernel(pos, got, out):
    low = lax.broadcasted_iota(jnp.int32, (1, 8, 1), 1) < 4
    tiles = got[...].astype(F32).reshape(LINE // 2, 2, 4, 8, LANES)
    even, odd = tiles[:, 0], tiles[:, 1]
    fifth = jnp.where(low, even[:, 2], pltpu.roll(odd[:, 2], 4, 1))
    sums = jnp.sum(tiles[:, :, 2:], axis=(0, 1))
    weights = (even[:, 0], even[:, 1], fifth, odd[:, 0], odd[:, 1])
    for w, value in enumerate(weights):
        value = value.astype(BF16)
        for t in range(LINE // 2):
            out[:, 5 * t + w] = jnp.broadcast_to(value[t][None], (LINE, 8, LANES))
    for n in range(2):
        out[:, 20 + n] = jnp.broadcast_to(sums[n].astype(BF16)[None], (LINE, 8, LANES))


def final_kernel(pos, mine, theirs, *refs):
    weights, (head, msa_gain, pair_gain) = refs[:5], refs[5:]
    for n, w in enumerate((0, 1, 4, 2, 3)):
        for side, got in enumerate((mine, theirs)):
            column = pl.multiple_of(LANES * jnp.bitwise_xor(pos[0], side), LANES)
            value = jnp.stack([got[:, 5 * t + n] for t in range(LINE // 2)], axis=1)
            value = value.astype(F32).reshape(FEATURES, LANES)
            weights[w][:, pl.ds(column, LANES)] = value
    sums = sum(jnp.sum(got[:, 20:].astype(F32), axis=0) for got in (mine, theirs))
    head[...] = sums[1]
    pair_gain[...] = sums[0, 4:5]
    msa_gain[:, :LANES] = sums[0, 5:6]
    msa_gain[:, LANES:] = sums[0, 6:7]


def on_device(msa, flags, pair, gain, pair_gain, wq, wk, wv, wg, wo, w_bias, grad):
    index = lax.axis_index("dap")
    pos = jnp.stack([index % CORES, index, index // CORES]).astype(jnp.int32)
    same_core = [[CORES * m + c for m in range(CHIPS)] for c in range(CORES)]
    along_z = [[g[LINE * q + z] for z in range(LINE)] for g in same_core for q in range(LINE)]
    across = [[g[LINE * q + z] for q in range(LINE)] for g in same_core for z in range(LINE)]
    partner = [(i, i ^ 1) for i in range(N)]

    def exchange(x, groups):
        return lax.all_to_all(
            x, "dap", split_axis=0, concat_axis=0, tiled=True, axis_index_groups=groups
        )

    w_bias = w_bias.T
    gain = gain.reshape(1, FEATURES)
    pair_gain = pair_gain.reshape(1, LANES)
    kept = (pair, pair_gain, w_bias, wq, wk, wv, wg, wo, gain)
    sent, *kept = call(
        entry_kernel,
        (jax.ShapeDtypeStruct((CHIPS * IN_ROWS, LANES), BF16),)
        + tuple(jax.ShapeDtypeStruct(v.shape, v.dtype) for v in kept),
        [
            pltpu.VMEM((N, FEATURES), BF16),
            pltpu.VMEM((N, FEATURES), BF16),
            pltpu.VMEM((1, N), jnp.int32),
            pltpu.VMEM((CHIPS * IN_ROWS, LANES), F32),
            pltpu.VMEM((N, LANES), F32),
            pltpu.SemaphoreType.DMA((12,)),
        ],
        *kept, msa.reshape(N, FEATURES), grad.reshape(N, FEATURES), flags.reshape(1, N),
        far_in=range(12),
    )
    pair, pair_gain, w_bias, wq, wk, wv, wg, wo, gain = kept
    near = exchange(sent.reshape(CHIPS, IN_ROWS // 2, 2, LANES), same_core)
    near = near.reshape(CHIPS * IN_ROWS, LANES)
    far = lax.ppermute(near, "dap", partner)
    part = (TILES, PART_TILES, 8, LANES)
    own, other, d_gain = call(
        sequence_kernel,
        (
            jax.ShapeDtypeStruct(part, F32),
            jax.ShapeDtypeStruct(part, BF16),
            jax.ShapeDtypeStruct((1, FEATURES), F32),
        ),
        [
            pltpu.VMEM((CORES, CHIPS * IN_ROWS, LANES), F32),
            pltpu.VMEM((CHIPS * 8, LANES), F32),
            pltpu.VMEM((CHIPS * 8, LANES), F32),
            pltpu.VMEM((4 * N, FEATURES), F32),
            pltpu.VMEM((4 * N, FEATURES), F32),
            pltpu.VMEM((N, HEADS * LANES), BF16),
            pltpu.VMEM((N, HEADS * LANES), BF16),
        ],
        pos, near, far, gain, wq, wk, wv, wg, wo,
    )
    paired = (own + lax.ppermute(other, "dap", partner).astype(F32)).astype(BF16)
    got = exchange(paired.reshape(CHIPS, PART_TILES, 4, LANES), same_core)
    got = got.reshape(CHIPS * PART_ROWS, LANES)
    shard, d_bias = call(
        owner_kernel,
        (
            jax.ShapeDtypeStruct((LINE, SUM_ROWS, LANES), BF16),
            jax.ShapeDtypeStruct((HEADS, LANES), F32),
        ),
        [pltpu.VMEM((N, LANES), F32), pltpu.VMEM((2 * PART_ROWS, LANES), F32)],
        pos, got, pair, pair_gain, w_bias, d_gain,
    )
    line = call(
        line_kernel,
        jax.ShapeDtypeStruct((LINE, LINE_TILES, 8, LANES), BF16),
        [],
        pos, exchange(shard, along_z),
    )
    mine = exchange(line, across)
    row_shape = jax.ShapeDtypeStruct((N, FEATURES), BF16)
    update, adjoint, couple = call(
        unpack_kernel,
        (row_shape, row_shape, jax.ShapeDtypeStruct((1, N, LANES), BF16)),
        [pltpu.VMEM((CHIPS * PART_ROWS, LANES), F32), pltpu.VMEM((N, LANES), F32)],
        pos, got, d_bias, pair, pair_gain, w_bias,
    )
    theirs = lax.ppermute(mine, "dap", partner)
    *weights, head, msa_gain, pair_gain = call(
        final_kernel,
        (jax.ShapeDtypeStruct((FEATURES, FEATURES), F32),) * 5
        + (
            jax.ShapeDtypeStruct((HEADS, LANES), F32),
            jax.ShapeDtypeStruct((1, FEATURES), F32),
            jax.ShapeDtypeStruct((1, LANES), F32),
        ),
        [],
        pos, mine, theirs,
    )
    return (
        update.reshape(N, 1, FEATURES),
        adjoint.reshape(N, 1, FEATURES),
        couple,
        *weights,
        head.T,
        msa_gain.reshape(FEATURES),
        pair_gain.reshape(LANES),
    )


def solution(mesh):
    rows = P("dp", "dap", None)
    pair = P(("dp", "dap"), None, None)
    in_specs = (rows, P("dp", "dap"), pair) + (P(),) * 8 + (rows,)
    out_specs = (rows, rows, pair) + (P("dp", None),) * 6 + (P("dp"), P("dp"))
    return jax.shard_map(
        on_device, mesh=mesh, in_specs=in_specs, out_specs=out_specs, check_vma=False
    )
```

```python
import jax
import jax.numpy as jnp
from jax import lax
from jax.experimental import pallas as pl
from jax.experimental.pallas import tpu as pltpu
from jax.sharding import PartitionSpec as P

FEATURES = 256
HEADS = 8
HEAD_DIM = 32
LANES = 128
CORES = 2
CHIPS = 64
N = CORES * CHIPS
TILES = CHIPS // 2
SCALE = HEAD_DIM ** (-0.5)
EPS = 1e-05

F32 = jnp.float32
BF16 = jnp.bfloat16

IN_ROWS = 18
PART_ROWS = 36
PART_TILES = 9
SUM_ROWS = 32
LINE = 8
LINE_TILES = 22

VMEM = pl.BlockSpec(memory_space=pltpu.VMEM)
SMEM = pl.BlockSpec(memory_space=pltpu.SMEM)
HBM = pl.BlockSpec(memory_space=pltpu.HBM)


def dot(a, b):
    return jnp.dot(a, b, preferred_element_type=F32)


def dot_nt(a, b):
    return lax.dot_general(a, b, (((1,), (1,)), ((), ())), preferred_element_type=F32)


def dot_tn(a, b):
    return lax.dot_general(a, b, (((0,), (0,)), ((), ())), preferred_element_type=F32)


def layer_norm(value, gain):
    mean = jnp.mean(value, axis=-1, keepdims=True)
    centered = value - mean
    variance = jnp.mean(centered * centered, axis=-1, keepdims=True)
    inv = lax.rsqrt(variance + EPS)
    hat = centered * inv
    return hat, inv, hat * gain


def layer_norm_adjoint(upstream, hat, inv, gain):
    ug = upstream * gain
    return inv * (
        ug
        - jnp.mean(ug, axis=-1, keepdims=True)
        - hat * jnp.mean(ug * hat, axis=-1, keepdims=True)
    )


def split(x):
    high = x.astype(BF16)
    rest = x - high.astype(F32)
    mid = rest.astype(BF16)
    return high, mid, (rest - mid.astype(F32)).astype(BF16)


ORDER = [(c, p) for c in range(CORES) for p in range(2)]


LINES = (7, 4, 5, 6, 3, 0, 1, 2)
LINE_ROWS = 2 * 8


def listed(value):
    return jnp.concatenate(
        [value[q * LINE_ROWS : (q + 1) * LINE_ROWS] for q in LINES], axis=0
    )


def natural(value):
    at = [LINES.index(q) * LINE_ROWS for q in range(8)]
    return jnp.concatenate([value[a : a + LINE_ROWS] for a in at], axis=0)


def reordered(rows):
    return jnp.concatenate(
        [rows[pl.ds(2 * p + c, TILES, stride=4), :] for c, p in ORDER], axis=0
    )


def restore(rows, value):
    for n, (c, p) in enumerate(ORDER):
        rows[pl.ds(2 * p + c, TILES, stride=4), :] = value[n * TILES : (n + 1) * TILES]


def bias_row(h):
    return 4 + h if h < 5 else 8 + h


def call(kernel, out_shape, scratch, *operands, far_in=()):
    in_specs = [SMEM] + [VMEM] * (len(operands) - 1)
    operands = list(operands)
    for n in far_in:
        in_specs[n] = HBM
        operands[n] = pltpu.with_memory_space_constraint(operands[n], pltpu.HBM)
    return pl.pallas_call(
        kernel,
        out_shape=out_shape,
        in_specs=in_specs,
        out_specs=jax.tree.map(lambda _: VMEM, out_shape),
        scratch_shapes=scratch,
        compiler_params=pltpu.CompilerParams(vmem_limit_bytes=12 * 1024 * 1024),
    )(*operands)


def entry_kernel(*refs):
    sources, out, kept, (msa, grad, flags, stage, rows, sems) = (
        refs[:12], refs[12], refs[13:22], refs[22:]
    )
    targets = kept + (msa, grad, flags)
    copies = [
        pltpu.make_async_copy(a, b, sems.at[i]) for i, (a, b) in enumerate(zip(sources, targets))
    ]
    for n in (0, 1, 2, 9, 10, 11, 3, 4, 5, 6, 7, 8):
        copies[n].start()
    pair, gain, w_bias = kept[:3]
    for copy in copies[:3]:
        copy.wait()
    rows[...] = listed(pair[0].astype(F32))
    _, _, scaled = layer_norm(reordered(rows), gain[...])
    bias = dot_nt(w_bias[...], scaled.astype(BF16))
    for copy in copies[9:]:
        copy.wait()
    for r, ref in enumerate((msa, grad)):
        value = listed(ref[...].astype(F32))
        stage[pl.ds(2 * r, N, stride=9), :] = value[:, :LANES]
        stage[pl.ds(2 * r + 1, N, stride=9), :] = value[:, LANES:]
    lines = [(bias_row(h), bias[h : h + 1]) for h in range(HEADS)]
    lines += [(16, flags[...].astype(F32)), (17, jnp.zeros((1, LANES), F32))]
    for r, value in lines:
        stage[pl.ds(r, CHIPS, stride=IN_ROWS), :] = jnp.broadcast_to(value, (CHIPS, LANES))
    out[...] = stage[...].astype(BF16)
    for copy in copies[3:9]:
        copy.wait()


def sequence_kernel(
    pos, near, far, gain_ref, wq_ref, wk_ref, wv_ref, wg_ref, wo_ref,
    own, other, gain_out, rows, mine, theirs, scores_ref, dp_ref, p_ref, ds_ref
):
    core = pos[0]
    first = core == 0
    rows[core] = near[...].astype(F32)
    rows[1 - core] = far[...].astype(F32)

    def row(r):
        return jnp.concatenate(
            [
                rows.at[c][pl.ds(r + p * IN_ROWS, TILES, stride=2 * IN_ROWS), :]
                for c, p in ORDER
            ],
            axis=0,
        )

    def line(r):
        return jnp.where(first, row(r), row(9 + r))

    def halves(value):
        return (
            jnp.where(first, value[:CHIPS], value[CHIPS:]),
            jnp.where(first, value[CHIPS:], value[:CHIPS]),
        )

    gain = gain_ref[...]
    msa = jnp.concatenate([line(0), line(1)], axis=1)
    grad = jnp.concatenate([line(2), line(3)], axis=1).astype(BF16)
    lane = lax.broadcasted_iota(jnp.int32, (8, LANES), 1)
    pick = jnp.where(lane == pos[1], 1.0, 0.0).astype(BF16)
    flags = dot_nt(pick, row(16).astype(BF16))[:1]
    masking = 1e9 * (flags - 1.0)
    hat, inv, scaled = layer_norm(msa, gain)
    x = scaled.astype(BF16)
    wo = wo_ref[...]
    q = (dot(x, wq_ref[...]) * SCALE).astype(BF16)
    k = dot(x, wk_ref[...]).astype(BF16)
    v = dot(x, wv_ref[...]).astype(BF16)
    gate = jax.nn.sigmoid(dot(x, wg_ref[...]))
    dw = dot_nt(grad, wo)
    d_attn = (dw * gate).astype(BF16)

    lane = lax.broadcasted_iota(jnp.int32, (1, FEATURES), 1)
    slot = (lane % LANES) // HEAD_DIM
    in_slot = [jnp.where(slot == s, 1.0, 0.0).astype(BF16) for s in range(4)]
    in_half = [jnp.where(lane // LANES == g, 1.0, 0.0).astype(BF16) for g in range(2)]

    def by_half(value):
        return jnp.concatenate([value * keep for keep in in_half], axis=0)

    def by_slot(value):
        return jnp.concatenate([value * keep for keep in in_slot], axis=0)

    def put(even, odd):
        for ref, rows8 in ((own, mine), (other, theirs)):
            value = rows8[...].astype(ref.dtype).reshape(2, TILES, 8, LANES)
            ref[:, even] = value[0]
            ref[:, odd] = value[1]

    k_halves, v_halves = by_half(k), by_half(v)
    scores_ref[...] = dot_nt(by_slot(q), k_halves)
    dp_ref[...] = dot_nt(by_slot(d_attn), v_halves)
    for s in range(4):
        for g in range(2):
            h = 4 * g + s
            span = (slice(s * N, (s + 1) * N), slice(g * LANES, (g + 1) * LANES))
            flat = slice((2 * s + g) * LANES, (2 * s + g + 1) * LANES)
            scores = scores_ref[span] + row(bias_row(h)) + masking
            e = jnp.exp(scores - jnp.max(scores, axis=-1, keepdims=True))
            p32 = e * (1.0 / jnp.sum(e, axis=-1, keepdims=True))
            p_ref[:, flat] = p32.astype(BF16)
            d_p = dp_ref[span]
            d_s = p32 * (d_p - jnp.sum(p32 * d_p, axis=-1, keepdims=True))
            a, b = halves(d_s)
            mine[pl.ds(h, CHIPS, stride=HEADS), :] = a
            theirs[pl.ds(h, CHIPS, stride=HEADS), :] = b
            ds_ref[:, flat] = d_s.astype(BF16)
    put(1, 6)
    attn = dot(p_ref[...], by_slot(v_halves))
    d_q = (dot(ds_ref[...], by_slot(k_halves)) * SCALE).astype(BF16)
    q_t = q.T
    da_t = d_attn.T
    dk_t = []
    dv_t = []
    for h in range(HEADS):
        g, s = divmod(h, 4)
        flat = slice((2 * s + g) * LANES, (2 * s + g + 1) * LANES)
        head = slice(h * HEAD_DIM, (h + 1) * HEAD_DIM)
        dk_t.append(dot(q_t[head], ds_ref[:, flat]))
        dv_t.append(dot(da_t[head], p_ref[:, flat]))
    d_k = jnp.concatenate(dk_t, axis=0).astype(BF16).T
    d_v = jnp.concatenate(dv_t, axis=0).astype(BF16).T
    weighted = (gate * attn).astype(BF16)
    update = dot(weighted, wo)
    d_g = (dw * attn * gate * (1.0 - gate)).astype(BF16)
    d_x = (
        dot_nt(d_q, wq_ref[...])
        + dot_nt(d_k, wk_ref[...])
        + dot_nt(d_v, wv_ref[...])
        + dot_nt(d_g, wg_ref[...])
    )
    adjoint = layer_norm_adjoint(d_x, hat, inv, gain)
    zeros = jnp.zeros((CHIPS, LANES), F32)
    for r, value in enumerate(
        (update[:, :LANES], update[:, LANES:], adjoint[:, :LANES], adjoint[:, LANES:])
    ):
        a, b = halves(value)
        mine[pl.ds(r, CHIPS, stride=8), :] = a
        mine[pl.ds(4 + r, CHIPS, stride=8), :] = zeros
        theirs[pl.ds(r, CHIPS, stride=8), :] = zeros
        theirs[pl.ds(4 + r, CHIPS, stride=8), :] = b
    put(0, 5)
    gain_out[...] = jnp.sum(d_x * hat, axis=0, keepdims=True)
    x_t = x.T
    w_t = weighted.T
    pairs = ((x_t, d_q), (x_t, d_k), (x_t, d_v), (x_t, d_g), (w_t, grad))
    mats = []
    for a, b in pairs:
        turned = jnp.concatenate([b[:, LANES:], b[:, :LANES]], axis=1)
        mats.append(dot(a, jnp.where(first, b, turned)))
    for ref, cols in ((own, slice(0, LANES)), (other, slice(LANES, FEATURES))):
        for tile, m in zip((2, 3, 7, 8, 4), mats):
            ref[:, tile] = m[:, cols].reshape(TILES, 8, LANES).astype(ref.dtype)


def pair_gradient(d_bias, pair, gain, w_bias, rows):
    rows[...] = listed(pair[0].astype(F32))
    hat, inv, scaled = layer_norm(reordered(rows), gain)
    parts = split(d_bias)[::-1]
    d_pln = sum(dot_tn(part, w_bias) for part in parts)
    head = sum(dot(part, scaled.astype(BF16)) for part in parts)
    return hat, inv, d_pln, head


def owner_kernel(pos, got, pair, gain, w_bias, d_gain, out, d_bias_out, rows, sums):
    value = got[...].astype(F32).reshape(TILES, 2 * PART_ROWS, LANES)
    sums[...] = jnp.sum(value, axis=0)
    total = sums[0:PART_ROWS, :] + sums[PART_ROWS:, :]
    sums[0:PART_ROWS, :] = total
    even = pos[2] % 2 == 0
    d_bias = jnp.where(even, sums[8:16, :], sums[12:20, :])
    weights = jnp.where(even, sums[16:32, :], sums[20:36, :])
    fifth = jnp.where(even, sums[32:36, :], sums[0:4, :])
    d_bias_out[...] = d_bias
    hat, _, d_pln, head = pair_gradient(d_bias, pair, gain[...], w_bias[...], rows)
    shard = jnp.concatenate(
        [
            weights,
            fifth,
            jnp.sum(d_pln * hat, axis=0, keepdims=True),
            d_gain[:, :LANES],
            d_gain[:, LANES:],
            jnp.zeros((1, LANES), F32),
            head,
        ],
        axis=0,
    )
    out[...] = jnp.broadcast_to(shard.astype(BF16)[None], (LINE, SUM_ROWS, LANES))


def unpack_kernel(pos, got, d_bias, pair, gain_ref, w_bias, update, adjoint, couple, stage, rows):
    stage[...] = got[...].astype(F32)
    first = pos[0] == 0
    even = pos[2] % 2 == 0

    def line(r):
        a, b = (stage[pl.ds(k, CHIPS, stride=PART_ROWS), :] for k in (r, 4 + r))
        return jnp.where(even, a, b)

    for index, out in enumerate((update, adjoint)):
        for half in range(2):
            r = 2 * index + half
            same, cross = line(r), line(4 + r)
            rows[pl.ds(0, CHIPS, stride=CORES), :] = jnp.where(first, same, cross)
            rows[pl.ds(1, CHIPS, stride=CORES), :] = jnp.where(first, cross, same)
            out[:, half * LANES : (half + 1) * LANES] = natural(rows[...]).astype(BF16)
    gain = gain_ref[...]
    hat, inv, d_pln, _ = pair_gradient(d_bias[...], pair, gain, w_bias[...], rows)
    restore(rows, layer_norm_adjoint(d_pln, hat, inv, gain))
    couple[0] = natural(rows[...]).astype(BF16)


def line_kernel(pos, got, out):
    low = lax.broadcasted_iota(jnp.int32, (1, 8, 1), 1) < 4
    tiles = got[...].astype(F32).reshape(LINE // 2, 2, 4, 8, LANES)
    even, odd = tiles[:, 0], tiles[:, 1]
    fifth = jnp.where(low, even[:, 2], pltpu.roll(odd[:, 2], 4, 1))
    sums = jnp.sum(tiles[:, :, 2:], axis=(0, 1))
    weights = (even[:, 0], even[:, 1], fifth, odd[:, 0], odd[:, 1])
    for w, value in enumerate(weights):
        value = value.astype(BF16)
        for t in range(LINE // 2):
            out[:, 5 * t + w] = jnp.broadcast_to(value[t][None], (LINE, 8, LANES))
    for n in range(2):
        out[:, 20 + n] = jnp.broadcast_to(sums[n].astype(BF16)[None], (LINE, 8, LANES))


def final_kernel(pos, mine, theirs, *refs):
    weights, (head, msa_gain, pair_gain) = refs[:5], refs[5:]
    for n, w in enumerate((0, 1, 4, 2, 3)):
        for side, got in enumerate((mine, theirs)):
            column = pl.multiple_of(LANES * jnp.bitwise_xor(pos[0], side), LANES)
            value = jnp.stack([got[:, 5 * t + n] for t in range(LINE // 2)], axis=1)
            value = value.astype(F32).reshape(FEATURES, LANES)
            weights[w][:, pl.ds(column, LANES)] = value
    sums = sum(jnp.sum(got[:, 20:].astype(F32), axis=0) for got in (mine, theirs))
    head[...] = sums[1]
    pair_gain[...] = sums[0, 4:5]
    msa_gain[:, :LANES] = sums[0, 5:6]
    msa_gain[:, LANES:] = sums[0, 6:7]


def on_device(msa, flags, pair, gain, pair_gain, wq, wk, wv, wg, wo, w_bias, grad):
    index = lax.axis_index("dap")
    pos = jnp.stack([index % CORES, index, index // CORES]).astype(jnp.int32)
    chips = [LINE * q + z for q in LINES for z in range(LINE)]
    same_core = [[CORES * m + c for m in chips] for c in range(CORES)]
    along_z = [g[LINE * q : LINE * (q + 1)] for g in same_core for q in range(LINE)]
    across = [g[z::LINE] for g in same_core for z in range(LINE)]
    partner = [(i, i ^ 1) for i in range(N)]

    def exchange(x, groups):
        return lax.all_to_all(
            x, "dap", split_axis=0, concat_axis=0, tiled=True, axis_index_groups=groups
        )

    w_bias = w_bias.T
    gain = gain.reshape(1, FEATURES)
    pair_gain = pair_gain.reshape(1, LANES)
    kept = (pair, pair_gain, w_bias, wq, wk, wv, wg, wo, gain)
    sent, *kept = call(
        entry_kernel,
        (jax.ShapeDtypeStruct((CHIPS * IN_ROWS, LANES), BF16),)
        + tuple(jax.ShapeDtypeStruct(v.shape, v.dtype) for v in kept),
        [
            pltpu.VMEM((N, FEATURES), BF16),
            pltpu.VMEM((N, FEATURES), BF16),
            pltpu.VMEM((1, N), jnp.int32),
            pltpu.VMEM((CHIPS * IN_ROWS, LANES), F32),
            pltpu.VMEM((N, LANES), F32),
            pltpu.SemaphoreType.DMA((12,)),
        ],
        *kept, msa.reshape(N, FEATURES), grad.reshape(N, FEATURES), flags.reshape(1, N),
        far_in=range(12),
    )
    pair, pair_gain, w_bias, wq, wk, wv, wg, wo, gain = kept
    near = exchange(sent.reshape(CHIPS, IN_ROWS // 2, 2, LANES), same_core)
    near = near.reshape(CHIPS * IN_ROWS, LANES)
    far = lax.ppermute(near, "dap", partner)
    part = (TILES, PART_TILES, 8, LANES)
    own, other, d_gain = call(
        sequence_kernel,
        (
            jax.ShapeDtypeStruct(part, F32),
            jax.ShapeDtypeStruct(part, BF16),
            jax.ShapeDtypeStruct((1, FEATURES), F32),
        ),
        [
            pltpu.VMEM((CORES, CHIPS * IN_ROWS, LANES), F32),
            pltpu.VMEM((CHIPS * 8, LANES), F32),
            pltpu.VMEM((CHIPS * 8, LANES), F32),
            pltpu.VMEM((4 * N, FEATURES), F32),
            pltpu.VMEM((4 * N, FEATURES), F32),
            pltpu.VMEM((N, HEADS * LANES), BF16),
            pltpu.VMEM((N, HEADS * LANES), BF16),
        ],
        pos, near, far, gain, wq, wk, wv, wg, wo,
    )
    paired = (own + lax.ppermute(other, "dap", partner).astype(F32)).astype(BF16)
    got = exchange(paired.reshape(CHIPS, PART_TILES, 4, LANES), same_core)
    got = got.reshape(CHIPS * PART_ROWS, LANES)
    shard, d_bias = call(
        owner_kernel,
        (
            jax.ShapeDtypeStruct((LINE, SUM_ROWS, LANES), BF16),
            jax.ShapeDtypeStruct((HEADS, LANES), F32),
        ),
        [pltpu.VMEM((N, LANES), F32), pltpu.VMEM((2 * PART_ROWS, LANES), F32)],
        pos, got, pair, pair_gain, w_bias, d_gain,
    )
    line = call(
        line_kernel,
        jax.ShapeDtypeStruct((LINE, LINE_TILES, 8, LANES), BF16),
        [],
        pos, exchange(shard, along_z),
    )
    mine = exchange(line, across)
    row_shape = jax.ShapeDtypeStruct((N, FEATURES), BF16)
    update, adjoint, couple = call(
        unpack_kernel,
        (row_shape, row_shape, jax.ShapeDtypeStruct((1, N, LANES), BF16)),
        [pltpu.VMEM((CHIPS * PART_ROWS, LANES), F32), pltpu.VMEM((N, LANES), F32)],
        pos, got, d_bias, pair, pair_gain, w_bias,
    )
    theirs = lax.ppermute(mine, "dap", partner)
    *weights, head, msa_gain, pair_gain = call(
        final_kernel,
        (jax.ShapeDtypeStruct((FEATURES, FEATURES), F32),) * 5
        + (
            jax.ShapeDtypeStruct((HEADS, LANES), F32),
            jax.ShapeDtypeStruct((1, FEATURES), F32),
            jax.ShapeDtypeStruct((1, LANES), F32),
        ),
        [],
        pos, mine, theirs,
    )
    return (
        update.reshape(N, 1, FEATURES),
        adjoint.reshape(N, 1, FEATURES),
        couple,
        *weights,
        head.T,
        msa_gain.reshape(FEATURES),
        pair_gain.reshape(LANES),
    )


def solution(mesh):
    rows = P("dp", "dap", None)
    pair = P(("dp", "dap"), None, None)
    in_specs = (rows, P("dp", "dap"), pair) + (P(),) * 8 + (rows,)
    out_specs = (rows, rows, pair) + (P("dp", None),) * 6 + (P("dp"), P("dp"))
    return jax.shard_map(
        on_device, mesh=mesh, in_specs=in_specs, out_specs=out_specs, check_vma=False
    )
```

```python
import jax
import jax.numpy as jnp
from jax import lax
from jax.experimental import pallas as pl
from jax.experimental.pallas import tpu as pltpu
from jax.sharding import PartitionSpec as P

FEATURES = 256
HEADS = 8
HEAD_DIM = 32
LANES = 128
CORES = 2
CHIPS = 64
N = CORES * CHIPS
TILES = CHIPS // 2
SCALE = HEAD_DIM ** (-0.5)
EPS = 1e-05

F32 = jnp.float32
BF16 = jnp.bfloat16

IN_ROWS = 18
PART_ROWS = 36
PART_TILES = 9
SUM_ROWS = 32
LINE = 8
LINE_TILES = 22

VMEM = pl.BlockSpec(memory_space=pltpu.VMEM)
SMEM = pl.BlockSpec(memory_space=pltpu.SMEM)
HBM = pl.BlockSpec(memory_space=pltpu.HBM)


def dot(a, b):
    return jnp.dot(a, b, preferred_element_type=F32)


def dot_nt(a, b):
    return lax.dot_general(a, b, (((1,), (1,)), ((), ())), preferred_element_type=F32)


def dot_tn(a, b):
    return lax.dot_general(a, b, (((0,), (0,)), ((), ())), preferred_element_type=F32)


def layer_norm(value, gain):
    mean = jnp.mean(value, axis=-1, keepdims=True)
    centered = value - mean
    variance = jnp.mean(centered * centered, axis=-1, keepdims=True)
    inv = lax.rsqrt(variance + EPS)
    hat = centered * inv
    return hat, inv, hat * gain


def layer_norm_adjoint(upstream, hat, inv, gain):
    ug = upstream * gain
    return inv * (
        ug
        - jnp.mean(ug, axis=-1, keepdims=True)
        - hat * jnp.mean(ug * hat, axis=-1, keepdims=True)
    )


def split(x):
    high = x.astype(BF16)
    rest = x - high.astype(F32)
    mid = rest.astype(BF16)
    return high, mid, (rest - mid.astype(F32)).astype(BF16)


ORDER = [(c, p) for c in range(CORES) for p in range(2)]


LINES = (7, 4, 5, 6, 3, 0, 1, 2)
FIRST_Z = 6


def turned(value):
    blocks = value.reshape(8, 2, 8, value.shape[-1])
    low = lax.broadcasted_iota(jnp.int32, (1, 8, 1), 1) < 4
    upper, lower = (pltpu.roll(blocks[:, n], 4, 1) for n in range(2))
    both = (jnp.where(low, lower, upper), jnp.where(low, upper, lower))
    return both


def listed(value):
    first, second = turned(value)
    return jnp.concatenate([v for q in LINES for v in (first[q], second[q])], axis=0)


def natural(value):
    first, second = turned(value)
    return jnp.concatenate(
        [v for q in range(8) for v in (second[LINES.index(q)], first[LINES.index(q)])], axis=0
    )


def reordered(rows):
    return jnp.concatenate(
        [rows[pl.ds(2 * p + c, TILES, stride=4), :] for c, p in ORDER], axis=0
    )


def restore(rows, value):
    for n, (c, p) in enumerate(ORDER):
        rows[pl.ds(2 * p + c, TILES, stride=4), :] = value[n * TILES : (n + 1) * TILES]


def bias_row(h):
    return 4 + h if h < 5 else 8 + h


def call(kernel, out_shape, scratch, *operands, far_in=()):
    in_specs = [SMEM] + [VMEM] * (len(operands) - 1)
    operands = list(operands)
    for n in far_in:
        in_specs[n] = HBM
        operands[n] = pltpu.with_memory_space_constraint(operands[n], pltpu.HBM)
    return pl.pallas_call(
        kernel,
        out_shape=out_shape,
        in_specs=in_specs,
        out_specs=jax.tree.map(lambda _: VMEM, out_shape),
        scratch_shapes=scratch,
        compiler_params=pltpu.CompilerParams(vmem_limit_bytes=12 * 1024 * 1024),
    )(*operands)


def entry_kernel(*refs):
    sources, out, kept, (msa, grad, flags, stage, rows, sems) = (
        refs[:12], refs[12], refs[13:22], refs[22:]
    )
    targets = kept + (msa, grad, flags)
    copies = [
        pltpu.make_async_copy(a, b, sems.at[i]) for i, (a, b) in enumerate(zip(sources, targets))
    ]
    for n in (0, 1, 2, 9, 10, 11, 3, 4, 5, 6, 7, 8):
        copies[n].start()
    pair, gain, w_bias = kept[:3]
    for copy in copies[:3]:
        copy.wait()
    rows[...] = listed(pair[0].astype(F32))
    _, _, scaled = layer_norm(reordered(rows), gain[...])
    bias = dot_nt(w_bias[...], scaled.astype(BF16))
    for copy in copies[9:]:
        copy.wait()
    for r, ref in enumerate((msa, grad)):
        value = listed(ref[...].astype(F32))
        stage[pl.ds(2 * r, N, stride=9), :] = value[:, :LANES]
        stage[pl.ds(2 * r + 1, N, stride=9), :] = value[:, LANES:]
    lines = [(bias_row(h), bias[h : h + 1]) for h in range(HEADS)]
    lines += [(16, flags[...].astype(F32)), (17, jnp.zeros((1, LANES), F32))]
    for r, value in lines:
        stage[pl.ds(r, CHIPS, stride=IN_ROWS), :] = jnp.broadcast_to(value, (CHIPS, LANES))
    out[...] = stage[...].astype(BF16)
    for copy in copies[3:9]:
        copy.wait()


def sequence_kernel(
    pos, near, far, gain_ref, wq_ref, wk_ref, wv_ref, wg_ref, wo_ref,
    own, other, gain_out, rows, mine, theirs, scores_ref, dp_ref, p_ref, ds_ref
):
    core = pos[0]
    first = core == 0
    rows[core] = near[...].astype(F32)
    rows[1 - core] = far[...].astype(F32)

    def row(r):
        return jnp.concatenate(
            [
                rows.at[c][pl.ds(r + p * IN_ROWS, TILES, stride=2 * IN_ROWS), :]
                for c, p in ORDER
            ],
            axis=0,
        )

    def line(r):
        return jnp.where(first, row(r), row(9 + r))

    def halves(value):
        return (
            jnp.where(first, value[:CHIPS], value[CHIPS:]),
            jnp.where(first, value[CHIPS:], value[:CHIPS]),
        )

    gain = gain_ref[...]
    msa = jnp.concatenate([line(0), line(1)], axis=1)
    grad = jnp.concatenate([line(2), line(3)], axis=1).astype(BF16)
    lane = lax.broadcasted_iota(jnp.int32, (8, LANES), 1)
    pick = jnp.where(lane == pos[1], 1.0, 0.0).astype(BF16)
    flags = dot_nt(pick, row(16).astype(BF16))[:1]
    masking = 1e9 * (flags - 1.0)
    hat, inv, scaled = layer_norm(msa, gain)
    x = scaled.astype(BF16)
    wo = wo_ref[...]
    q = (dot(x, wq_ref[...]) * SCALE).astype(BF16)
    k = dot(x, wk_ref[...]).astype(BF16)
    v = dot(x, wv_ref[...]).astype(BF16)
    gate = jax.nn.sigmoid(dot(x, wg_ref[...]))
    dw = dot_nt(grad, wo)
    d_attn = (dw * gate).astype(BF16)

    lane = lax.broadcasted_iota(jnp.int32, (1, FEATURES), 1)
    slot = (lane % LANES) // HEAD_DIM
    in_slot = [jnp.where(slot == s, 1.0, 0.0).astype(BF16) for s in range(4)]
    in_half = [jnp.where(lane // LANES == g, 1.0, 0.0).astype(BF16) for g in range(2)]

    def by_half(value):
        return jnp.concatenate([value * keep for keep in in_half], axis=0)

    def by_slot(value):
        return jnp.concatenate([value * keep for keep in in_slot], axis=0)

    def put(even, odd):
        for ref, rows8 in ((own, mine), (other, theirs)):
            value = rows8[...].astype(ref.dtype).reshape(2, TILES, 8, LANES)
            ref[:, even] = value[0]
            ref[:, odd] = value[1]

    k_halves, v_halves = by_half(k), by_half(v)
    scores_ref[...] = dot_nt(by_slot(q), k_halves)
    dp_ref[...] = dot_nt(by_slot(d_attn), v_halves)
    for s in range(4):
        for g in range(2):
            h = 4 * g + s
            span = (slice(s * N, (s + 1) * N), slice(g * LANES, (g + 1) * LANES))
            flat = slice((2 * s + g) * LANES, (2 * s + g + 1) * LANES)
            scores = scores_ref[span] + row(bias_row(h)) + masking
            e = jnp.exp(scores - jnp.max(scores, axis=-1, keepdims=True))
            p32 = e * (1.0 / jnp.sum(e, axis=-1, keepdims=True))
            p_ref[:, flat] = p32.astype(BF16)
            d_p = dp_ref[span]
            d_s = p32 * (d_p - jnp.sum(p32 * d_p, axis=-1, keepdims=True))
            a, b = halves(d_s)
            mine[pl.ds(h, CHIPS, stride=HEADS), :] = a
            theirs[pl.ds(h, CHIPS, stride=HEADS), :] = b
            ds_ref[:, flat] = d_s.astype(BF16)
    put(1, 6)
    attn = dot(p_ref[...], by_slot(v_halves))
    d_q = (dot(ds_ref[...], by_slot(k_halves)) * SCALE).astype(BF16)
    q_t = q.T
    da_t = d_attn.T
    dk_t = []
    dv_t = []
    for h in range(HEADS):
        g, s = divmod(h, 4)
        flat = slice((2 * s + g) * LANES, (2 * s + g + 1) * LANES)
        head = slice(h * HEAD_DIM, (h + 1) * HEAD_DIM)
        dk_t.append(dot(q_t[head], ds_ref[:, flat]))
        dv_t.append(dot(da_t[head], p_ref[:, flat]))
    d_k = jnp.concatenate(dk_t, axis=0).astype(BF16).T
    d_v = jnp.concatenate(dv_t, axis=0).astype(BF16).T
    weighted = (gate * attn).astype(BF16)
    update = dot(weighted, wo)
    d_g = (dw * attn * gate * (1.0 - gate)).astype(BF16)
    d_x = (
        dot_nt(d_q, wq_ref[...])
        + dot_nt(d_k, wk_ref[...])
        + dot_nt(d_v, wv_ref[...])
        + dot_nt(d_g, wg_ref[...])
    )
    adjoint = layer_norm_adjoint(d_x, hat, inv, gain)
    zeros = jnp.zeros((CHIPS, LANES), F32)
    for r, value in enumerate(
        (update[:, :LANES], update[:, LANES:], adjoint[:, :LANES], adjoint[:, LANES:])
    ):
        a, b = halves(value)
        mine[pl.ds(r, CHIPS, stride=8), :] = a
        mine[pl.ds(4 + r, CHIPS, stride=8), :] = zeros
        theirs[pl.ds(r, CHIPS, stride=8), :] = zeros
        theirs[pl.ds(4 + r, CHIPS, stride=8), :] = b
    put(0, 5)
    gain_out[...] = jnp.sum(d_x * hat, axis=0, keepdims=True)
    x_t = x.T
    w_t = weighted.T
    pairs = ((x_t, d_q), (x_t, d_k), (x_t, d_v), (x_t, d_g), (w_t, grad))
    mats = []
    for a, b in pairs:
        turned = jnp.concatenate([b[:, LANES:], b[:, :LANES]], axis=1)
        mats.append(dot(a, jnp.where(first, b, turned)))
    for ref, cols in ((own, slice(0, LANES)), (other, slice(LANES, FEATURES))):
        for tile, m in zip((2, 3, 7, 8, 4), mats):
            ref[:, tile] = m[:, cols].reshape(TILES, 8, LANES).astype(ref.dtype)


def pair_gradient(d_bias, pair, gain, w_bias, rows):
    rows[...] = listed(pair[0].astype(F32))
    hat, inv, scaled = layer_norm(reordered(rows), gain)
    parts = split(d_bias)[::-1]
    d_pln = sum(dot_tn(part, w_bias) for part in parts)
    head = sum(dot(part, scaled.astype(BF16)) for part in parts)
    return hat, inv, d_pln, head


def owner_kernel(pos, got, pair, gain, w_bias, d_gain, out, d_bias_out, rows, sums):
    value = got[...].astype(F32).reshape(TILES, 2 * PART_ROWS, LANES)
    sums[...] = jnp.sum(value, axis=0)
    total = sums[0:PART_ROWS, :] + sums[PART_ROWS:, :]
    sums[0:PART_ROWS, :] = total
    even = pos[2] % 2 == 0
    d_bias = jnp.where(even, sums[8:16, :], sums[12:20, :])
    weights = jnp.where(even, sums[16:32, :], sums[20:36, :])
    fifth = jnp.where(even, sums[32:36, :], sums[0:4, :])
    d_bias_out[...] = d_bias
    hat, _, d_pln, head = pair_gradient(d_bias, pair, gain[...], w_bias[...], rows)
    shard = jnp.concatenate(
        [
            weights,
            fifth,
            jnp.sum(d_pln * hat, axis=0, keepdims=True),
            d_gain[:, :LANES],
            d_gain[:, LANES:],
            jnp.zeros((1, LANES), F32),
            head,
        ],
        axis=0,
    )
    out[...] = jnp.broadcast_to(shard.astype(BF16)[None], (LINE, SUM_ROWS, LANES))


def unpack_kernel(pos, got, d_bias, pair, gain_ref, w_bias, update, adjoint, couple, stage, rows):
    stage[...] = got[...].astype(F32)
    first = pos[0] == 0
    even = pos[2] % 2 == 0

    def line(r):
        a, b = (stage[pl.ds(k, CHIPS, stride=PART_ROWS), :] for k in (r, 4 + r))
        return jnp.where(even, a, b)

    for index, out in enumerate((update, adjoint)):
        for half in range(2):
            r = 2 * index + half
            same, cross = line(r), line(4 + r)
            rows[pl.ds(0, CHIPS, stride=CORES), :] = jnp.where(first, same, cross)
            rows[pl.ds(1, CHIPS, stride=CORES), :] = jnp.where(first, cross, same)
            out[:, half * LANES : (half + 1) * LANES] = natural(rows[...]).astype(BF16)
    gain = gain_ref[...]
    hat, inv, d_pln, _ = pair_gradient(d_bias[...], pair, gain, w_bias[...], rows)
    restore(rows, layer_norm_adjoint(d_pln, hat, inv, gain))
    couple[0] = natural(rows[...]).astype(BF16)


def line_kernel(pos, got, out):
    low = lax.broadcasted_iota(jnp.int32, (1, 8, 1), 1) < 4
    tiles = got[...].astype(F32).reshape(LINE // 2, 2, 4, 8, LANES)
    even, odd = tiles[:, 0], tiles[:, 1]
    fifth = jnp.where(low, even[:, 2], pltpu.roll(odd[:, 2], 4, 1))
    sums = jnp.sum(tiles[:, :, 2:], axis=(0, 1))
    weights = (even[:, 0], even[:, 1], fifth, odd[:, 0], odd[:, 1])
    for w, value in enumerate(weights):
        value = value.astype(BF16)
        for t in range(LINE // 2):
            out[:, 5 * t + w] = jnp.broadcast_to(value[t][None], (LINE, 8, LANES))
    for n in range(2):
        out[:, 20 + n] = jnp.broadcast_to(sums[n].astype(BF16)[None], (LINE, 8, LANES))


def final_kernel(pos, mine, theirs, *refs):
    weights, (head, msa_gain, pair_gain) = refs[:5], refs[5:]
    for n, w in enumerate((0, 1, 4, 2, 3)):
        for side, got in enumerate((mine, theirs)):
            column = pl.multiple_of(LANES * jnp.bitwise_xor(pos[0], side), LANES)
            value = jnp.stack([got[:, 5 * t + n] for t in range(LINE // 2)], axis=1)
            value = value.astype(F32).reshape(FEATURES, LANES)
            weights[w][:, pl.ds(column, LANES)] = value
    sums = sum(jnp.sum(got[:, 20:].astype(F32), axis=0) for got in (mine, theirs))
    head[...] = sums[1]
    pair_gain[...] = sums[0, 4:5]
    msa_gain[:, :LANES] = sums[0, 5:6]
    msa_gain[:, LANES:] = sums[0, 6:7]


def on_device(msa, flags, pair, gain, pair_gain, wq, wk, wv, wg, wo, w_bias, grad):
    index = lax.axis_index("dap")
    pos = jnp.stack([index % CORES, index, index // CORES]).astype(jnp.int32)
    chips = [LINE * q + (FIRST_Z + z) % LINE for q in LINES for z in range(LINE)]
    same_core = [[CORES * m + c for m in chips] for c in range(CORES)]
    along_z = [g[LINE * q : LINE * (q + 1)] for g in same_core for q in range(LINE)]
    across = [g[z::LINE] for g in same_core for z in range(LINE)]
    partner = [(i, i ^ 1) for i in range(N)]

    def exchange(x, groups):
        return lax.all_to_all(
            x, "dap", split_axis=0, concat_axis=0, tiled=True, axis_index_groups=groups
        )

    w_bias = w_bias.T
    gain = gain.reshape(1, FEATURES)
    pair_gain = pair_gain.reshape(1, LANES)
    kept = (pair, pair_gain, w_bias, wq, wk, wv, wg, wo, gain)
    sent, *kept = call(
        entry_kernel,
        (jax.ShapeDtypeStruct((CHIPS * IN_ROWS, LANES), BF16),)
        + tuple(jax.ShapeDtypeStruct(v.shape, v.dtype) for v in kept),
        [
            pltpu.VMEM((N, FEATURES), BF16),
            pltpu.VMEM((N, FEATURES), BF16),
            pltpu.VMEM((1, N), jnp.int32),
            pltpu.VMEM((CHIPS * IN_ROWS, LANES), F32),
            pltpu.VMEM((N, LANES), F32),
            pltpu.SemaphoreType.DMA((12,)),
        ],
        *kept, msa.reshape(N, FEATURES), grad.reshape(N, FEATURES), flags.reshape(1, N),
        far_in=range(12),
    )
    pair, pair_gain, w_bias, wq, wk, wv, wg, wo, gain = kept
    near = exchange(sent.reshape(CHIPS, IN_ROWS // 2, 2, LANES), same_core)
    near = near.reshape(CHIPS * IN_ROWS, LANES)
    far = lax.ppermute(near, "dap", partner)
    part = (TILES, PART_TILES, 8, LANES)
    own, other, d_gain = call(
        sequence_kernel,
        (
            jax.ShapeDtypeStruct(part, F32),
            jax.ShapeDtypeStruct(part, BF16),
            jax.ShapeDtypeStruct((1, FEATURES), F32),
        ),
        [
            pltpu.VMEM((CORES, CHIPS * IN_ROWS, LANES), F32),
            pltpu.VMEM((CHIPS * 8, LANES), F32),
            pltpu.VMEM((CHIPS * 8, LANES), F32),
            pltpu.VMEM((4 * N, FEATURES), F32),
            pltpu.VMEM((4 * N, FEATURES), F32),
            pltpu.VMEM((N, HEADS * LANES), BF16),
            pltpu.VMEM((N, HEADS * LANES), BF16),
        ],
        pos, near, far, gain, wq, wk, wv, wg, wo,
    )
    paired = (own + lax.ppermute(other, "dap", partner).astype(F32)).astype(BF16)
    got = exchange(paired.reshape(CHIPS, PART_TILES, 4, LANES), same_core)
    got = got.reshape(CHIPS * PART_ROWS, LANES)
    shard, d_bias = call(
        owner_kernel,
        (
            jax.ShapeDtypeStruct((LINE, SUM_ROWS, LANES), BF16),
            jax.ShapeDtypeStruct((HEADS, LANES), F32),
        ),
        [pltpu.VMEM((N, LANES), F32), pltpu.VMEM((2 * PART_ROWS, LANES), F32)],
        pos, got, pair, pair_gain, w_bias, d_gain,
    )
    line = call(
        line_kernel,
        jax.ShapeDtypeStruct((LINE, LINE_TILES, 8, LANES), BF16),
        [],
        pos, exchange(shard, along_z),
    )
    mine = exchange(line, across)
    row_shape = jax.ShapeDtypeStruct((N, FEATURES), BF16)
    update, adjoint, couple = call(
        unpack_kernel,
        (row_shape, row_shape, jax.ShapeDtypeStruct((1, N, LANES), BF16)),
        [pltpu.VMEM((CHIPS * PART_ROWS, LANES), F32), pltpu.VMEM((N, LANES), F32)],
        pos, got, d_bias, pair, pair_gain, w_bias,
    )
    theirs = lax.ppermute(mine, "dap", partner)
    *weights, head, msa_gain, pair_gain = call(
        final_kernel,
        (jax.ShapeDtypeStruct((FEATURES, FEATURES), F32),) * 5
        + (
            jax.ShapeDtypeStruct((HEADS, LANES), F32),
            jax.ShapeDtypeStruct((1, FEATURES), F32),
            jax.ShapeDtypeStruct((1, LANES), F32),
        ),
        [],
        pos, mine, theirs,
    )
    return (
        update.reshape(N, 1, FEATURES),
        adjoint.reshape(N, 1, FEATURES),
        couple,
        *weights,
        head.T,
        msa_gain.reshape(FEATURES),
        pair_gain.reshape(LANES),
    )


def solution(mesh):
    rows = P("dp", "dap", None)
    pair = P(("dp", "dap"), None, None)
    in_specs = (rows, P("dp", "dap"), pair) + (P(),) * 8 + (rows,)
    out_specs = (rows, rows, pair) + (P("dp", None),) * 6 + (P("dp"), P("dp"))
    return jax.shard_map(
        on_device, mesh=mesh, in_specs=in_specs, out_specs=out_specs, check_vma=False
    )
```

```python
import jax
import jax.numpy as jnp
from jax import lax
from jax.experimental import pallas as pl
from jax.experimental.pallas import tpu as pltpu
from jax.sharding import PartitionSpec as P

FEATURES = 256
HEADS = 8
HEAD_DIM = 32
LANES = 128
CORES = 2
CHIPS = 64
N = CORES * CHIPS
TILES = CHIPS // 2
SCALE = HEAD_DIM ** (-0.5)
EPS = 1e-05

F32 = jnp.float32
BF16 = jnp.bfloat16

IN_ROWS = 18
PART_ROWS = 36
PART_TILES = 9
SUM_ROWS = 32
LINE = 8
LINE_TILES = 22

VMEM = pl.BlockSpec(memory_space=pltpu.VMEM)
SMEM = pl.BlockSpec(memory_space=pltpu.SMEM)
HBM = pl.BlockSpec(memory_space=pltpu.HBM)


def dot(a, b):
    return jnp.dot(a, b, preferred_element_type=F32)


def dot_nt(a, b):
    return lax.dot_general(a, b, (((1,), (1,)), ((), ())), preferred_element_type=F32)


def dot_tn(a, b):
    return lax.dot_general(a, b, (((0,), (0,)), ((), ())), preferred_element_type=F32)


def layer_norm(value, gain):
    mean = jnp.mean(value, axis=-1, keepdims=True)
    centered = value - mean
    variance = jnp.mean(centered * centered, axis=-1, keepdims=True)
    inv = lax.rsqrt(variance + EPS)
    hat = centered * inv
    return hat, inv, hat * gain


def layer_norm_adjoint(upstream, hat, inv, gain):
    ug = upstream * gain
    return inv * (
        ug
        - jnp.mean(ug, axis=-1, keepdims=True)
        - hat * jnp.mean(ug * hat, axis=-1, keepdims=True)
    )


def split(x):
    high = x.astype(BF16)
    rest = x - high.astype(F32)
    mid = rest.astype(BF16)
    return high, mid, (rest - mid.astype(F32)).astype(BF16)


ORDER = [(c, p) for c in range(CORES) for p in range(2)]


LINES = (7, 4, 5, 6, 3, 0, 1, 2)
FIRST_Z = 6


def turned(value):
    blocks = value.reshape(8, 2, 8, value.shape[-1])
    low = lax.broadcasted_iota(jnp.int32, (1, 8, 1), 1) < 4
    upper, lower = (pltpu.roll(blocks[:, n], 4, 1) for n in range(2))
    both = (jnp.where(low, lower, upper), jnp.where(low, upper, lower))
    return both


def listed(value):
    first, second = turned(value)
    return jnp.concatenate([v for q in LINES for v in (first[q], second[q])], axis=0)


def natural(value):
    first, second = turned(value)
    return jnp.concatenate(
        [v for q in range(8) for v in (second[LINES.index(q)], first[LINES.index(q)])], axis=0
    )


def reordered(rows):
    return jnp.concatenate(
        [rows[pl.ds(2 * p + c, TILES, stride=4), :] for c, p in ORDER], axis=0
    )


def restore(rows, value):
    for n, (c, p) in enumerate(ORDER):
        rows[pl.ds(2 * p + c, TILES, stride=4), :] = value[n * TILES : (n + 1) * TILES]


def bias_row(h):
    return 4 + h if h < 5 else 8 + h


def call(kernel, out_shape, scratch, *operands, far_in=()):
    in_specs = [SMEM] + [VMEM] * (len(operands) - 1)
    operands = list(operands)
    for n in far_in:
        in_specs[n] = HBM
        operands[n] = pltpu.with_memory_space_constraint(operands[n], pltpu.HBM)
    return pl.pallas_call(
        kernel,
        out_shape=out_shape,
        in_specs=in_specs,
        out_specs=jax.tree.map(lambda _: VMEM, out_shape),
        scratch_shapes=scratch,
        compiler_params=pltpu.CompilerParams(vmem_limit_bytes=12 * 1024 * 1024),
    )(*operands)


def entry_kernel(*refs):
    sources, out, kept, (msa, grad, flags, stage, rows, sems) = (
        refs[:12], refs[12], refs[13:22], refs[22:]
    )
    targets = kept + (msa, grad, flags)
    copies = [
        pltpu.make_async_copy(a, b, sems.at[i]) for i, (a, b) in enumerate(zip(sources, targets))
    ]
    for n in (0, 1, 2, 9, 10, 11, 3, 4, 5, 6, 7, 8):
        copies[n].start()
    pair, gain, w_bias = kept[:3]
    for copy in copies[:3]:
        copy.wait()
    rows[...] = listed(pair[0].astype(F32))
    _, _, scaled = layer_norm(reordered(rows), gain[...])
    bias = dot_nt(w_bias[...], scaled.astype(BF16))
    for copy in copies[9:]:
        copy.wait()
    for r, ref in enumerate((msa, grad)):
        value = listed(ref[...].astype(F32))
        stage[pl.ds(2 * r, N, stride=9), :] = value[:, :LANES]
        stage[pl.ds(2 * r + 1, N, stride=9), :] = value[:, LANES:]
    lines = [(bias_row(h), bias[h : h + 1]) for h in range(HEADS)]
    lines += [(16, flags[...].astype(F32)), (17, jnp.zeros((1, LANES), F32))]
    for r, value in lines:
        stage[pl.ds(r, CHIPS, stride=IN_ROWS), :] = jnp.broadcast_to(value, (CHIPS, LANES))
    out[...] = stage[...].astype(BF16)
    for copy in copies[3:9]:
        copy.wait()


def sequence_kernel(
    pos, near, far, gain_ref, wq_ref, wk_ref, wv_ref, wg_ref, wo_ref,
    own, other, gain_out, rows, mine, theirs, scores_ref, dp_ref, p_ref, ds_ref
):
    core = pos[0]
    first = core == 0
    rows[core] = near[...].astype(F32)
    rows[1 - core] = far[...].astype(F32)

    def row(r):
        return jnp.concatenate(
            [
                rows.at[c][pl.ds(r + p * IN_ROWS, TILES, stride=2 * IN_ROWS), :]
                for c, p in ORDER
            ],
            axis=0,
        )

    def line(r):
        return jnp.where(first, row(r), row(9 + r))

    def halves(value):
        return (
            jnp.where(first, value[:CHIPS], value[CHIPS:]),
            jnp.where(first, value[CHIPS:], value[:CHIPS]),
        )

    gain = gain_ref[...]
    msa = jnp.concatenate([line(0), line(1)], axis=1)
    grad = jnp.concatenate([line(2), line(3)], axis=1).astype(BF16)
    lane = lax.broadcasted_iota(jnp.int32, (8, LANES), 1)
    pick = jnp.where(lane == pos[1], 1.0, 0.0).astype(BF16)
    flags = dot_nt(pick, row(16).astype(BF16))[:1]
    masking = 1e9 * (flags - 1.0)
    hat, inv, scaled = layer_norm(msa, gain)
    x = scaled.astype(BF16)
    wo = wo_ref[...]
    q = (dot(x, wq_ref[...]) * SCALE).astype(BF16)
    k = dot(x, wk_ref[...]).astype(BF16)
    v = dot(x, wv_ref[...]).astype(BF16)
    gate = jax.nn.sigmoid(dot(x, wg_ref[...]))
    dw = dot_nt(grad, wo)
    d_attn = (dw * gate).astype(BF16)

    lane = lax.broadcasted_iota(jnp.int32, (1, FEATURES), 1)
    slot = (lane % LANES) // HEAD_DIM
    in_slot = [jnp.where(slot == s, 1.0, 0.0).astype(BF16) for s in range(4)]
    in_half = [jnp.where(lane // LANES == g, 1.0, 0.0).astype(BF16) for g in range(2)]

    def by_half(value):
        return jnp.concatenate([value * keep for keep in in_half], axis=0)

    def by_slot(value):
        return jnp.concatenate([value * keep for keep in in_slot], axis=0)

    def put(even, odd):
        for ref, rows8 in ((own, mine), (other, theirs)):
            value = rows8[...].astype(ref.dtype).reshape(2, TILES, 8, LANES)
            ref[:, even] = value[0]
            ref[:, odd] = value[1]

    k_halves, v_halves = by_half(k), by_half(v)
    scores_ref[...] = dot_nt(by_slot(q), k_halves)
    dp_ref[...] = dot_nt(by_slot(d_attn), v_halves)
    for s in range(4):
        for g in range(2):
            h = 4 * g + s
            span = (slice(s * N, (s + 1) * N), slice(g * LANES, (g + 1) * LANES))
            flat = slice((2 * s + g) * LANES, (2 * s + g + 1) * LANES)
            scores = scores_ref[span] + row(bias_row(h)) + masking
            e = jnp.exp(scores - jnp.max(scores, axis=-1, keepdims=True))
            p32 = e * (1.0 / jnp.sum(e, axis=-1, keepdims=True))
            p_ref[:, flat] = p32.astype(BF16)
            d_p = dp_ref[span]
            d_s = p32 * (d_p - jnp.sum(p32 * d_p, axis=-1, keepdims=True))
            a, b = halves(d_s)
            mine[pl.ds(h, CHIPS, stride=HEADS), :] = a
            theirs[pl.ds(h, CHIPS, stride=HEADS), :] = b
            ds_ref[:, flat] = d_s.astype(BF16)
    put(1, 6)
    attn = dot(p_ref[...], by_slot(v_halves))
    d_q = (dot(ds_ref[...], by_slot(k_halves)) * SCALE).astype(BF16)
    q_t = q.T
    da_t = d_attn.T
    dk_t = [None] * HEADS
    dv_t = [None] * HEADS
    for s in range(4):
        flat = slice(2 * s * LANES, 2 * (s + 1) * LANES)
        for out, left, right in ((dk_t, q_t, ds_ref), (dv_t, da_t, p_ref)):
            both = jnp.concatenate(
                [left[h * HEAD_DIM : (h + 1) * HEAD_DIM] for h in (s, 4 + s)], axis=0
            )
            both = dot(both, right[:, flat])
            out[s] = both[:HEAD_DIM, :LANES]
            out[4 + s] = both[HEAD_DIM:, LANES:]
    d_k = jnp.concatenate(dk_t, axis=0).astype(BF16).T
    d_v = jnp.concatenate(dv_t, axis=0).astype(BF16).T
    weighted = (gate * attn).astype(BF16)
    update = dot(weighted, wo)
    d_g = (dw * attn * gate * (1.0 - gate)).astype(BF16)
    d_x = (
        dot_nt(d_q, wq_ref[...])
        + dot_nt(d_k, wk_ref[...])
        + dot_nt(d_v, wv_ref[...])
        + dot_nt(d_g, wg_ref[...])
    )
    adjoint = layer_norm_adjoint(d_x, hat, inv, gain)
    zeros = jnp.zeros((CHIPS, LANES), F32)
    for r, value in enumerate(
        (update[:, :LANES], update[:, LANES:], adjoint[:, :LANES], adjoint[:, LANES:])
    ):
        a, b = halves(value)
        mine[pl.ds(r, CHIPS, stride=8), :] = a
        mine[pl.ds(4 + r, CHIPS, stride=8), :] = zeros
        theirs[pl.ds(r, CHIPS, stride=8), :] = zeros
        theirs[pl.ds(4 + r, CHIPS, stride=8), :] = b
    put(0, 5)
    gain_out[...] = jnp.sum(d_x * hat, axis=0, keepdims=True)
    x_t = x.T
    w_t = weighted.T
    pairs = ((x_t, d_q), (x_t, d_k), (x_t, d_v), (x_t, d_g), (w_t, grad))
    mats = []
    for a, b in pairs:
        turned = jnp.concatenate([b[:, LANES:], b[:, :LANES]], axis=1)
        mats.append(dot(a, jnp.where(first, b, turned)))
    for ref, cols in ((own, slice(0, LANES)), (other, slice(LANES, FEATURES))):
        for tile, m in zip((2, 3, 7, 8, 4), mats):
            ref[:, tile] = m[:, cols].reshape(TILES, 8, LANES).astype(ref.dtype)


def pair_gradient(d_bias, pair, gain, w_bias, rows):
    rows[...] = listed(pair[0].astype(F32))
    hat, inv, scaled = layer_norm(reordered(rows), gain)
    parts = split(d_bias)[::-1]
    d_pln = sum(dot_tn(part, w_bias) for part in parts)
    head = sum(dot(part, scaled.astype(BF16)) for part in parts)
    return hat, inv, d_pln, head


def owner_kernel(pos, got, pair, gain, w_bias, d_gain, out, d_bias_out, rows, sums):
    value = got[...].astype(F32).reshape(TILES, 2 * PART_ROWS, LANES)
    sums[...] = jnp.sum(value, axis=0)
    total = sums[0:PART_ROWS, :] + sums[PART_ROWS:, :]
    sums[0:PART_ROWS, :] = total
    even = pos[2] % 2 == 0
    d_bias = jnp.where(even, sums[8:16, :], sums[12:20, :])
    weights = jnp.where(even, sums[16:32, :], sums[20:36, :])
    fifth = jnp.where(even, sums[32:36, :], sums[0:4, :])
    d_bias_out[...] = d_bias
    hat, _, d_pln, head = pair_gradient(d_bias, pair, gain[...], w_bias[...], rows)
    shard = jnp.concatenate(
        [
            weights,
            fifth,
            jnp.sum(d_pln * hat, axis=0, keepdims=True),
            d_gain[:, :LANES],
            d_gain[:, LANES:],
            jnp.zeros((1, LANES), F32),
            head,
        ],
        axis=0,
    )
    out[...] = jnp.broadcast_to(shard.astype(BF16)[None], (LINE, SUM_ROWS, LANES))


def unpack_kernel(pos, got, d_bias, pair, gain_ref, w_bias, update, adjoint, couple, stage, rows):
    stage[...] = got[...].astype(F32)
    first = pos[0] == 0
    even = pos[2] % 2 == 0

    def line(r):
        a, b = (stage[pl.ds(k, CHIPS, stride=PART_ROWS), :] for k in (r, 4 + r))
        return jnp.where(even, a, b)

    for index, out in enumerate((update, adjoint)):
        for half in range(2):
            r = 2 * index + half
            same, cross = line(r), line(4 + r)
            rows[pl.ds(0, CHIPS, stride=CORES), :] = jnp.where(first, same, cross)
            rows[pl.ds(1, CHIPS, stride=CORES), :] = jnp.where(first, cross, same)
            out[:, half * LANES : (half + 1) * LANES] = natural(rows[...]).astype(BF16)
    gain = gain_ref[...]
    hat, inv, d_pln, _ = pair_gradient(d_bias[...], pair, gain, w_bias[...], rows)
    restore(rows, layer_norm_adjoint(d_pln, hat, inv, gain))
    couple[0] = natural(rows[...]).astype(BF16)


def line_kernel(pos, got, out):
    low = lax.broadcasted_iota(jnp.int32, (1, 8, 1), 1) < 4
    tiles = got[...].astype(F32).reshape(LINE // 2, 2, 4, 8, LANES)
    even, odd = tiles[:, 0], tiles[:, 1]
    fifth = jnp.where(low, even[:, 2], pltpu.roll(odd[:, 2], 4, 1))
    sums = jnp.sum(tiles[:, :, 2:], axis=(0, 1))
    weights = (even[:, 0], even[:, 1], fifth, odd[:, 0], odd[:, 1])
    for w, value in enumerate(weights):
        value = value.astype(BF16)
        for t in range(LINE // 2):
            out[:, 5 * t + w] = jnp.broadcast_to(value[t][None], (LINE, 8, LANES))
    for n in range(2):
        out[:, 20 + n] = jnp.broadcast_to(sums[n].astype(BF16)[None], (LINE, 8, LANES))


def final_kernel(pos, mine, theirs, *refs):
    weights, (head, msa_gain, pair_gain) = refs[:5], refs[5:]
    for n, w in enumerate((0, 1, 4, 2, 3)):
        for side, got in enumerate((mine, theirs)):
            column = pl.multiple_of(LANES * jnp.bitwise_xor(pos[0], side), LANES)
            value = jnp.stack([got[:, 5 * t + n] for t in range(LINE // 2)], axis=1)
            value = value.astype(F32).reshape(FEATURES, LANES)
            weights[w][:, pl.ds(column, LANES)] = value
    sums = sum(jnp.sum(got[:, 20:].astype(F32), axis=0) for got in (mine, theirs))
    head[...] = sums[1]
    pair_gain[...] = sums[0, 4:5]
    msa_gain[:, :LANES] = sums[0, 5:6]
    msa_gain[:, LANES:] = sums[0, 6:7]


def on_device(msa, flags, pair, gain, pair_gain, wq, wk, wv, wg, wo, w_bias, grad):
    index = lax.axis_index("dap")
    pos = jnp.stack([index % CORES, index, index // CORES]).astype(jnp.int32)
    chips = [LINE * q + (FIRST_Z + z) % LINE for q in LINES for z in range(LINE)]
    same_core = [[CORES * m + c for m in chips] for c in range(CORES)]
    along_z = [g[LINE * q : LINE * (q + 1)] for g in same_core for q in range(LINE)]
    across = [g[z::LINE] for g in same_core for z in range(LINE)]
    partner = [(i, i ^ 1) for i in range(N)]

    def exchange(x, groups):
        return lax.all_to_all(
            x, "dap", split_axis=0, concat_axis=0, tiled=True, axis_index_groups=groups
        )

    w_bias = w_bias.T
    gain = gain.reshape(1, FEATURES)
    pair_gain = pair_gain.reshape(1, LANES)
    kept = (pair, pair_gain, w_bias, wq, wk, wv, wg, wo, gain)
    sent, *kept = call(
        entry_kernel,
        (jax.ShapeDtypeStruct((CHIPS * IN_ROWS, LANES), BF16),)
        + tuple(jax.ShapeDtypeStruct(v.shape, v.dtype) for v in kept),
        [
            pltpu.VMEM((N, FEATURES), BF16),
            pltpu.VMEM((N, FEATURES), BF16),
            pltpu.VMEM((1, N), jnp.int32),
            pltpu.VMEM((CHIPS * IN_ROWS, LANES), F32),
            pltpu.VMEM((N, LANES), F32),
            pltpu.SemaphoreType.DMA((12,)),
        ],
        *kept, msa.reshape(N, FEATURES), grad.reshape(N, FEATURES), flags.reshape(1, N),
        far_in=range(12),
    )
    pair, pair_gain, w_bias, wq, wk, wv, wg, wo, gain = kept
    near = exchange(sent.reshape(CHIPS, IN_ROWS // 2, 2, LANES), same_core)
    near = near.reshape(CHIPS * IN_ROWS, LANES)
    far = lax.ppermute(near, "dap", partner)
    part = (TILES, PART_TILES, 8, LANES)
    own, other, d_gain = call(
        sequence_kernel,
        (
            jax.ShapeDtypeStruct(part, F32),
            jax.ShapeDtypeStruct(part, BF16),
            jax.ShapeDtypeStruct((1, FEATURES), F32),
        ),
        [
            pltpu.VMEM((CORES, CHIPS * IN_ROWS, LANES), F32),
            pltpu.VMEM((CHIPS * 8, LANES), F32),
            pltpu.VMEM((CHIPS * 8, LANES), F32),
            pltpu.VMEM((4 * N, FEATURES), F32),
            pltpu.VMEM((4 * N, FEATURES), F32),
            pltpu.VMEM((N, HEADS * LANES), BF16),
            pltpu.VMEM((N, HEADS * LANES), BF16),
        ],
        pos, near, far, gain, wq, wk, wv, wg, wo,
    )
    paired = (own + lax.ppermute(other, "dap", partner).astype(F32)).astype(BF16)
    got = exchange(paired.reshape(CHIPS, PART_TILES, 4, LANES), same_core)
    got = got.reshape(CHIPS * PART_ROWS, LANES)
    shard, d_bias = call(
        owner_kernel,
        (
            jax.ShapeDtypeStruct((LINE, SUM_ROWS, LANES), BF16),
            jax.ShapeDtypeStruct((HEADS, LANES), F32),
        ),
        [pltpu.VMEM((N, LANES), F32), pltpu.VMEM((2 * PART_ROWS, LANES), F32)],
        pos, got, pair, pair_gain, w_bias, d_gain,
    )
    line = call(
        line_kernel,
        jax.ShapeDtypeStruct((LINE, LINE_TILES, 8, LANES), BF16),
        [],
        pos, exchange(shard, along_z),
    )
    mine = exchange(line, across)
    row_shape = jax.ShapeDtypeStruct((N, FEATURES), BF16)
    update, adjoint, couple = call(
        unpack_kernel,
        (row_shape, row_shape, jax.ShapeDtypeStruct((1, N, LANES), BF16)),
        [pltpu.VMEM((CHIPS * PART_ROWS, LANES), F32), pltpu.VMEM((N, LANES), F32)],
        pos, got, d_bias, pair, pair_gain, w_bias,
    )
    theirs = lax.ppermute(mine, "dap", partner)
    *weights, head, msa_gain, pair_gain = call(
        final_kernel,
        (jax.ShapeDtypeStruct((FEATURES, FEATURES), F32),) * 5
        + (
            jax.ShapeDtypeStruct((HEADS, LANES), F32),
            jax.ShapeDtypeStruct((1, FEATURES), F32),
            jax.ShapeDtypeStruct((1, LANES), F32),
        ),
        [],
        pos, mine, theirs,
    )
    return (
        update.reshape(N, 1, FEATURES),
        adjoint.reshape(N, 1, FEATURES),
        couple,
        *weights,
        head.T,
        msa_gain.reshape(FEATURES),
        pair_gain.reshape(LANES),
    )


def solution(mesh):
    rows = P("dp", "dap", None)
    pair = P(("dp", "dap"), None, None)
    in_specs = (rows, P("dp", "dap"), pair) + (P(),) * 8 + (rows,)
    out_specs = (rows, rows, pair) + (P("dp", None),) * 6 + (P("dp"), P("dp"))
    return jax.shard_map(
        on_device, mesh=mesh, in_specs=in_specs, out_specs=out_specs, check_vma=False
    )
```
